32 devices in a mesh: group: 2 (over x), date: 16 (over z, y, core).
Axes of the slice: x: 2, y: 2, z: 4, core: 2. Of those that a mesh axis runs over, the one named last changes fastest.
Arguments:
- slc_stack: bfloat16 [16, 2, 32, 16384], P('date', None, 'group'), parts along dimension 2, may hold values from -30 to 30
- band_taps: bfloat16 [2, 2, 32], replicated, may hold values from -1 to 1
- pair_flags: int32 [16, 4], P('date'), may hold values from 0 to 1, as said below
Outputs:
- iono_phase: float32 [16, 8, 1024], P('date', 'group'), parts along dimension 1
- weight_sum: float32 [16, 8, 1024], P('date', 'group'), parts along dimension 1
The draws below stay inside these ranges and needn't reach their ends.
There are 2 independent parts, one for each index of `group`. The reference program is written for one: setup_inputs(seed, part) draws one part's arguments, and reference() takes and returns one part's arrays. A program takes and returns all parts, laid end to end along the dimension named above; an argument that names none is the same for every part. Nothing has to cross between parts.
Inputs may be any that keep to these rules, and one draw needn't show every extreme that they name: pair_flags[d,0] is 1 for every date but the last; pair_flags[d,k] is 0 where d + k + 1 >= 16.
All inputs are finite; a program needn't handle non-finite values.
Results may differ from the reference program's by a relative error of at most 0.002.
Values may be sent and summed in bfloat16 or wider, within the bound.
A program may use at most 128 MiB of HBM per device.

```python
import jax
import jax.numpy as jnp
from jax import lax

ROWS = 16
RANGE = 16384
TAPS = 32
ML_AZ = 4
ML_RG = 16
SPAN = 4
RADIUS = 8
ITERS = 4
DATES = 16
AZ_L = 4
RG_L = 1024


def draw_slc_stack(key, part):
    keys = jax.random.split(jax.random.fold_in(key, 17), 5)
    scenery = jax.random.normal(keys[0], (2, ROWS, RANGE), jnp.float32)
    slopes = jax.random.uniform(keys[1], (DATES, 1, 1), jnp.float32, -3.0, 3.0)
    columns = jnp.arange(RANGE, dtype=jnp.float32)[None, None, :] * (25.0 / RANGE)
    rough = 0.4 * jax.random.normal(keys[2], (DATES, ROWS, RANGE), jnp.float32)
    angles = slopes * columns + rough
    real_part = scenery[0][None] * jnp.cos(angles) - scenery[1][None] * jnp.sin(angles)
    imag_part = scenery[0][None] * jnp.sin(angles) + scenery[1][None] * jnp.cos(angles)
    noise = 0.5 * jax.random.normal(keys[4], (DATES, 2, ROWS, RANGE), jnp.float32)
    result = jnp.stack([real_part, imag_part], axis=1) + noise
    return jnp.clip(result, -30.0, 30.0).astype(jnp.bfloat16)


def draw_pair_flags(key, part):
    flags = jax.random.randint(jax.random.fold_in(key, 29), (DATES, SPAN), 0, 2, jnp.int32)
    column = lax.broadcasted_iota(jnp.int32, (DATES, SPAN), 1)
    date_ids = lax.broadcasted_iota(jnp.int32, (DATES, SPAN), 0)
    flags = jnp.where(column == 0, 1, flags)
    present = (date_ids + column + 1 < DATES).astype(jnp.int32)
    return (flags * present).astype(jnp.int32)


def scatter_about(key, shape, scale, bound, held_as=jnp.bfloat16):
    drawn = scale * jax.random.normal(key, shape, jnp.float32)
    return jnp.clip(drawn, min=-bound, max=bound).astype(held_as)


def setup_inputs(seed: int = 0, part: int = 0) -> dict:
    seeds = jax.random.split(jax.random.key(seed), 4)
    part_splits = jax.random.split(jax.random.fold_in(seeds[3], part), 4)
    return {
        "slc_stack": draw_slc_stack(jax.random.fold_in(jax.random.fold_in(seeds[3], part), 71), part),
        "band_taps": scatter_about(seeds[1], (2, 2, TAPS), TAPS ** -0.5, 1.0),
        "pair_flags": draw_pair_flags(jax.random.fold_in(seeds[3], 71), part),
    }


eps_power = 1e-06
floor_weight = 0.1
ridge_weight = 0.05
split_coef = 2.0

def band_split(one_scene, band_taps):
    signal = one_scene.astype(jnp.float32)
    left_pad = TAPS // 2
    padded = jnp.pad(signal, ((0, 0), (0, 0), (left_pad, TAPS - 1 - left_pad)))
    coeffs = band_taps.astype(jnp.float32)
    result = jnp.zeros((2, 2, ROWS, RANGE), jnp.float32)
    for offset in range(TAPS):
        window = padded[:, :, offset:offset + RANGE]
        real_tap = coeffs[:, 0, offset][:, None, None]
        imag_tap = coeffs[:, 1, offset][:, None, None]
        real_part = real_tap * window[0] - imag_tap * window[1]
        imag_part = imag_tap * window[0] + real_tap * window[1]
        result = result + jnp.stack([real_part, imag_part], axis=1)
    return result.astype(jnp.bfloat16)

def multilook(values):
    shaped = values.reshape(values.shape[:-2] + (AZ_L, ML_AZ, RG_L, ML_RG))
    return shaped.sum(axis=(-3, -1))

def later_of(values, offset):
    return jnp.concatenate([values[offset:], jnp.zeros_like(values[:offset])], axis=0)

def earlier_of(values, offset):
    return jnp.concatenate([jnp.zeros_like(values[:offset]), values[:-offset]], axis=0)

def reference(slc_stack, band_taps, pair_flags):
    bands = lax.map(lambda one_scene: band_split(one_scene, band_taps), slc_stack)

    def power_of(piece):
        values = piece.astype(jnp.float32)
        return multilook(values[:, 0] * values[:, 0] + values[:, 1] * values[:, 1])
    powers = lax.map(power_of, bands)
    date_ids = jnp.arange(DATES, dtype=jnp.int32)

    def pair_of(date_index):
        own_bands = lax.dynamic_index_in_dim(bands, date_index, 0, keepdims=False).astype(jnp.float32)
        real_list = []
        imag_list = []
        for offset in range(1, SPAN + 1):
            other_index = jnp.minimum(date_index + offset, DATES - 1).astype(jnp.int32)
            present = (date_index + offset < DATES).astype(jnp.float32)
            partner = lax.dynamic_index_in_dim(bands, other_index, 0, keepdims=False).astype(jnp.float32) * present
            real_part = own_bands[:, 0] * partner[:, 0] + own_bands[:, 1] * partner[:, 1]
            imag_part = own_bands[:, 1] * partner[:, 0] - own_bands[:, 0] * partner[:, 1]
            real_list.append(multilook(real_part))
            imag_list.append(multilook(imag_part))
        return (jnp.stack(real_list, axis=0), jnp.stack(imag_list, axis=0))
    cross_real, cross_imag = lax.map(pair_of, date_ids)
    partner_power = jnp.stack([later_of(powers, offset) for offset in range(1, SPAN + 1)], axis=1)
    own_power = powers[:, None]
    coherence = (cross_real ** 2 + cross_imag ** 2) / (own_power * partner_power + eps_power)
    flags = pair_flags.astype(jnp.float32)[:, :, None, None]
    weight = flags * 0.5 * (coherence[:, :, 0] + coherence[:, :, 1])
    normalizer = jnp.sqrt((own_power[:, :, 0] * partner_power[:, :, 0] + eps_power) * (own_power[:, :, 1] * partner_power[:, :, 1] + eps_power))
    cross_term = cross_imag[:, :, 0] * cross_real[:, :, 1] - cross_real[:, :, 0] * cross_imag[:, :, 1]
    raw_phase = split_coef * cross_term / normalizer
    row_ids = lax.broadcasted_iota(jnp.int32, (RG_L, RG_L), 0)
    col_ids = lax.broadcasted_iota(jnp.int32, (RG_L, RG_L), 1)
    box_matrix = (jnp.abs(row_ids - col_ids) <= RADIUS).astype(jnp.float32)
    numerator = jnp.matmul(weight * raw_phase, box_matrix, precision=lax.Precision.HIGHEST)
    denominator = jnp.matmul(weight, box_matrix, precision=lax.Precision.HIGHEST)
    pair_phase = numerator / (denominator + floor_weight)
    smooth_weight = denominator / (2 * RADIUS + 1)
    first_pair = pair_phase[:, 0]
    chain_start = jnp.cumsum(jnp.concatenate([jnp.zeros_like(first_pair[:1]), first_pair[:-1]], axis=0), axis=0)
    low_weight = [earlier_of(smooth_weight[:, offset - 1], offset) for offset in range(1, SPAN + 1)]
    low_phase = [earlier_of(pair_phase[:, offset - 1], offset) for offset in range(1, SPAN + 1)]
    weight_sum = jnp.zeros_like(chain_start)
    for offset in range(1, SPAN + 1):
        weight_sum = weight_sum + smooth_weight[:, offset - 1] + low_weight[offset - 1]
    diagonal = weight_sum + ridge_weight
    iono_phase = chain_start
    for sweep_index in range(ITERS):
        accumulated = ridge_weight * chain_start
        for offset in range(1, SPAN + 1):
            accumulated = accumulated + smooth_weight[:, offset - 1] * (later_of(iono_phase, offset) - pair_phase[:, offset - 1])
            accumulated = accumulated + low_weight[offset - 1] * (earlier_of(iono_phase, offset) + low_phase[offset - 1])
        iono_phase = accumulated / diagonal
    return (iono_phase, weight_sum)
```

```python
import functools

import jax
import jax.numpy as jnp
from jax import lax
from jax.experimental import pallas as pl
from jax.experimental.pallas import tpu as pltpu
from jax.sharding import PartitionSpec as P

TAPS = 32
ML_AZ = 4
ML_RG = 16
SPAN = 4
RADIUS = 8
ITERS = 4

LANES = 128
CELLS = LANES // ML_RG
SUB = 16
SIDE = SPAN // 2
WIN = SPAN + 2 * SIDE
SLOT = ML_AZ + 1

eps_power = 1e-06
floor_weight = 0.1
ridge_weight = 0.05
split_coef = 2.0

F32 = jnp.float32
BF16 = jnp.bfloat16

OWN = tuple(range(SIDE, SIDE + SPAN))
FAR = tuple(range(SIDE)) + tuple(range(SIDE + SPAN, WIN))


def first_date(k):
    return 0 if k == SPAN else 1


PAIRS = [(first_date(k) + g, k) for k in range(1, SPAN + 1) for g in range(SPAN)]
OWN_PAIRS = [(w, k) for w, k in PAIRS if w in OWN and w + k in OWN]
FAR_PAIRS = [p for p in PAIRS if p not in OWN_PAIRS]


def listing():
    order = {}
    for dates, pairs in ((OWN, OWN_PAIRS), (FAR, FAR_PAIRS)):
        for w in dates:
            for band in range(2):
                order["p", w, band] = len(order)
        for w, k in pairs:
            for band in range(2):
                order["r", w, k, band] = len(order)
                order["i", w, k, band] = len(order)
    return order


ORDER = listing()
OWN_COUNT = 2 * SPAN + 4 * len(OWN_PAIRS)
FAR_COUNT = 2 * SPAN + 4 * len(FAR_PAIRS)


def kernel(
    n, steps,
    slc_hbm, flags_hbm, taps_hbm, out_ref,
    slc, flags_in, taps_in, taps_ref, turn, data, recv, mat, bands_own, bands_far, both, red, qty, quant,
    msg, got, fin, pack, back,
    in_sem, send_sem, recv_sem, fsend_sem, bsend_sem, brecv_sem, dsend_sem, drecv_sem, wave_sem,
):
    me = lax.axis_index("date")
    q = lax.rem(me, SPAN)
    z = me // SPAN
    slabs = n // SPAN
    wide = LANES // slabs
    has_left = z > 0
    has_right = z < slabs - 1
    mesh_id = pl.DeviceIdType.MESH

    slc_load = pltpu.make_async_copy(slc_hbm.at[0], slc, in_sem.at[0])
    slc_load.start()
    flags_load = pltpu.make_async_copy(flags_hbm, flags_in, in_sem.at[1])
    flags_load.start()
    taps_load = pltpu.make_async_copy(taps_hbm, taps_in, in_sem.at[2])
    taps_load.start()
    barrier = pltpu.get_barrier_semaphore()

    for hop in range(1, SPAN):
        pl.semaphore_signal(
            barrier, inc=1, device_id={"date": z * SPAN + lax.rem(q + hop, SPAN)}, device_id_type=mesh_id
        )

    @pl.when(has_left)
    def _():
        pl.semaphore_signal(barrier, inc=1, device_id={"date": me - SPAN}, device_id_type=mesh_id)

    @pl.when(has_right)
    def _():
        pl.semaphore_signal(barrier, inc=1, device_id={"date": me + SPAN}, device_id_type=mesh_id)

    flags_load.wait()
    tile_row = lax.broadcasted_iota(jnp.int32, (SUB, 2 * LANES), 0)
    own_flags = flags_in[...].astype(F32)
    flag_tile = jnp.zeros((SUB, 2 * LANES), F32)
    for k in range(SPAN):
        flag_tile = jnp.where(tile_row == k, jnp.broadcast_to(own_flags[0:1, k:k + 1], flag_tile.shape), flag_tile)
    flag_tile = flag_tile.astype(BF16)
    for s in range(SPAN):
        data[s, SLOT + ML_AZ] = flag_tile
    taps_load.wait()
    taps_ref[...] = jnp.zeros_like(taps_ref)
    for band in range(2):
        taps_ref[2 * band:2 * band + 2, 0:TAPS] = taps_in[band].astype(F32)

    k_id = lax.broadcasted_iota(jnp.int32, (LANES, LANES), 0)
    j_id = lax.broadcasted_iota(jnp.int32, (LANES, LANES), 1)
    reach = k_id - j_id + TAPS // 2
    circ = []
    for m in range(4):
        base = jnp.broadcast_to(taps_ref[m:m + 1, :], (LANES, LANES))
        circ.append(pltpu.roll(base, LANES - TAPS // 2, 1, stride=1, stride_axis=0).T)
    for edge in range(2):
        inside = (reach >= 0) & (reach < LANES)
        keep = inside if edge == 0 else jnp.logical_not(inside)
        row = edge * 2 * LANES
        for band in range(2):
            re_part = jnp.where(keep, circ[2 * band], 0.0).astype(BF16)
            im_value = jnp.where(keep, circ[2 * band + 1], 0.0)
            im_part = im_value.astype(BF16)
            im_minus = (-im_value).astype(BF16)
            col = band * 2 * LANES
            mat[row:row + 128, col:col + 128] = re_part
            mat[row:row + 128, col + 128:col + 256] = im_part
            mat[row + 128:row + 256, col:col + 128] = im_minus
            mat[row + 128:row + 256, col + 128:col + 256] = re_part

    slc_load.wait()

    def regroup(j, carry):
        for part in range(2):
            for i in range(SUB):
                at = pl.multiple_of((steps * i + j) * LANES, LANES)
                value = slc[part, :, pl.ds(at, LANES)].astype(F32)
                turn[pl.ds(part * SUB * SUB + i, SUB, stride=SUB), :] = value
        for part in range(2):
            for s in range(SPAN):
                for r in range(ML_AZ):
                    row = part * SUB * SUB + (ML_AZ * s + r) * SUB
                    value = turn[row:row + SUB, :].astype(BF16)
                    data[s, SLOT * (j + 1) + r, :, part * LANES:part * LANES + LANES] = value
        return carry

    lax.fori_loop(0, steps, regroup, 0)

    def chunk(ref, j, first):
        return ref.at[pl.ds(SLOT * (j + 1), SLOT if first else ML_AZ)]

    def slab_copy(target, j, first):
        return pltpu.make_async_remote_copy(
            src_ref=chunk(data.at[target], j, first), dst_ref=chunk(recv.at[q + SIDE], j, first),
            send_sem=send_sem.at[target, j], recv_sem=recv_sem.at[q + SIDE, j],
            device_id={"date": z * SPAN + target}, device_id_type=mesh_id,
        )

    def own_copy(j, first):
        return pltpu.make_async_copy(
            chunk(data.at[q], j, first), chunk(recv.at[q + SIDE], j, first), recv_sem.at[q + SIDE, j]
        )

    def side_copy(w, j, first):
        go_left = w < SPAN
        to, device = (w + SPAN, me - SPAN) if go_left else (w - SPAN, me + SPAN)
        return pltpu.make_async_remote_copy(
            src_ref=chunk(recv.at[w], j, first), dst_ref=chunk(recv.at[to], j, first),
            send_sem=fsend_sem.at[w - SIDE, j], recv_sem=recv_sem.at[to, j],
            device_id={"date": device}, device_id_type=mesh_id,
        )

    def arrived(w, j, first):
        ref = chunk(recv.at[w], j, first)
        pltpu.make_async_copy(ref, ref, recv_sem.at[w, j]).wait()

    near = SPAN - 1 + has_left.astype(jnp.int32) + has_right.astype(jnp.int32)
    pl.semaphore_wait(barrier, near)

    def send_chunk(j, first):
        own_copy(j, first).start()
        for hop in (2, 3, 1):
            slab_copy(lax.rem(q + hop, SPAN), j, first).start()

    send_chunk(0, True)

    def send_more(j, carry):
        send_chunk(j, False)
        return carry

    lax.fori_loop(1, steps, send_more, 0)

    @pl.when(jnp.logical_not(has_left))
    def _():
        for w in range(SIDE):
            recv[w] = jnp.zeros(recv.shape[1:], BF16)

    @pl.when(jnp.logical_not(has_right))
    def _():
        for w in range(SIDE + SPAN, WIN):
            recv[w] = jnp.zeros(recv.shape[1:], BF16)

    sel_row = lax.broadcasted_iota(jnp.int32, (CELLS, 2 * LANES), 0)
    sel_lane = lax.broadcasted_iota(jnp.int32, (CELLS, 2 * LANES), 1)
    selector = jnp.where(lax.rem(sel_lane, LANES) // ML_RG == sel_row, 1.0, 0.0).astype(BF16)
    contract = (((1,), (1,)), ((), ()))
    edge_lane = lax.rem(lax.broadcasted_iota(jnp.int32, (ML_AZ, SUB, 2 * LANES), 2), LANES)
    from_before = edge_lane >= LANES - TAPS // 2
    sub_row = lax.broadcasted_iota(jnp.int32, (ML_AZ, SUB, 2 * LANES), 1)

    def own_arrive(j, first):
        for w in OWN:
            arrived(w, j, first)

        @pl.when(has_left)
        def _():
            for w in OWN[:SIDE]:
                side_copy(w, j, first).start()

        @pl.when(has_right)
        def _():
            for w in OWN[SIDE:]:
                side_copy(w, j, first).start()

    def far_arrive(j, first):
        @pl.when(has_left)
        def _():
            for w in FAR[:SIDE]:
                arrived(w, j, first)

        @pl.when(has_right)
        def _():
            for w in FAR[SIDE:]:
                arrived(w, j, first)

    def make_after(dates):
        for w in dates:
            value = recv[w, SLOT:SLOT + ML_AZ].astype(F32)
            value = jnp.where(sub_row < SUB - 1, pltpu.roll(value, SUB - 1, 1), 0.0)
            recv[w, SLOT * (steps + 1):SLOT * (steps + 1) + ML_AZ] = value.astype(BF16)

    def make_before(dates):
        for w in dates:
            value = recv[w, SLOT * steps:SLOT * steps + ML_AZ].astype(F32)
            value = jnp.where(sub_row > 0, pltpu.roll(value, 1, 1), 0.0)
            recv[w, 0:ML_AZ] = value.astype(BF16)

    def band_split(dates, j):
        rows = []
        for w in dates:
            here = recv[w, pl.ds(SLOT * (j + 1), ML_AZ)]
            before = recv[w, pl.ds(SLOT * j, ML_AZ)]
            after = recv[w, pl.ds(SLOT * (j + 2), ML_AZ)]
            edge = jnp.where(from_before, before, after)
            rows.append(jnp.concatenate([here, edge], axis=2).reshape(ML_AZ * SUB, 4 * LANES))
        made = jnp.dot(jnp.concatenate(rows, axis=0), mat[...], preferred_element_type=F32)
        return made.astype(BF16).astype(F32).reshape(len(dates), ML_AZ, SUB, 4 * LANES)

    def read(w, j, band, part):
        cols = slice((2 * band + part) * LANES, (2 * band + part + 1) * LANES)
        if w in OWN:
            return [bands_own[j, OWN.index(w), r, :, cols] for r in range(ML_AZ)]
        return [bands_far[FAR.index(w), r, :, cols] for r in range(ML_AZ)]

    def total(terms):
        terms = list(terms)
        while len(terms) > 1:
            terms = [a + b for a, b in zip(terms[::2], terms[1::2])]
        return terms[0]

    def keep_sum(at, value):
        high = value.astype(BF16)
        low = (value - high.astype(F32)).astype(BF16)
        both[at * SUB:at * SUB + SUB, 0:LANES] = high
        both[at * SUB:at * SUB + SUB, LANES:2 * LANES] = low

    def products(dates, pairs, start, j):
        for band in range(2):
            for w in dates:
                re, im = (read(w, j, band, part) for part in range(2))
                keep_sum(ORDER["p", w, band] - start, total([a * a for a in re]) + total([a * a for a in im]))
            for w, k in pairs:
                a_re, a_im = (read(w, j, band, part) for part in range(2))
                b_re, b_im = (read(w + k, j, band, part) for part in range(2))
                re = total([a * b for a, b in zip(a_re, b_re)]) + total([a * b for a, b in zip(a_im, b_im)])
                im = total([a * b for a, b in zip(a_im, b_re)]) - total([a * b for a, b in zip(a_re, b_im)])
                keep_sum(ORDER["r", w, k, band] - start, re)
                keep_sum(ORDER["i", w, k, band] - start, im)

    def own_step(j):
        bands_own[j] = band_split(OWN, j)
        products(OWN, OWN_PAIRS, 0, j)
        red[j, :, 0:OWN_COUNT * SUB] = lax.dot_general(
            selector, both[0:OWN_COUNT * SUB], contract, preferred_element_type=F32
        )

    def far_step(j):
        bands_far[...] = band_split(FAR, j)
        products(FAR, FAR_PAIRS, OWN_COUNT, j)
        red[j, :, OWN_COUNT * SUB:(OWN_COUNT + FAR_COUNT) * SUB] = lax.dot_general(
            selector, both[0:FAR_COUNT * SUB], contract, preferred_element_type=F32
        )

    own_arrive(0, True)
    make_after(OWN)

    def stream(t, carry):
        @pl.when(t < steps)
        def _():
            own_arrive(t, False)

        @pl.when(t == steps - 1)
        def _():
            make_before(OWN)

        @pl.when((t >= 2) & (t < steps + 2))
        def _():
            own_step(lax.rem(t - 1, steps))

        @pl.when(t == 1)
        def _():
            far_arrive(0, True)
            make_after(FAR)

        @pl.when((t >= 2) & (t <= steps))
        def _():
            far_arrive(t - 1, False)

        @pl.when(t == steps)
        def _():
            make_before(FAR)

        @pl.when(t >= 3)
        def _():
            far_step(lax.rem(t - 2, steps))

        return carry

    lax.fori_loop(1, steps + 3, stream, 0)

    def wave(t, carry):
        @pl.when(has_left)
        def _():
            pl.semaphore_signal(wave_sem.at[1], inc=1, device_id={"date": me - SPAN}, device_id_type=mesh_id)

        @pl.when(has_right)
        def _():
            pl.semaphore_signal(wave_sem.at[0], inc=1, device_id={"date": me + SPAN}, device_id_type=mesh_id)

        @pl.when(has_left)
        def _():
            pl.semaphore_wait(wave_sem.at[0], 1)

        @pl.when(has_right)
        def _():
            pl.semaphore_wait(wave_sem.at[1], 1)

        return carry

    lax.fori_loop(1, slabs, wave, 0)

    lane = lax.broadcasted_iota(jnp.int32, (CELLS, LANES), 1)
    for g in range(len(ORDER) // steps):
        rows = [red[j, :, g * LANES:g * LANES + LANES] for j in range(steps)]
        bit = 1
        while bit < steps:
            upper = lax.rem(lane // (SUB * bit), 2) == 1
            turned = list(rows)
            for a in range(steps):
                if a & bit == 0:
                    b = a | bit
                    turned[a] = jnp.where(upper, pltpu.roll(rows[b], SUB * bit, 1), rows[a])
                    turned[b] = jnp.where(upper, rows[b], pltpu.roll(rows[a], LANES - SUB * bit, 1))
            rows = turned
            bit *= 2
        for u in range(steps):
            qty[g * steps + u] = rows[u]

    shape = (SPAN, CELLS, LANES)
    c_id = lax.broadcasted_iota(jnp.int32, shape, 1)
    l_id = lax.broadcasted_iota(jnp.int32, shape, 2)
    last_row = LANES - SUB

    def block_after(x):
        wrap = jnp.where(l_id == LANES - 1, 0.0, pltpu.roll(x, last_row - 1, 2))
        return jnp.where(l_id < last_row, pltpu.roll(x, last_row, 2), wrap)

    def block_before(x):
        wrap = jnp.where(l_id == 0, 0.0, pltpu.roll(x, SUB + 1, 2))
        return jnp.where(l_id >= SUB, pltpu.roll(x, SUB, 2), wrap)

    def box(value):
        prefix = value
        for hop in (1, 2, 4):
            prefix = prefix + jnp.where(c_id >= hop, pltpu.roll(prefix, hop, 1), 0.0)
        whole = jnp.sum(value, axis=1, keepdims=True)
        suffix = whole - prefix + value
        return block_before(suffix) + whole + block_after(prefix)

    def stacked(*keys):
        return jnp.concatenate([qty[ORDER[key]][None] for key in keys], axis=0)

    for k in range(1, SPAN + 1):
        dates = range(first_date(k), first_date(k) + SPAN)
        cr0, cr1 = (stacked(*[("r", w, k, band) for w in dates]) for band in range(2))
        ci0, ci1 = (stacked(*[("i", w, k, band) for w in dates]) for band in range(2))
        ab0, ab1 = (
            stacked(*[("p", w, band) for w in dates]) * stacked(*[("p", w + k, band) for w in dates]) + eps_power
            for band in range(2)
        )
        flag = jnp.concatenate(
            [
                jnp.broadcast_to(
                    recv[w, SLOT + ML_AZ].astype(F32)[k - 1:k, 0:LANES], (CELLS, LANES)
                )[None] for w in dates
            ], axis=0
        )
        weight = flag * 0.5 * ((cr0 * cr0 + ci0 * ci0) / ab0 + (cr1 * cr1 + ci1 * ci1) / ab1)
        phase = split_coef * (ci0 * cr1 - cr0 * ci1) / jnp.sqrt(ab0 * ab1)
        den = box(weight)
        num = box(weight * phase)
        quant[k - 1] = den / (2 * RADIUS + 1)
        quant[SPAN + k - 1] = num / (den + floor_weight)

    kinds = 2 * SPAN
    per = LANES // (SPAN * wide)
    pieces = kinds // per

    def line_copy(target):
        return pltpu.make_async_remote_copy(
            src_ref=msg.at[target], dst_ref=got.at[z],
            send_sem=bsend_sem.at[target], recv_sem=brecv_sem.at[z],
            device_id={"date": target * SPAN + q}, device_id_type=mesh_id,
        )

    def pack_line(target):
        for m in range(pieces):
            value = None
            for u in range(per):
                for g in range(SPAN):
                    at = (u * SPAN + g) * wide
                    shift = lax.rem(at - target * wide + LANES, LANES)
                    moved = pltpu.roll(quant[m * per + u, g], shift, 1)
                    value = moved if value is None else jnp.where(lane >= at, moved, value)
            msg[target, m] = value

    def send_line(target):
        @pl.when(target != z)
        def _():
            line_copy(target).start()

        @pl.when(target == z)
        def _():
            pltpu.make_async_copy(msg.at[z], got.at[z], brecv_sem.at[z]).start()

    def each_line(target, carry):
        pack_line(target)
        send_line(target)
        return carry

    lax.fori_loop(0, slabs, each_line, 0)

    def line_arrive(s, carry):
        pltpu.make_async_copy(got.at[s], got.at[s], brecv_sem.at[s]).wait()
        return carry

    lax.fori_loop(0, slabs, line_arrive, 0)

    regs = n * wide // LANES
    zero = jnp.zeros((CELLS, LANES), F32)

    def gather(kind):
        out = []
        for v in range(regs):
            value = None
            for s in range(v * slabs // regs, (v + 1) * slabs // regs):
                to = s * SPAN * wide - v * LANES
                at = (kind % per) * SPAN * wide
                piece = got[s, kind // per]
                if to != at:
                    piece = pltpu.roll(piece, (to - at) % LANES, 1)
                value = piece if value is None else jnp.where(lane >= to, piece, value)
            out.append(value)
        return out

    def shift(x, dates):
        far, by = divmod(dates * wide, LANES)
        out = []
        for v in range(regs):
            low = x[v + far] if 0 <= v + far < regs else zero
            if by == 0:
                out.append(low)
                continue
            high = x[v + far + 1] if 0 <= v + far + 1 < regs else zero
            out.append(jnp.where(lane < LANES - by, pltpu.roll(low, LANES - by, 1), pltpu.roll(high, LANES - by, 1)))
        return out

    def add(x, y):
        return [a + b for a, b in zip(x, y)]

    ahead, behind = [], []
    wsum = [zero] * regs
    rhs = [zero] * regs
    for k in range(1, SPAN + 1):
        skip = SIDE - first_date(k)
        w = gather(k - 1)
        p = gather(SPAN + k - 1)
        wp = [a * b for a, b in zip(w, p)]
        ahead.append(shift(w, skip))
        behind.append(shift(w, skip - k))
        wsum = add(wsum, add(ahead[-1], behind[-1]))
        rhs = add(rhs, [b - a for a, b in zip(shift(wp, skip), shift(wp, skip - k))])
        if k == 1:
            chain = shift(p, skip)
    hop = 1
    while hop < n:
        chain = add(chain, shift(chain, -hop))
        hop *= 2
    chain = shift(chain, -1)
    rhs = [r + ridge_weight * c for r, c in zip(rhs, chain)]
    inv = [1.0 / (t + ridge_weight) for t in wsum]
    phi = chain
    for sweep in range(ITERS):
        acc = rhs
        for k in range(1, SPAN + 1):
            acc = add(acc, [a * b for a, b in zip(ahead[k - 1], shift(phi, k))])
            acc = add(acc, [a * b for a, b in zip(behind[k - 1], shift(phi, -k))])
        phi = [a * b for a, b in zip(acc, inv)]
    for v in range(regs):
        fin[0, v] = phi[v]
        fin[1, v] = wsum[v]

    def out_copy(target):
        return pltpu.make_async_remote_copy(
            src_ref=pack.at[target], dst_ref=back.at[me],
            send_sem=dsend_sem.at[target], recv_sem=drecv_sem.at[me],
            device_id={"date": target}, device_id_type=mesh_id,
        )

    mine = lane // wide == z
    half = LANES // 2

    def finish(i, carry):
        target = lax.rem(me + i, n)
        v = target * wide // LANES
        at = lax.rem(target * wide, LANES)
        phase = pltpu.roll(fin[0, v], lax.rem(z * wide - at + LANES, LANES), 1)
        weight = pltpu.roll(fin[1, v], lax.rem(z * wide + half - at + LANES, LANES), 1)
        pack[target] = jnp.where(mine, phase, weight)

        @pl.when(i > 0)
        def _():
            out_copy(target).start()

        return carry

    lax.fori_loop(0, n, finish, 0)
    pltpu.make_async_copy(pack.at[me], back.at[me], drecv_sem.at[me]).start()

    def drain_out(i, carry):
        out_copy(lax.rem(me + i, n)).wait_send()
        return carry

    lax.fori_loop(1, n, drain_out, 0)

    def drain_line(s, carry):
        @pl.when(s != z)
        def _():
            line_copy(s).wait_send()
        return carry

    lax.fori_loop(0, slabs, drain_line, 0)

    def drain(j, first):
        for hop in range(1, SPAN):
            slab_copy(lax.rem(q + hop, SPAN), j, first).wait_send()

        @pl.when(has_left)
        def _():
            for w in OWN[:SIDE]:
                side_copy(w, j, first).wait_send()

        @pl.when(has_right)
        def _():
            for w in OWN[SIDE:]:
                side_copy(w, j, first).wait_send()

    drain(0, True)

    def drain_more(j, carry):
        drain(j, False)
        return carry

    lax.fori_loop(1, steps, drain_more, 0)

    def arrive(s, carry):
        pltpu.make_async_copy(back.at[s], back.at[s], drecv_sem.at[s]).wait()
        return carry

    lax.fori_loop(0, n, arrive, 0)

    rows = []
    for kind in range(2):
        place_of = lax.rem(lane + kind * half, LANES) // wide
        for s in range(SPAN):
            value = zero
            for line in range(slabs):
                value = jnp.where(place_of == line, back[line * SPAN + s], value)
            rows.append(pltpu.roll(value, half, 1) if kind else value)
    value = jnp.concatenate(rows, axis=0)
    high = value.astype(BF16)
    rest = value - high.astype(F32)
    middle = rest.astype(BF16)
    low = (rest - middle.astype(F32)).astype(BF16)
    width = out_ref.shape[2]
    place_row = lax.broadcasted_iota(jnp.int32, (LANES, width), 0)
    place_block = lax.broadcasted_iota(jnp.int32, (LANES, width), 1) // CELLS
    place = place_row == lax.rem(place_block, steps) * SUB + place_block // steps
    spread = jnp.dot(
        jnp.concatenate([high, middle, low], axis=0), jnp.where(place, 1.0, 0.0).astype(BF16),
        preferred_element_type=F32,
    )
    count = 2 * SPAN * CELLS
    spread = spread[0:count] + spread[count:2 * count] + spread[2 * count:3 * count]
    spread = spread.reshape(2 * SPAN, CELLS, width)
    s_row = lax.broadcasted_iota(jnp.int32, spread.shape, 1)
    s_col = lax.broadcasted_iota(jnp.int32, spread.shape, 2)
    result = jnp.sum(jnp.where(lax.rem(s_col, CELLS) == s_row, spread, 0.0), axis=1)
    out_ref[0] = result[0:SPAN]
    out_ref[1] = result[SPAN:2 * SPAN]


def local(slc_stack, band_taps, pair_flags):
    n = lax.axis_size("date")
    rows, span = slc_stack.shape[2:]
    steps = span // LANES // SUB
    slabs = n // SPAN
    assert rows == SUB and rows // ML_AZ == SPAN and span == LANES * LANES
    assert n % SPAN == 0 and LANES % slabs == 0 and slabs % SPAN == 0
    wide = LANES // slabs
    pieces = 2 * SPAN * SPAN * wide // LANES
    regs = n * wide // LANES
    tiles = SLOT * (steps + 2)

    vmem = pl.BlockSpec(memory_space=pltpu.VMEM)
    small = lambda *lead: pltpu.VMEM((*lead, CELLS, LANES), F32)
    sem = lambda *lead: pltpu.SemaphoreType.DMA(lead)
    both = pl.pallas_call(
        functools.partial(kernel, n, steps),
        out_shape=jax.ShapeDtypeStruct((2, rows // ML_AZ, span // ML_RG), F32),
        in_specs=[pl.BlockSpec(memory_space=pl.ANY)] * 3,
        out_specs=vmem,
        scratch_shapes=[
            pltpu.VMEM((2, rows, span), BF16),
            pltpu.VMEM((1, SPAN), jnp.int32),
            pltpu.VMEM((2, 2, TAPS), BF16),
            pltpu.VMEM((8, LANES), F32),
            pltpu.VMEM((2 * SUB * SUB, LANES), F32),
            pltpu.VMEM((SPAN, tiles, SUB, 2 * LANES), BF16),
            pltpu.VMEM((WIN, tiles, SUB, 2 * LANES), BF16),
            pltpu.VMEM((4 * LANES, 4 * LANES), BF16),
            pltpu.VMEM((steps, SPAN, ML_AZ, SUB, 4 * LANES), F32),
            pltpu.VMEM((SPAN, ML_AZ, SUB, 4 * LANES), F32),
            pltpu.VMEM((max(OWN_COUNT, FAR_COUNT) * SUB, 2 * LANES), BF16),
            pltpu.VMEM((steps, CELLS, len(ORDER) * SUB), F32),
            small(len(ORDER)),
            small(2 * SPAN, SPAN),
            small(slabs, pieces),
            small(slabs, pieces),
            small(2, regs),
            small(n),
            small(n),
            sem(3), sem(SPAN, steps), sem(WIN, steps), sem(SPAN, steps),
            sem(slabs), sem(slabs), sem(n), sem(n), pltpu.SemaphoreType.REGULAR((2,)),
        ],
        compiler_params=pltpu.CompilerParams(
            collective_id=0, has_side_effects=True, vmem_limit_bytes=60 * 1024 * 1024
        ),
    )(slc_stack, pair_flags, band_taps)
    return both[0:1], both[1:2]


def solution(mesh):
    in_specs = (P("date", None, "group", None), P(), P("date", None))
    out_specs = (P("date", "group", None), P("date", "group", None))
    return jax.shard_map(local, mesh=mesh, in_specs=in_specs, out_specs=out_specs, check_vma=False)
```

```python
import functools

import jax
import jax.numpy as jnp
from jax import lax
from jax.experimental import pallas as pl
from jax.experimental.pallas import tpu as pltpu
from jax.sharding import PartitionSpec as P

TAPS = 32
ML_AZ = 4
ML_RG = 16
SPAN = 4
RADIUS = 8
ITERS = 4

LANES = 128
CELLS = LANES // ML_RG
SUB = 16
SIDE = SPAN // 2
WIN = SPAN + 2 * SIDE
SLOT = ML_AZ + 1
LAG = 2

eps_power = 1e-06
floor_weight = 0.1
ridge_weight = 0.05
split_coef = 2.0

F32 = jnp.float32
BF16 = jnp.bfloat16

OWN = tuple(range(SIDE, SIDE + SPAN))
FAR = tuple(range(SIDE)) + tuple(range(SIDE + SPAN, WIN))


def first_date(k):
    return 0 if k == SPAN else 1


PAIRS = [(first_date(k) + g, k) for k in range(1, SPAN + 1) for g in range(SPAN)]
OWN_PAIRS = [(w, k) for w, k in PAIRS if w in OWN and w + k in OWN]
FAR_PAIRS = [p for p in PAIRS if p not in OWN_PAIRS]


def listing():
    order = {}
    for dates, pairs in ((OWN, OWN_PAIRS), (FAR, FAR_PAIRS)):
        for w in dates:
            for band in range(2):
                order["p", w, band] = len(order)
        for w, k in pairs:
            for band in range(2):
                order["r", w, k, band] = len(order)
                order["i", w, k, band] = len(order)
    return order


ORDER = listing()
OWN_COUNT = 2 * SPAN + 4 * len(OWN_PAIRS)
FAR_COUNT = 2 * SPAN + 4 * len(FAR_PAIRS)


def kernel(
    n, steps,
    slc_hbm, flags_hbm, taps_hbm, out_ref,
    slc, flags_in, taps_in, taps_ref, turn, data, recv, mat, bands_own, bands_far, both, red, qty, quant,
    msg, got, fin, pack, back,
    in_sem, send_sem, recv_sem, wave_sem,
):
    me = lax.axis_index("date")
    q = lax.rem(me, SPAN)
    z = me // SPAN
    slabs = n // SPAN
    wide = LANES // slabs
    has_left = z > 0
    has_right = z < slabs - 1
    mesh_id = pl.DeviceIdType.MESH

    slc_load = pltpu.make_async_copy(slc_hbm.at[0], slc, in_sem.at[0])
    slc_load.start()
    flags_load = pltpu.make_async_copy(flags_hbm, flags_in, in_sem.at[1])
    flags_load.start()
    taps_load = pltpu.make_async_copy(taps_hbm, taps_in, in_sem.at[2])
    taps_load.start()
    barrier = pltpu.get_barrier_semaphore()

    for hop in range(1, SPAN):
        pl.semaphore_signal(
            barrier, inc=1, device_id={"date": z * SPAN + lax.rem(q + hop, SPAN)}, device_id_type=mesh_id
        )

    @pl.when(has_left)
    def _():
        pl.semaphore_signal(barrier, inc=1, device_id={"date": me - SPAN}, device_id_type=mesh_id)

    @pl.when(has_right)
    def _():
        pl.semaphore_signal(barrier, inc=1, device_id={"date": me + SPAN}, device_id_type=mesh_id)

    flags_load.wait()
    tile_row = lax.broadcasted_iota(jnp.int32, (SUB, 2 * LANES), 0)
    own_flags = flags_in[...].astype(F32)
    flag_tile = jnp.zeros((SUB, 2 * LANES), F32)
    for k in range(SPAN):
        flag_tile = jnp.where(tile_row == k, jnp.broadcast_to(own_flags[0:1, k:k + 1], flag_tile.shape), flag_tile)
    flag_tile = flag_tile.astype(BF16)
    for s in range(SPAN):
        data[s, SLOT + ML_AZ] = flag_tile
    taps_load.wait()
    taps_ref[...] = jnp.zeros_like(taps_ref)
    for band in range(2):
        taps_ref[2 * band:2 * band + 2, 0:TAPS] = taps_in[band].astype(F32)

    k_id = lax.broadcasted_iota(jnp.int32, (LANES, LANES), 0)
    j_id = lax.broadcasted_iota(jnp.int32, (LANES, LANES), 1)
    reach = k_id - j_id + TAPS // 2
    circ = []
    for m in range(4):
        base = jnp.broadcast_to(taps_ref[m:m + 1, :], (LANES, LANES))
        circ.append(pltpu.roll(base, LANES - TAPS // 2, 1, stride=1, stride_axis=0).T)
    for edge in range(2):
        inside = (reach >= 0) & (reach < LANES)
        keep = inside if edge == 0 else jnp.logical_not(inside)
        row = edge * 2 * LANES
        for band in range(2):
            re_part = jnp.where(keep, circ[2 * band], 0.0).astype(BF16)
            im_value = jnp.where(keep, circ[2 * band + 1], 0.0)
            im_part = im_value.astype(BF16)
            im_minus = (-im_value).astype(BF16)
            col = band * 2 * LANES
            mat[row:row + 128, col:col + 128] = re_part
            mat[row:row + 128, col + 128:col + 256] = im_part
            mat[row + 128:row + 256, col:col + 128] = im_minus
            mat[row + 128:row + 256, col + 128:col + 256] = re_part

    slc_load.wait()

    def regroup(j, carry):
        for part in range(2):
            for i in range(SUB):
                at = pl.multiple_of((steps * i + j) * LANES, LANES)
                value = slc[part, :, pl.ds(at, LANES)].astype(F32)
                turn[(part * SUB + i) * SUB:(part * SUB + i + 1) * SUB, :] = value
        for part in range(2):
            for s in range(SPAN):
                for r in range(ML_AZ):
                    row = part * SUB * SUB + ML_AZ * s + r
                    value = turn[pl.ds(row, SUB, stride=SUB), :].astype(BF16)
                    data[s, SLOT * (j + 1) + r, :, part * LANES:part * LANES + LANES] = value
        return carry

    lax.fori_loop(0, steps, regroup, 0)

    def chunk(ref, j, first):
        return ref.at[pl.ds(SLOT * (j + 1), SLOT if first else ML_AZ)]

    def slab_copy(target, j, first):
        return pltpu.make_async_remote_copy(
            src_ref=chunk(data.at[target], j, first), dst_ref=chunk(recv.at[q + SIDE], j, first),
            send_sem=send_sem.at[0], recv_sem=recv_sem.at[1, j],
            device_id={"date": z * SPAN + target}, device_id_type=mesh_id,
        )

    def own_copy(j, first):
        return pltpu.make_async_copy(
            chunk(data.at[q], j, first), chunk(recv.at[q + SIDE], j, first), recv_sem.at[1, j]
        )

    def side_copy(w, j, first):
        go_left = w < SPAN
        to, device = (w + SPAN, me - SPAN) if go_left else (w - SPAN, me + SPAN)
        return pltpu.make_async_remote_copy(
            src_ref=chunk(recv.at[w], j, first), dst_ref=chunk(recv.at[to], j, first),
            send_sem=send_sem.at[1 if go_left else 2], recv_sem=recv_sem.at[2 if go_left else 0, j],
            device_id={"date": device}, device_id_type=mesh_id,
        )

    def arrived(dates, side, j, first):
        ref = recv.at[pl.ds(dates[0], len(dates)), pl.ds(SLOT * (j + 1), SLOT if first else ML_AZ)]
        pltpu.make_async_copy(ref, ref, recv_sem.at[side, j]).wait()

    near = SPAN - 1 + has_left.astype(jnp.int32) + has_right.astype(jnp.int32)
    pl.semaphore_wait(barrier, near)

    def send_chunk(j, first):
        own_copy(j, first).start()
        for hop in (2, 3, 1):
            slab_copy(lax.rem(q + hop, SPAN), j, first).start()

    send_chunk(0, True)

    def send_more(j, carry):
        send_chunk(j, False)
        return carry

    lax.fori_loop(1, steps, send_more, 0)

    @pl.when(jnp.logical_not(has_left))
    def _():
        for w in range(SIDE):
            recv[w] = jnp.zeros(recv.shape[1:], BF16)

    @pl.when(jnp.logical_not(has_right))
    def _():
        for w in range(SIDE + SPAN, WIN):
            recv[w] = jnp.zeros(recv.shape[1:], BF16)

    sel_row = lax.broadcasted_iota(jnp.int32, (CELLS, 2 * LANES), 0)
    sel_lane = lax.broadcasted_iota(jnp.int32, (CELLS, 2 * LANES), 1)
    selector = jnp.where(lax.rem(sel_lane, LANES) // ML_RG == sel_row, 1.0, 0.0).astype(BF16)
    contract = (((1,), (1,)), ((), ()))
    edge_lane = lax.rem(lax.broadcasted_iota(jnp.int32, (ML_AZ, SUB, 2 * LANES), 2), LANES)
    from_before = edge_lane >= LANES - TAPS // 2
    sub_row = lax.broadcasted_iota(jnp.int32, (ML_AZ, SUB, 2 * LANES), 1)

    def own_arrive(j, first):
        arrived(OWN, 1, j, first)

        @pl.when(has_left)
        def _():
            for w in OWN[:SIDE]:
                side_copy(w, j, first).start()

        @pl.when(has_right)
        def _():
            for w in OWN[SIDE:]:
                side_copy(w, j, first).start()

    def far_arrive(j, first):
        @pl.when(has_left)
        def _():
            arrived(FAR[:SIDE], 0, j, first)

        @pl.when(has_right)
        def _():
            arrived(FAR[SIDE:], 2, j, first)

    def make_after(dates):
        for w in dates:
            value = recv[w, SLOT:SLOT + ML_AZ].astype(F32)
            value = jnp.where(sub_row < SUB - 1, pltpu.roll(value, SUB - 1, 1), 0.0)
            recv[w, SLOT * (steps + 1):SLOT * (steps + 1) + ML_AZ] = value.astype(BF16)

    def make_before(dates):
        for w in dates:
            value = recv[w, SLOT * steps:SLOT * steps + ML_AZ].astype(F32)
            value = jnp.where(sub_row > 0, pltpu.roll(value, 1, 1), 0.0)
            recv[w, 0:ML_AZ] = value.astype(BF16)

    def band_split(dates, j):
        rows = []
        for w in dates:
            here = recv[w, pl.ds(SLOT * (j + 1), ML_AZ)]
            before = recv[w, pl.ds(SLOT * j, ML_AZ)]
            after = recv[w, pl.ds(SLOT * (j + 2), ML_AZ)]
            edge = jnp.where(from_before, before, after)
            rows.append(jnp.concatenate([here, edge], axis=2).reshape(ML_AZ * SUB, 4 * LANES))
        made = jnp.dot(jnp.concatenate(rows, axis=0), mat[...], preferred_element_type=F32)
        return made.astype(BF16).astype(F32).reshape(len(dates), ML_AZ, SUB, 4 * LANES)

    def read(w, j, band, part):
        cols = slice((2 * band + part) * LANES, (2 * band + part + 1) * LANES)
        if w in OWN:
            return [bands_own[j, OWN.index(w), r, :, cols] for r in range(ML_AZ)]
        return [bands_far[FAR.index(w), r, :, cols] for r in range(ML_AZ)]

    def total(terms):
        terms = list(terms)
        while len(terms) > 1:
            terms = [a + b for a, b in zip(terms[::2], terms[1::2])]
        return terms[0]

    def keep_sum(at, value):
        high = value.astype(BF16)
        low = (value - high.astype(F32)).astype(BF16)
        both[at * SUB:at * SUB + SUB, 0:LANES] = high
        both[at * SUB:at * SUB + SUB, LANES:2 * LANES] = low

    def products(dates, pairs, start, j):
        for band in range(2):
            for w in dates:
                re, im = (read(w, j, band, part) for part in range(2))
                keep_sum(ORDER["p", w, band] - start, total([a * a for a in re]) + total([a * a for a in im]))
            for w, k in pairs:
                a_re, a_im = (read(w, j, band, part) for part in range(2))
                b_re, b_im = (read(w + k, j, band, part) for part in range(2))
                re = total([a * b for a, b in zip(a_re, b_re)]) + total([a * b for a, b in zip(a_im, b_im)])
                im = total([a * b for a, b in zip(a_im, b_re)]) - total([a * b for a, b in zip(a_re, b_im)])
                keep_sum(ORDER["r", w, k, band] - start, re)
                keep_sum(ORDER["i", w, k, band] - start, im)

    def own_step(j):
        bands_own[j] = band_split(OWN, j)
        products(OWN, OWN_PAIRS, 0, j)
        red[j, :, 0:OWN_COUNT * SUB] = lax.dot_general(
            selector, both[0:OWN_COUNT * SUB], contract, preferred_element_type=F32
        )

    def far_step(j):
        bands_far[...] = band_split(FAR, j)
        products(FAR, FAR_PAIRS, OWN_COUNT, j)
        red[j, :, OWN_COUNT * SUB:(OWN_COUNT + FAR_COUNT) * SUB] = lax.dot_general(
            selector, both[0:FAR_COUNT * SUB], contract, preferred_element_type=F32
        )

    def wave_signal():
        @pl.when(has_left)
        def _():
            pl.semaphore_signal(wave_sem.at[1], inc=1, device_id={"date": me - SPAN}, device_id_type=mesh_id)

        @pl.when(has_right)
        def _():
            pl.semaphore_signal(wave_sem.at[0], inc=1, device_id={"date": me + SPAN}, device_id_type=mesh_id)

    def wave(t, carry):
        @pl.when(has_left)
        def _():
            pl.semaphore_wait(wave_sem.at[0], 1)

        @pl.when(has_right)
        def _():
            pl.semaphore_wait(wave_sem.at[1], 1)

        @pl.when(t < slabs - 1)
        def _():
            wave_signal()

        return carry

    own_arrive(0, True)
    make_after(OWN)

    wave_signal()

    def stream(t, carry):
        @pl.when(t < steps)
        def _():
            own_arrive(t, False)

        @pl.when(t == steps - 1)
        def _():
            make_before(OWN)

        @pl.when(t < slabs)
        def _():
            wave(t, 0)

        @pl.when((t >= 2) & (t < steps + 2))
        def _():
            own_step(lax.rem(t - 1, steps))

        @pl.when(t == LAG)
        def _():
            far_arrive(0, True)
            make_after(FAR)

        @pl.when((t > LAG) & (t < steps + LAG))
        def _():
            far_arrive(t - LAG, False)

        @pl.when(t == steps + LAG - 1)
        def _():
            make_before(FAR)

        @pl.when(t >= LAG + 2)
        def _():
            far_step(lax.rem(t - LAG - 1, steps))

        return carry

    lax.fori_loop(1, steps + LAG + 2, stream, 0)
    lax.fori_loop(steps + LAG + 2, slabs, wave, 0)

    lane = lax.broadcasted_iota(jnp.int32, (CELLS, LANES), 1)
    for g in range(len(ORDER) // steps):
        rows = [red[j, :, g * LANES:g * LANES + LANES] for j in range(steps)]
        bit = 1
        while bit < steps:
            upper = lax.rem(lane // (SUB * bit), 2) == 1
            turned = list(rows)
            for a in range(steps):
                if a & bit == 0:
                    b = a | bit
                    turned[a] = jnp.where(upper, pltpu.roll(rows[b], SUB * bit, 1), rows[a])
                    turned[b] = jnp.where(upper, rows[b], pltpu.roll(rows[a], LANES - SUB * bit, 1))
            rows = turned
            bit *= 2
        for u in range(steps):
            qty[g * steps + u] = rows[u]

    shape = (SPAN, CELLS, LANES)
    c_id = lax.broadcasted_iota(jnp.int32, shape, 1)
    l_id = lax.broadcasted_iota(jnp.int32, shape, 2)
    last_row = LANES - SUB

    def block_after(x):
        wrap = jnp.where(l_id == LANES - 1, 0.0, pltpu.roll(x, last_row - 1, 2))
        return jnp.where(l_id < last_row, pltpu.roll(x, last_row, 2), wrap)

    def block_before(x):
        wrap = jnp.where(l_id == 0, 0.0, pltpu.roll(x, SUB + 1, 2))
        return jnp.where(l_id >= SUB, pltpu.roll(x, SUB, 2), wrap)

    def box(value):
        prefix = value
        for hop in (1, 2, 4):
            prefix = prefix + jnp.where(c_id >= hop, pltpu.roll(prefix, hop, 1), 0.0)
        whole = jnp.sum(value, axis=1, keepdims=True)
        suffix = whole - prefix + value
        return block_before(suffix) + whole + block_after(prefix)

    def stacked(*keys):
        return jnp.concatenate([qty[ORDER[key]][None] for key in keys], axis=0)

    for k in range(1, SPAN + 1):
        dates = range(first_date(k), first_date(k) + SPAN)
        cr0, cr1 = (stacked(*[("r", w, k, band) for w in dates]) for band in range(2))
        ci0, ci1 = (stacked(*[("i", w, k, band) for w in dates]) for band in range(2))
        ab0, ab1 = (
            stacked(*[("p", w, band) for w in dates]) * stacked(*[("p", w + k, band) for w in dates]) + eps_power
            for band in range(2)
        )
        flag = jnp.concatenate(
            [
                jnp.broadcast_to(
                    recv[w, SLOT + ML_AZ].astype(F32)[k - 1:k, 0:LANES], (CELLS, LANES)
                )[None] for w in dates
            ], axis=0
        )
        weight = flag * 0.5 * ((cr0 * cr0 + ci0 * ci0) / ab0 + (cr1 * cr1 + ci1 * ci1) / ab1)
        phase = split_coef * (ci0 * cr1 - cr0 * ci1) / jnp.sqrt(ab0 * ab1)
        den = box(weight)
        num = box(weight * phase)
        quant[k - 1] = den / (2 * RADIUS + 1)
        quant[SPAN + k - 1] = num / (den + floor_weight)

    kinds = 2 * SPAN
    per = LANES // (SPAN * wide)
    pieces = kinds // per

    def line_copy(target):
        return pltpu.make_async_remote_copy(
            src_ref=msg.at[target], dst_ref=got.at[z],
            send_sem=send_sem.at[3], recv_sem=recv_sem.at[0, steps],
            device_id={"date": target * SPAN + q}, device_id_type=mesh_id,
        )

    def pack_line(target):
        for m in range(pieces):
            value = None
            for u in range(per):
                for g in range(SPAN):
                    at = (u * SPAN + g) * wide
                    shift = lax.rem(at - target * wide + LANES, LANES)
                    moved = pltpu.roll(quant[m * per + u, g], shift, 1)
                    value = moved if value is None else jnp.where(lane >= at, moved, value)
            msg[target, m] = value

    def send_line(target):
        @pl.when(target != z)
        def _():
            line_copy(target).start()

        @pl.when(target == z)
        def _():
            pltpu.make_async_copy(msg.at[z], got.at[z], recv_sem.at[0, steps]).start()

    def each_line(target, carry):
        pack_line(target)
        send_line(target)
        return carry

    if slabs <= steps:
        for target in range(slabs):
            each_line(target, 0)
    else:
        lax.fori_loop(0, slabs, each_line, 0)

    pltpu.make_async_copy(got, got, recv_sem.at[0, steps]).wait()

    regs = n * wide // LANES
    zero = jnp.zeros((CELLS, LANES), F32)

    def gather(kind):
        out = []
        for v in range(regs):
            value = None
            for s in range(v * slabs // regs, (v + 1) * slabs // regs):
                to = s * SPAN * wide - v * LANES
                at = (kind % per) * SPAN * wide
                piece = got[s, kind // per]
                if to != at:
                    piece = pltpu.roll(piece, (to - at) % LANES, 1)
                value = piece if value is None else jnp.where(lane >= to, piece, value)
            out.append(value)
        return out

    def shift(x, dates):
        far, by = divmod(dates * wide, LANES)
        out = []
        for v in range(regs):
            low = x[v + far] if 0 <= v + far < regs else zero
            if by == 0:
                out.append(low)
                continue
            high = x[v + far + 1] if 0 <= v + far + 1 < regs else zero
            out.append(jnp.where(lane < LANES - by, pltpu.roll(low, LANES - by, 1), pltpu.roll(high, LANES - by, 1)))
        return out

    def add(x, y):
        return [a + b for a, b in zip(x, y)]

    ahead, behind = [], []
    wsum = [zero] * regs
    rhs = [zero] * regs
    for k in range(1, SPAN + 1):
        skip = SIDE - first_date(k)
        w = gather(k - 1)
        p = gather(SPAN + k - 1)
        wp = [a * b for a, b in zip(w, p)]
        ahead.append(shift(w, skip))
        behind.append(shift(w, skip - k))
        wsum = add(wsum, add(ahead[-1], behind[-1]))
        rhs = add(rhs, [b - a for a, b in zip(shift(wp, skip), shift(wp, skip - k))])
        if k == 1:
            chain = shift(p, skip)
    hop = 1
    while hop < n:
        chain = add(chain, shift(chain, -hop))
        hop *= 2
    chain = shift(chain, -1)
    rhs = [r + ridge_weight * c for r, c in zip(rhs, chain)]
    inv = [1.0 / (t + ridge_weight) for t in wsum]
    phi = chain
    for sweep in range(ITERS):
        acc = rhs
        for k in range(1, SPAN + 1):
            acc = add(acc, [a * b for a, b in zip(ahead[k - 1], shift(phi, k))])
            acc = add(acc, [a * b for a, b in zip(behind[k - 1], shift(phi, -k))])
        phi = [a * b for a, b in zip(acc, inv)]

    def out_copy(target):
        return pltpu.make_async_remote_copy(
            src_ref=pack.at[target], dst_ref=back.at[me],
            send_sem=send_sem.at[4], recv_sem=recv_sem.at[0, steps + 1],
            device_id={"date": target}, device_id_type=mesh_id,
        )

    mine = lane // wide == z
    half = LANES // 2

    def finish(target, phase, weight, at):
        phase = pltpu.roll(phase, lax.rem(LANES - at, LANES), 1)
        weight = pltpu.roll(weight, lax.rem(LANES - at, LANES), 1)
        pack[target] = jnp.where(mine, phase, weight)

        @pl.when(target != me)
        def _():
            out_copy(target).start()

    phi = [pltpu.roll(x, z * wide, 1) for x in phi]
    wsum = [pltpu.roll(x, lax.rem(z * wide + half, LANES), 1) for x in wsum]
    if n <= 2 * SUB:
        for target in range(n):
            v = target * wide // LANES
            finish(target, phi[v], wsum[v], target * wide % LANES)
    else:
        for v in range(regs):
            fin[0, v] = phi[v]
            fin[1, v] = wsum[v]

        def finish_more(target, carry):
            v = target * wide // LANES
            finish(target, fin[0, v], fin[1, v], lax.rem(target * wide, LANES))
            return carry

        lax.fori_loop(0, n, finish_more, 0)
    pltpu.make_async_copy(pack.at[me], back.at[me], recv_sem.at[0, steps + 1]).start()

    def drain(ref, sem):
        pltpu.make_async_copy(ref, ref, sem).wait()

    tiles = SLOT + ML_AZ * (steps - 1)
    drain(data.at[pl.ds(0, SPAN - 1), pl.ds(0, tiles)], send_sem.at[0])

    @pl.when(has_left)
    def _():
        drain(data.at[pl.ds(0, SIDE), pl.ds(0, tiles)], send_sem.at[1])

    @pl.when(has_right)
    def _():
        drain(data.at[pl.ds(0, SIDE), pl.ds(0, tiles)], send_sem.at[2])

    drain(msg.at[pl.ds(0, slabs - 1)], send_sem.at[3])
    drain(back, recv_sem.at[0, steps + 1])
    drain(pack.at[pl.ds(0, n - 1)], send_sem.at[4])

    rows = []
    for kind in range(2):
        place_of = lax.rem(lane + kind * half, LANES) // wide
        for s in range(SPAN):
            value = zero
            for line in range(slabs):
                value = jnp.where(place_of == line, back[line * SPAN + s], value)
            rows.append(pltpu.roll(value, half, 1) if kind else value)
    value = jnp.concatenate(rows, axis=0)
    high = value.astype(BF16)
    rest = value - high.astype(F32)
    middle = rest.astype(BF16)
    low = (rest - middle.astype(F32)).astype(BF16)
    width = out_ref.shape[2]
    place_row = lax.broadcasted_iota(jnp.int32, (LANES, width), 0)
    place_block = lax.broadcasted_iota(jnp.int32, (LANES, width), 1) // CELLS
    place = place_row == lax.rem(place_block, steps) * SUB + place_block // steps
    spread = jnp.dot(
        jnp.concatenate([high, middle, low], axis=0), jnp.where(place, 1.0, 0.0).astype(BF16),
        preferred_element_type=F32,
    )
    count = 2 * SPAN * CELLS
    spread = spread[0:count] + spread[count:2 * count] + spread[2 * count:3 * count]
    spread = spread.reshape(2 * SPAN, CELLS, width)
    s_row = lax.broadcasted_iota(jnp.int32, spread.shape, 1)
    s_col = lax.broadcasted_iota(jnp.int32, spread.shape, 2)
    result = jnp.sum(jnp.where(lax.rem(s_col, CELLS) == s_row, spread, 0.0), axis=1)
    out_ref[0] = result[0:SPAN]
    out_ref[1] = result[SPAN:2 * SPAN]


def local(slc_stack, band_taps, pair_flags):
    n = lax.axis_size("date")
    rows, span = slc_stack.shape[2:]
    steps = span // LANES // SUB
    slabs = n // SPAN
    assert rows == SUB and rows // ML_AZ == SPAN and span == LANES * LANES
    assert n % SPAN == 0 and LANES % slabs == 0 and slabs % SPAN == 0
    wide = LANES // slabs
    pieces = 2 * SPAN * SPAN * wide // LANES
    regs = n * wide // LANES
    tiles = SLOT * (steps + 2)

    vmem = pl.BlockSpec(memory_space=pltpu.VMEM)
    small = lambda *lead: pltpu.VMEM((*lead, CELLS, LANES), F32)
    sem = lambda *lead: pltpu.SemaphoreType.DMA(lead)
    both = pl.pallas_call(
        functools.partial(kernel, n, steps),
        out_shape=jax.ShapeDtypeStruct((2, rows // ML_AZ, span // ML_RG), F32),
        in_specs=[pl.BlockSpec(memory_space=pl.ANY)] * 3,
        out_specs=vmem,
        scratch_shapes=[
            pltpu.VMEM((2, rows, span), BF16),
            pltpu.VMEM((1, SPAN), jnp.int32),
            pltpu.VMEM((2, 2, TAPS), BF16),
            pltpu.VMEM((8, LANES), F32),
            pltpu.VMEM((2 * SUB * SUB, LANES), F32),
            pltpu.VMEM((SPAN, tiles, SUB, 2 * LANES), BF16),
            pltpu.VMEM((WIN, tiles, SUB, 2 * LANES), BF16),
            pltpu.VMEM((4 * LANES, 4 * LANES), BF16),
            pltpu.VMEM((steps, SPAN, ML_AZ, SUB, 4 * LANES), F32),
            pltpu.VMEM((SPAN, ML_AZ, SUB, 4 * LANES), F32),
            pltpu.VMEM((max(OWN_COUNT, FAR_COUNT) * SUB, 2 * LANES), BF16),
            pltpu.VMEM((steps, CELLS, len(ORDER) * SUB), F32),
            small(len(ORDER)),
            small(2 * SPAN, SPAN),
            small(slabs, pieces),
            small(slabs, pieces),
            small(2, regs),
            small(n),
            small(n),
            sem(3), sem(5), sem(3, steps + 2), pltpu.SemaphoreType.REGULAR((2,)),
        ],
        compiler_params=pltpu.CompilerParams(
            collective_id=0, has_side_effects=True, vmem_limit_bytes=60 * 1024 * 1024
        ),
    )(slc_stack, pair_flags, band_taps)
    return both[0:1], both[1:2]


def solution(mesh):
    in_specs = (P("date", None, "group", None), P(), P("date", None))
    out_specs = (P("date", "group", None), P("date", "group", None))
    return jax.shard_map(local, mesh=mesh, in_specs=in_specs, out_specs=out_specs, check_vma=False)
```

```python
import functools

import jax
import jax.numpy as jnp
from jax import lax
from jax.experimental import pallas as pl
from jax.experimental.pallas import tpu as pltpu
from jax.sharding import PartitionSpec as P

TAPS = 32
ML_AZ = 4
ML_RG = 16
SPAN = 4
RADIUS = 8
ITERS = 4

LANES = 128
CELLS = LANES // ML_RG
SUB = 16
SIDE = SPAN // 2
WIN = SPAN + 2 * SIDE
SLOT = ML_AZ + 1
LAG = 2

eps_power = 1e-06
floor_weight = 0.1
ridge_weight = 0.05
split_coef = 2.0

F32 = jnp.float32
BF16 = jnp.bfloat16

OWN = tuple(range(SIDE, SIDE + SPAN))
FAR = tuple(range(SIDE)) + tuple(range(SIDE + SPAN, WIN))


def first_date(k):
    return 0 if k == SPAN else 1


PAIRS = [(first_date(k) + g, k) for k in range(1, SPAN + 1) for g in range(SPAN)]
OWN_PAIRS = [(w, k) for w, k in PAIRS if w in OWN and w + k in OWN]
FAR_PAIRS = [p for p in PAIRS if p not in OWN_PAIRS]


HALVES = 2
GROUP = SPAN * SPAN // HALVES


def pair_slot(imag, band, w, k):
    return ((2 * band + imag) * HALVES + (k - 1) // HALVES) * GROUP + (k - 1) % HALVES * SPAN + w - first_date(k)


def power_slot(band, w):
    return 4 * HALVES * GROUP + band * WIN + w


SLOTS = power_slot(1, WIN - 1) + 1


def kernel(
    n, steps,
    slc_hbm, flags_hbm, taps_hbm, out_ref,
    slc, flags_in, taps_in, taps_ref, turn, data, recv, mat, bands_own, bands_far, both, red, quant,
    got, pack, back,
    in_sem, send_sem, recv_sem, wave_sem,
):
    me = lax.axis_index("date")
    q = lax.rem(me, SPAN)
    z = me // SPAN
    slabs = n // SPAN
    has_left = z > 0
    has_right = z < slabs - 1
    mesh_id = pl.DeviceIdType.MESH

    slc_load = pltpu.make_async_copy(slc_hbm.at[0], slc, in_sem.at[0])
    slc_load.start()
    flags_load = pltpu.make_async_copy(flags_hbm, flags_in, in_sem.at[1])
    flags_load.start()
    taps_load = pltpu.make_async_copy(taps_hbm, taps_in, in_sem.at[2])
    taps_load.start()
    barrier = pltpu.get_barrier_semaphore()

    for hop in range(1, SPAN):
        pl.semaphore_signal(
            barrier, inc=1, device_id={"date": z * SPAN + lax.rem(q + hop, SPAN)}, device_id_type=mesh_id
        )

    @pl.when(has_left)
    def _():
        pl.semaphore_signal(barrier, inc=1, device_id={"date": me - SPAN}, device_id_type=mesh_id)

    @pl.when(has_right)
    def _():
        pl.semaphore_signal(barrier, inc=1, device_id={"date": me + SPAN}, device_id_type=mesh_id)

    flags_load.wait()
    tile_row = lax.broadcasted_iota(jnp.int32, (SUB, 2 * LANES), 0)
    own_flags = flags_in[...].astype(F32)
    flag_tile = jnp.zeros((SUB, 2 * LANES), F32)
    for k in range(SPAN):
        flag_tile = jnp.where(tile_row == k, jnp.broadcast_to(own_flags[0:1, k:k + 1], flag_tile.shape), flag_tile)
    flag_tile = flag_tile.astype(BF16)
    for s in range(SPAN):
        data[s, SLOT + ML_AZ] = flag_tile
    taps_load.wait()
    taps_ref[...] = jnp.zeros_like(taps_ref)
    for band in range(2):
        taps_ref[2 * band:2 * band + 2, 0:TAPS] = taps_in[band].astype(F32)

    k_id = lax.broadcasted_iota(jnp.int32, (LANES, LANES), 0)
    j_id = lax.broadcasted_iota(jnp.int32, (LANES, LANES), 1)
    reach = k_id - j_id + TAPS // 2
    circ = []
    for m in range(4):
        base = jnp.broadcast_to(taps_ref[m:m + 1, :], (LANES, LANES))
        circ.append(pltpu.roll(base, LANES - TAPS // 2, 1, stride=1, stride_axis=0).T)
    for edge in range(2):
        inside = (reach >= 0) & (reach < LANES)
        keep = inside if edge == 0 else jnp.logical_not(inside)
        row = edge * 2 * LANES
        for band in range(2):
            re_part = jnp.where(keep, circ[2 * band], 0.0).astype(BF16)
            im_value = jnp.where(keep, circ[2 * band + 1], 0.0)
            im_part = im_value.astype(BF16)
            im_minus = (-im_value).astype(BF16)
            col = band * 2 * LANES
            mat[row:row + 128, col:col + 128] = re_part
            mat[row:row + 128, col + 128:col + 256] = im_part
            mat[row + 128:row + 256, col:col + 128] = im_minus
            mat[row + 128:row + 256, col + 128:col + 256] = re_part

    slc_load.wait()

    def regroup(j, carry):
        for part in range(2):
            for i in range(SUB):
                at = pl.multiple_of((steps * i + j) * LANES, LANES)
                value = slc[part, :, pl.ds(at, LANES)].astype(F32)
                turn[(part * SUB + i) * SUB:(part * SUB + i + 1) * SUB, :] = value
        for part in range(2):
            for s in range(SPAN):
                for r in range(ML_AZ):
                    row = part * SUB * SUB + ML_AZ * s + r
                    value = turn[pl.ds(row, SUB, stride=SUB), :].astype(BF16)
                    data[s, SLOT * (j + 1) + r, :, part * LANES:part * LANES + LANES] = value
        return carry

    lax.fori_loop(0, steps, regroup, 0)

    def chunk(ref, j, first):
        return ref.at[pl.ds(SLOT * (j + 1), SLOT if first else ML_AZ)]

    def slab_copy(target, j, first):
        return pltpu.make_async_remote_copy(
            src_ref=chunk(data.at[target], j, first), dst_ref=chunk(recv.at[q + SIDE], j, first),
            send_sem=send_sem.at[0], recv_sem=recv_sem.at[1, j],
            device_id={"date": z * SPAN + target}, device_id_type=mesh_id,
        )

    def own_copy(j, first):
        return pltpu.make_async_copy(
            chunk(data.at[q], j, first), chunk(recv.at[q + SIDE], j, first), recv_sem.at[1, j]
        )

    def side_copy(w, j, first):
        go_left = w < SPAN
        to, device = (w + SPAN, me - SPAN) if go_left else (w - SPAN, me + SPAN)
        return pltpu.make_async_remote_copy(
            src_ref=chunk(recv.at[w], j, first), dst_ref=chunk(recv.at[to], j, first),
            send_sem=send_sem.at[1 if go_left else 2], recv_sem=recv_sem.at[2 if go_left else 0, j],
            device_id={"date": device}, device_id_type=mesh_id,
        )

    def arrived(dates, side, j, first):
        ref = recv.at[pl.ds(dates[0], len(dates)), pl.ds(SLOT * (j + 1), SLOT if first else ML_AZ)]
        pltpu.make_async_copy(ref, ref, recv_sem.at[side, j]).wait()

    near = SPAN - 1 + has_left.astype(jnp.int32) + has_right.astype(jnp.int32)
    pl.semaphore_wait(barrier, near)

    def send_chunk(j, first):
        own_copy(j, first).start()
        for hop in (2, 3, 1):
            slab_copy(lax.rem(q + hop, SPAN), j, first).start()

    send_chunk(0, True)

    def send_more(j, carry):
        send_chunk(j, False)
        return carry

    lax.fori_loop(1, steps, send_more, 0)

    @pl.when(jnp.logical_not(has_left))
    def _():
        for w in range(SIDE):
            recv[w] = jnp.zeros(recv.shape[1:], BF16)

    @pl.when(jnp.logical_not(has_right))
    def _():
        for w in range(SIDE + SPAN, WIN):
            recv[w] = jnp.zeros(recv.shape[1:], BF16)

    sel_row = lax.broadcasted_iota(jnp.int32, (CELLS, 2 * LANES), 0)
    sel_lane = lax.broadcasted_iota(jnp.int32, (CELLS, 2 * LANES), 1)
    selector = jnp.where(lax.rem(sel_lane, LANES) // ML_RG == sel_row, 1.0, 0.0).astype(BF16)
    contract = (((1,), (1,)), ((), ()))
    edge_lane = lax.rem(lax.broadcasted_iota(jnp.int32, (ML_AZ, SUB, 2 * LANES), 2), LANES)
    from_before = edge_lane >= LANES - TAPS // 2
    sub_row = lax.broadcasted_iota(jnp.int32, (ML_AZ, SUB, 2 * LANES), 1)

    def own_arrive(j, first):
        arrived(OWN, 1, j, first)

        @pl.when(has_left)
        def _():
            for w in OWN[:SIDE]:
                side_copy(w, j, first).start()

        @pl.when(has_right)
        def _():
            for w in OWN[SIDE:]:
                side_copy(w, j, first).start()

    def far_arrive(j, first):
        @pl.when(has_left)
        def _():
            arrived(FAR[:SIDE], 0, j, first)

        @pl.when(has_right)
        def _():
            arrived(FAR[SIDE:], 2, j, first)

    def make_after(dates):
        for w in dates:
            value = recv[w, SLOT:SLOT + ML_AZ].astype(F32)
            value = jnp.where(sub_row < SUB - 1, pltpu.roll(value, SUB - 1, 1), 0.0)
            recv[w, SLOT * (steps + 1):SLOT * (steps + 1) + ML_AZ] = value.astype(BF16)

    def make_before(dates):
        for w in dates:
            value = recv[w, SLOT * steps:SLOT * steps + ML_AZ].astype(F32)
            value = jnp.where(sub_row > 0, pltpu.roll(value, 1, 1), 0.0)
            recv[w, 0:ML_AZ] = value.astype(BF16)

    def band_split(dates, j):
        rows = []
        for w in dates:
            here = recv[w, pl.ds(SLOT * (j + 1), ML_AZ)]
            before = recv[w, pl.ds(SLOT * j, ML_AZ)]
            after = recv[w, pl.ds(SLOT * (j + 2), ML_AZ)]
            edge = jnp.where(from_before, before, after)
            rows.append(jnp.concatenate([here, edge], axis=2).reshape(ML_AZ * SUB, 4 * LANES))
        made = jnp.dot(jnp.concatenate(rows, axis=0), mat[...], preferred_element_type=F32)
        return made.astype(BF16).astype(F32).reshape(len(dates), ML_AZ, SUB, 4 * LANES)

    def read(w, j, band, part):
        cols = slice((2 * band + part) * LANES, (2 * band + part + 1) * LANES)
        if w in OWN:
            return [bands_own[j, OWN.index(w), r, :, cols] for r in range(ML_AZ)]
        return [bands_far[FAR.index(w), r, :, cols] for r in range(ML_AZ)]

    def total(terms):
        terms = list(terms)
        while len(terms) > 1:
            terms = [a + b for a, b in zip(terms[::2], terms[1::2])]
        return terms[0]

    def keep_sum(j, at, value):
        high = value.astype(BF16)
        low = (value - high.astype(F32)).astype(BF16)
        both[j, at * SUB:at * SUB + SUB, 0:LANES] = high
        both[j, at * SUB:at * SUB + SUB, LANES:2 * LANES] = low

    def products(dates, pairs, j):
        for band in range(2):
            for w in dates:
                re, im = (read(w, j, band, part) for part in range(2))
                keep_sum(j, power_slot(band, w), total([a * a for a in re]) + total([a * a for a in im]))
            for w, k in pairs:
                a_re, a_im = (read(w, j, band, part) for part in range(2))
                b_re, b_im = (read(w + k, j, band, part) for part in range(2))
                re = total([a * b for a, b in zip(a_re, b_re)]) + total([a * b for a, b in zip(a_im, b_im)])
                im = total([a * b for a, b in zip(a_im, b_re)]) - total([a * b for a, b in zip(a_re, b_im)])
                keep_sum(j, pair_slot(0, band, w, k), re)
                keep_sum(j, pair_slot(1, band, w, k), im)

    def own_step(j):
        bands_own[j] = band_split(OWN, j)
        products(OWN, OWN_PAIRS, j)

    def far_step(j):
        bands_far[...] = band_split(FAR, j)
        products(FAR, FAR_PAIRS, j)
        red[j] = lax.dot_general(selector, both[j], contract, preferred_element_type=F32)

    def wave_signal():
        @pl.when(has_left)
        def _():
            pl.semaphore_signal(wave_sem.at[1], inc=1, device_id={"date": me - SPAN}, device_id_type=mesh_id)

        @pl.when(has_right)
        def _():
            pl.semaphore_signal(wave_sem.at[0], inc=1, device_id={"date": me + SPAN}, device_id_type=mesh_id)

    def wave(t, carry):
        @pl.when(has_left)
        def _():
            pl.semaphore_wait(wave_sem.at[0], 1)

        @pl.when(has_right)
        def _():
            pl.semaphore_wait(wave_sem.at[1], 1)

        @pl.when(t < slabs - 1)
        def _():
            wave_signal()

        return carry

    own_arrive(0, True)
    make_after(OWN)

    wave_signal()

    def stream(t, carry):
        @pl.when(t < steps)
        def _():
            own_arrive(t, False)

        @pl.when(t == steps - 1)
        def _():
            make_before(OWN)

        @pl.when(t < slabs)
        def _():
            wave(t, 0)

        @pl.when((t >= 2) & (t < steps + 2))
        def _():
            own_step(lax.rem(t - 1, steps))

        @pl.when(t == LAG)
        def _():
            far_arrive(0, True)
            make_after(FAR)

        @pl.when((t > LAG) & (t < steps + LAG))
        def _():
            far_arrive(t - LAG, False)

        @pl.when(t == steps + LAG - 1)
        def _():
            make_before(FAR)

        @pl.when(t >= LAG + 2)
        def _():
            far_step(lax.rem(t - LAG - 1, steps))

        return carry

    lax.fori_loop(1, steps + LAG + 2, stream, 0)
    lax.fori_loop(steps + LAG + 2, slabs, wave, 0)

    shape = (steps, CELLS, LANES)
    c_id = lax.broadcasted_iota(jnp.int32, shape, 1)
    l_id = lax.broadcasted_iota(jnp.int32, shape, 2)
    i_id = lax.rem(l_id, SUB)

    def box(value):
        prefix = value
        for hop in (1, 2, 4):
            prefix = prefix + jnp.where(c_id >= hop, pltpu.roll(prefix, hop, 1), 0.0)
        whole = jnp.sum(value, axis=1, keepdims=True)
        suffix = whole - prefix + value
        first = jnp.where(i_id[0:1] > 0, pltpu.roll(suffix[steps - 1:steps], 1, 2), 0.0)
        last = jnp.where(i_id[0:1] < SUB - 1, pltpu.roll(prefix[0:1], LANES - 1, 2), 0.0)
        before = jnp.concatenate([first, suffix[0:steps - 1]], axis=0)
        after = jnp.concatenate([prefix[1:steps], last], axis=0)
        return before + whole + after

    def register(at):
        return red[:, :, at * LANES:at * LANES + LANES]

    lane = lax.broadcasted_iota(jnp.int32, (CELLS, LANES), 1)
    span_lanes = SPAN * SUB

    def aligned(value, ks, partner):
        parts = []
        for at, k in enumerate(ks):
            w = first_date(k) + (k if partner else 0)
            move = (at * SPAN - w) * SUB % LANES
            parts.append(pltpu.roll(value, move, 2) if move else value)
        return jnp.where(l_id < span_lanes, parts[0], parts[1])

    for h in range(HALVES):
        ks = (HALVES * h + 1, HALVES * h + 2)
        cr0, ci0, cr1, ci1 = (register(m * HALVES + h) for m in range(4))
        ab0, ab1 = (
            aligned(power, ks, False) * aligned(power, ks, True) + eps_power
            for power in (register(4 * HALVES), register(4 * HALVES + 1))
        )
        flag = jnp.zeros((CELLS, LANES), F32)
        for at, k in enumerate(ks):
            for g in range(SPAN):
                one = recv[first_date(k) + g, SLOT + ML_AZ].astype(F32)[k - 1:k, 0:LANES]
                flag = jnp.where(lane >= (at * SPAN + g) * SUB, jnp.broadcast_to(one, flag.shape), flag)
        weight = flag[None] * 0.5 * ((cr0 * cr0 + ci0 * ci0) / ab0 + (cr1 * cr1 + ci1 * ci1) / ab1)
        phase = split_coef * (ci0 * cr1 - cr0 * ci1) / jnp.sqrt(ab0 * ab1)
        den = box(weight)
        num = box(weight * phase)
        quant[:, h] = den / (2 * RADIUS + 1)
        quant[:, HALVES + h] = num / (den + floor_weight)

    share = got.shape[1]
    workers = steps // share
    base = (slabs - workers) // 2
    is_worker = (z >= base) & (z < base + workers)

    def line_copy(u):
        return pltpu.make_async_remote_copy(
            src_ref=quant.at[pl.ds(u * share, share)], dst_ref=got.at[z],
            send_sem=send_sem.at[3], recv_sem=recv_sem.at[0, steps],
            device_id={"date": (base + u) * SPAN + q}, device_id_type=mesh_id,
        )

    for u in range(workers):
        @pl.when(z != base + u)
        def _():
            line_copy(u).start()

        @pl.when(z == base + u)
        def _():
            pltpu.make_async_copy(
                quant.at[pl.ds(u * share, share)], got.at[z], recv_sem.at[0, steps]
            ).start()

    def out_copy(target):
        return pltpu.make_async_remote_copy(
            src_ref=pack.at[target], dst_ref=back.at[(z - base) * SPAN + q],
            send_sem=send_sem.at[4], recv_sem=recv_sem.at[0, steps + 1],
            device_id={"date": target}, device_id_type=mesh_id,
        )

    def turned(rows):
        rows = list(rows)
        bit = 1
        while bit < len(rows):
            upper = lax.rem(lane // (SUB * bit), 2) == 1
            for a in range(len(rows)):
                if a & bit == 0:
                    low, high = rows[a], rows[a | bit]
                    rows[a] = jnp.where(upper, pltpu.roll(high, SUB * bit, 1), low)
                    rows[a | bit] = jnp.where(upper, high, pltpu.roll(low, LANES - SUB * bit, 1))
            bit *= 2
        return rows

    regs = n * SUB // LANES
    zero = jnp.zeros((CELLS, LANES), F32)
    per = LANES // span_lanes

    def gather(jj, kind, k):
        out = []
        at = (k - 1) % HALVES * span_lanes
        for v in range(regs):
            value = None
            for m in range(per):
                piece = got[v * per + m, jj, kind * HALVES + (k - 1) // HALVES]
                move = (m * span_lanes - at) % LANES
                piece = pltpu.roll(piece, move, 1) if move else piece
                value = piece if value is None else jnp.where(lane >= m * span_lanes, piece, value)
            out.append(value)
        return out

    def shift(x, dates):
        far, by = divmod(dates * SUB, LANES)
        out = []
        for v in range(regs):
            low = x[v + far] if 0 <= v + far < regs else zero
            if by == 0:
                out.append(low)
                continue
            high = x[v + far + 1] if 0 <= v + far + 1 < regs else zero
            out.append(pltpu.roll(jnp.where(lane >= by, low, high), LANES - by, 1))
        return out

    def add(x, y):
        return [a + b for a, b in zip(x, y)]

    def relax(jj):
        ahead, behind = [], []
        wsum = [zero] * regs
        rhs = [zero] * regs
        for k in range(1, SPAN + 1):
            skip = SIDE - first_date(k)
            w = gather(jj, 0, k)
            p = gather(jj, 1, k)
            wp = [a * b for a, b in zip(w, p)]
            ahead.append(shift(w, skip))
            behind.append(shift(w, skip - k))
            wsum = add(wsum, add(ahead[-1], behind[-1]))
            rhs = add(rhs, [b - a for a, b in zip(shift(wp, skip), shift(wp, skip - k))])
            if k == 1:
                chain = shift(p, skip)
        hop = 1
        while hop < n:
            chain = add(chain, shift(chain, -hop))
            hop *= 2
        chain = shift(chain, -1)
        rhs = [r + ridge_weight * c for r, c in zip(rhs, chain)]
        inv = [1.0 / (t + ridge_weight) for t in wsum]
        phi = chain
        for sweep in range(ITERS):
            acc = rhs
            for k in range(1, SPAN + 1):
                acc = add(acc, [a * b for a, b in zip(ahead[k - 1], shift(phi, k))])
                acc = add(acc, [a * b for a, b in zip(behind[k - 1], shift(phi, -k))])
            phi = [a * b for a, b in zip(acc, inv)]
        return phi, wsum

    half = LANES // 2
    ranks = LANES // SUB

    @pl.when(is_worker)
    def _():
        pltpu.make_async_copy(got, got, recv_sem.at[0, steps]).wait()
        made = [relax(jj) for jj in range(share)]
        for v in range(regs):
            rows = [zero] * ranks
            for jj in range(share):
                for kind in range(2):
                    rows[kind * ranks // 2 + jj] = made[jj][kind][v]
            for d, value in enumerate(turned(rows)):
                pack[v * ranks + d] = value

        def send_back(i, carry):
            out_copy(lax.rem(me + i, n)).start()
            return carry

        lax.fori_loop(1, n, send_back, 0)
        pltpu.make_async_copy(
            pack.at[me], back.at[(z - base) * SPAN + q], recv_sem.at[0, steps + 1]
        ).start()

    def drain(ref, sem):
        pltpu.make_async_copy(ref, ref, sem).wait()

    tiles = SLOT + ML_AZ * (steps - 1)
    drain(data.at[pl.ds(0, SPAN - 1), pl.ds(0, tiles)], send_sem.at[0])

    @pl.when(has_left)
    def _():
        drain(data.at[pl.ds(0, SIDE), pl.ds(0, tiles)], send_sem.at[1])

    @pl.when(has_right)
    def _():
        drain(data.at[pl.ds(0, SIDE), pl.ds(0, tiles)], send_sem.at[2])

    drain(quant.at[pl.ds(0, steps - share)], send_sem.at[3])

    @pl.when(jnp.logical_not(is_worker))
    def _():
        drain(quant.at[pl.ds(0, share)], send_sem.at[3])

    drain(back, recv_sem.at[0, steps + 1])

    @pl.when(is_worker)
    def _():
        drain(pack.at[pl.ds(0, n - 1)], send_sem.at[4])

    rows = []
    for kind in range(2):
        for s in range(SPAN):
            value = None
            for u in range(workers):
                move = (u * share * SUB - kind * half) % LANES
                piece = back[u * SPAN + s]
                piece = pltpu.roll(piece, move, 1) if move else piece
                value = piece if value is None else jnp.where(lane >= u * share * SUB, piece, value)
            rows.append(value)
    value = jnp.concatenate(rows, axis=0)
    high = value.astype(BF16)
    rest = value - high.astype(F32)
    middle = rest.astype(BF16)
    low = (rest - middle.astype(F32)).astype(BF16)
    width = out_ref.shape[2]
    place_row = lax.broadcasted_iota(jnp.int32, (LANES, width), 0)
    place_block = lax.broadcasted_iota(jnp.int32, (LANES, width), 1) // CELLS
    place = place_row == lax.rem(place_block, steps) * SUB + place_block // steps
    spread = jnp.dot(
        jnp.concatenate([high, middle, low], axis=0), jnp.where(place, 1.0, 0.0).astype(BF16),
        preferred_element_type=F32,
    )
    count = 2 * SPAN * CELLS
    spread = spread[0:count] + spread[count:2 * count] + spread[2 * count:3 * count]
    spread = spread.reshape(2 * SPAN, CELLS, width)
    s_row = lax.broadcasted_iota(jnp.int32, spread.shape, 1)
    s_col = lax.broadcasted_iota(jnp.int32, spread.shape, 2)
    result = jnp.sum(jnp.where(lax.rem(s_col, CELLS) == s_row, spread, 0.0), axis=1)
    out_ref[0] = result[0:SPAN]
    out_ref[1] = result[SPAN:2 * SPAN]


def local(slc_stack, band_taps, pair_flags):
    n = lax.axis_size("date")
    rows, span = slc_stack.shape[2:]
    steps = span // LANES // SUB
    slabs = n // SPAN
    assert rows == SUB and rows // ML_AZ == SPAN and span == LANES * LANES
    assert n % (LANES // SUB) == 0 and steps == LANES // SUB
    workers = 1
    while 2 * workers <= min(steps, slabs // 2):
        workers *= 2
    tiles = SLOT * (steps + 2)

    vmem = pl.BlockSpec(memory_space=pltpu.VMEM)
    small = lambda *lead: pltpu.VMEM((*lead, CELLS, LANES), F32)
    sem = lambda *lead: pltpu.SemaphoreType.DMA(lead)
    both = pl.pallas_call(
        functools.partial(kernel, n, steps),
        out_shape=jax.ShapeDtypeStruct((2, rows // ML_AZ, span // ML_RG), F32),
        in_specs=[pl.BlockSpec(memory_space=pl.ANY)] * 3,
        out_specs=vmem,
        scratch_shapes=[
            pltpu.VMEM((2, rows, span), BF16),
            pltpu.VMEM((1, SPAN), jnp.int32),
            pltpu.VMEM((2, 2, TAPS), BF16),
            pltpu.VMEM((8, LANES), F32),
            pltpu.VMEM((2 * SUB * SUB, LANES), F32),
            pltpu.VMEM((SPAN, tiles, SUB, 2 * LANES), BF16),
            pltpu.VMEM((WIN, tiles, SUB, 2 * LANES), BF16),
            pltpu.VMEM((4 * LANES, 4 * LANES), BF16),
            pltpu.VMEM((steps, SPAN, ML_AZ, SUB, 4 * LANES), F32),
            pltpu.VMEM((SPAN, ML_AZ, SUB, 4 * LANES), F32),
            pltpu.VMEM((steps, SLOTS * SUB, 2 * LANES), BF16),
            pltpu.VMEM((steps, CELLS, SLOTS * SUB), F32),
            small(steps, 2 * HALVES),
            small(slabs, steps // workers, 2 * HALVES),
            small(n),
            small(workers * SPAN),
            sem(3), sem(5), sem(3, steps + 2), pltpu.SemaphoreType.REGULAR((2,)),
        ],
        compiler_params=pltpu.CompilerParams(
            collective_id=0, has_side_effects=True, vmem_limit_bytes=60 * 1024 * 1024
        ),
    )(slc_stack, pair_flags, band_taps)
    return both[0:1], both[1:2]


def solution(mesh):
    in_specs = (P("date", None, "group", None), P(), P("date", None))
    out_specs = (P("date", "group", None), P("date", "group", None))
    return jax.shard_map(local, mesh=mesh, in_specs=in_specs, out_specs=out_specs, check_vma=False)
```

```python
import functools

import jax
import jax.numpy as jnp
from jax import lax
from jax.experimental import pallas as pl
from jax.experimental.pallas import tpu as pltpu
from jax.sharding import PartitionSpec as P

TAPS = 32
ML_AZ = 4
ML_RG = 16
SPAN = 4
RADIUS = 8
ITERS = 4

LANES = 128
CELLS = LANES // ML_RG
SUB = 16
SIDE = SPAN // 2
WIN = SPAN + 2 * SIDE
SLOT = ML_AZ + 2
REACH = TAPS // 2
LAG = 3

eps_power = 1e-06
floor_weight = 0.1
ridge_weight = 0.05
split_coef = 2.0

F32 = jnp.float32
BF16 = jnp.bfloat16

OWN = tuple(range(SIDE, SIDE + SPAN))
FAR = tuple(range(SIDE)) + tuple(range(SIDE + SPAN, WIN))


def first_date(k):
    return 0 if k == SPAN else 1


PAIRS = [(first_date(k) + g, k) for k in range(1, SPAN + 1) for g in range(SPAN)]
OWN_PAIRS = [(w, k) for w, k in PAIRS if w in OWN and w + k in OWN]
FAR_PAIRS = [p for p in PAIRS if p not in OWN_PAIRS]


HALVES = 2
GROUP = SPAN * SPAN // HALVES


def pair_slot(imag, band, w, k):
    return ((2 * band + imag) * HALVES + (k - 1) // HALVES) * GROUP + (k - 1) % HALVES * SPAN + w - first_date(k)


def power_slot(band, w):
    return 4 * HALVES * GROUP + band * WIN + w


SLOTS = power_slot(1, WIN - 1) + 1


def kernel(
    n, steps,
    slc_hbm, flags_hbm, taps_hbm, out_ref,
    slc, flags_in, taps_in, taps_ref, turn, data, recv, mat, bands_own, bands_far, both, red, quant,
    got, pack, back, place,
    in_sem, send_sem, recv_sem, wave_sem,
):
    me = lax.axis_index("date")
    q = lax.rem(me, SPAN)
    z = me // SPAN
    slabs = n // SPAN
    has_left = z > 0
    has_right = z < slabs - 1
    mesh_id = pl.DeviceIdType.MESH

    slc_load = pltpu.make_async_copy(slc_hbm.at[0], slc, in_sem.at[0])
    slc_load.start()
    flags_load = pltpu.make_async_copy(flags_hbm, flags_in, in_sem.at[1])
    flags_load.start()
    taps_load = pltpu.make_async_copy(taps_hbm, taps_in, in_sem.at[2])
    taps_load.start()
    barrier = pltpu.get_barrier_semaphore()

    for hop in range(1, SPAN):
        pl.semaphore_signal(
            barrier, inc=1, device_id={"date": z * SPAN + lax.rem(q + hop, SPAN)}, device_id_type=mesh_id
        )

    @pl.when(has_left)
    def _():
        pl.semaphore_signal(barrier, inc=1, device_id={"date": me - SPAN}, device_id_type=mesh_id)

    @pl.when(has_right)
    def _():
        pl.semaphore_signal(barrier, inc=1, device_id={"date": me + SPAN}, device_id_type=mesh_id)

    flags_load.wait()
    tile_row = lax.broadcasted_iota(jnp.int32, (SUB, 2 * LANES), 0)
    own_flags = flags_in[...].astype(F32)
    flag_tile = jnp.zeros((SUB, 2 * LANES), F32)
    for k in range(SPAN):
        flag_tile = jnp.where(tile_row == k, jnp.broadcast_to(own_flags[0:1, k:k + 1], flag_tile.shape), flag_tile)
    flag_tile = flag_tile.astype(BF16)
    for s in range(SPAN):
        data[s, SLOT + ML_AZ] = flag_tile
    taps_load.wait()
    taps_ref[...] = jnp.zeros_like(taps_ref)
    for band in range(2):
        taps_ref[2 * band:2 * band + 2, 0:TAPS] = taps_in[band].astype(F32)

    k_id = lax.broadcasted_iota(jnp.int32, (LANES, LANES), 0)
    j_id = lax.broadcasted_iota(jnp.int32, (LANES, LANES), 1)
    reach = k_id - j_id + TAPS // 2
    circ = []
    for m in range(4):
        base = jnp.broadcast_to(taps_ref[m:m + 1, :], (LANES, LANES))
        circ.append(pltpu.roll(base, LANES - TAPS // 2, 1, stride=1, stride_axis=0).T)
    for edge in range(2):
        inside = (reach >= 0) & (reach < LANES)
        keep = inside if edge == 0 else jnp.logical_not(inside)
        row = edge * 2 * LANES
        for band in range(2):
            re_part = jnp.where(keep, circ[2 * band], 0.0).astype(BF16)
            im_value = jnp.where(keep, circ[2 * band + 1], 0.0)
            im_part = im_value.astype(BF16)
            im_minus = (-im_value).astype(BF16)
            col = band * 2 * LANES
            mat[row:row + 128, col:col + 128] = re_part
            mat[row:row + 128, col + 128:col + 256] = im_part
            mat[row + 128:row + 256, col:col + 128] = im_minus
            mat[row + 128:row + 256, col + 128:col + 256] = re_part

    slc_load.wait()

    def regroup(j, carry):
        for part in range(2):
            for i in range(SUB):
                at = pl.multiple_of((steps * i + j) * LANES, LANES)
                value = slc[part, :, pl.ds(at, LANES)].astype(F32)
                turn[(part * SUB + i) * SUB:(part * SUB + i + 1) * SUB, :] = value
        for part in range(2):
            for s in range(SPAN):
                for r in range(ML_AZ):
                    row = part * SUB * SUB + ML_AZ * s + r
                    value = turn[pl.ds(row, SUB, stride=SUB), :].astype(BF16)
                    data[s, SLOT * (j + 1) + r, :, part * LANES:part * LANES + LANES] = value
        return carry

    tap_lane = lax.broadcasted_iota(jnp.int32, (SUB, LANES), 1)


    def edge_at(r, part):
        return r // 2, (r % 2 * 2 + part) * 2 * REACH

    def send_edges():
        for s in range(SPAN):
            packed = [None, None]
            for r in range(ML_AZ):
                for part in range(2):
                    value = data[s, SLOT * steps + r, :, part * LANES:part * LANES + LANES].astype(F32)
                    tile, at = edge_at(r, part)
                    head = pltpu.roll(value, at, 1) if at else value
                    tail = pltpu.roll(value, (at + 2 * REACH) % LANES, 1)
                    both_ends = jnp.where(tap_lane < at + REACH, head, tail)
                    old = packed[tile]
                    packed[tile] = both_ends if old is None else jnp.where(tap_lane >= at, both_ends, old)
            data[s, SLOT + ML_AZ + 1] = jnp.concatenate(packed, axis=1).astype(BF16)

    regroup(steps - 1, 0)
    send_edges()
    regroup(0, 0)
    regroup(1, 0)

    def chunk(ref, j, first):
        return ref.at[pl.ds(SLOT * (j + 1), SLOT if first else ML_AZ)]

    def slab_copy(target, j, first):
        return pltpu.make_async_remote_copy(
            src_ref=chunk(data.at[target], j, first), dst_ref=chunk(recv.at[q + SIDE], j, first),
            send_sem=send_sem.at[0], recv_sem=recv_sem.at[1, j],
            device_id={"date": z * SPAN + target}, device_id_type=mesh_id,
        )

    def own_copy(j, first):
        return pltpu.make_async_copy(
            chunk(data.at[q], j, first), chunk(recv.at[q + SIDE], j, first), recv_sem.at[1, j]
        )

    def side_copy(w, j, first):
        go_left = w < SPAN
        to, device = (w + SPAN, me - SPAN) if go_left else (w - SPAN, me + SPAN)
        return pltpu.make_async_remote_copy(
            src_ref=chunk(recv.at[w], j, first), dst_ref=chunk(recv.at[to], j, first),
            send_sem=send_sem.at[1 if go_left else 2], recv_sem=recv_sem.at[2 if go_left else 0, j],
            device_id={"date": device}, device_id_type=mesh_id,
        )

    def arrived(dates, side, j, first):
        ref = recv.at[pl.ds(dates[0], len(dates)), pl.ds(SLOT * (j + 1), SLOT if first else ML_AZ)]
        pltpu.make_async_copy(ref, ref, recv_sem.at[side, j]).wait()

    near = SPAN - 1 + has_left.astype(jnp.int32) + has_right.astype(jnp.int32)
    pl.semaphore_wait(barrier, near)

    def send_chunk(j, first):
        own_copy(j, first).start()
        for hop in (2, 3, 1):
            slab_copy(lax.rem(q + hop, SPAN), j, first).start()

    send_chunk(0, True)

    def send_more(j, carry):
        regroup(j + 1, 0)
        send_chunk(j, False)
        return carry

    lax.fori_loop(1, steps - 2, send_more, 0)
    for j in range(steps - 2, steps):
        send_chunk(j, False)

    @pl.when(jnp.logical_not(has_left))
    def _():
        for w in range(SIDE):
            recv[w] = jnp.zeros(recv.shape[1:], BF16)

    @pl.when(jnp.logical_not(has_right))
    def _():
        for w in range(SIDE + SPAN, WIN):
            recv[w] = jnp.zeros(recv.shape[1:], BF16)

    width = out_ref.shape[2]
    place_row = lax.broadcasted_iota(jnp.int32, (LANES, width), 0)
    place_block = lax.broadcasted_iota(jnp.int32, (LANES, width), 1) // CELLS
    on_place = place_row == lax.rem(place_block, steps) * SUB + place_block // steps
    place[...] = jnp.where(on_place, 1.0, 0.0).astype(BF16)

    sel_row = lax.broadcasted_iota(jnp.int32, (CELLS, 2 * LANES), 0)
    sel_lane = lax.broadcasted_iota(jnp.int32, (CELLS, 2 * LANES), 1)
    selector = jnp.where(lax.rem(sel_lane, LANES) // ML_RG == sel_row, 1.0, 0.0).astype(BF16)
    contract = (((1,), (1,)), ((), ()))
    edge_lane = lax.rem(lax.broadcasted_iota(jnp.int32, (ML_AZ, SUB, 2 * LANES), 2), LANES)
    from_before = edge_lane >= LANES - TAPS // 2
    sub_row = lax.broadcasted_iota(jnp.int32, (ML_AZ, SUB, 2 * LANES), 1)

    def own_arrive(j, first):
        arrived(OWN, 1, j, first)

        @pl.when(has_left)
        def _():
            for w in OWN[:SIDE]:
                side_copy(w, j, first).start()

        @pl.when(has_right)
        def _():
            for w in OWN[SIDE:]:
                side_copy(w, j, first).start()

    def far_arrive(j, first):
        @pl.when(has_left)
        def _():
            arrived(FAR[:SIDE], 0, j, first)

        @pl.when(has_right)
        def _():
            arrived(FAR[SIDE:], 2, j, first)

    def make_after(dates):
        for w in dates:
            value = recv[w, SLOT:SLOT + ML_AZ].astype(F32)
            value = jnp.where(sub_row < SUB - 1, pltpu.roll(value, SUB - 1, 1), 0.0)
            recv[w, SLOT * (steps + 1):SLOT * (steps + 1) + ML_AZ] = value.astype(BF16)

    def make_edges(dates):
        for w in dates:
            tiles = recv[w, SLOT + ML_AZ + 1].astype(F32)
            for r in range(ML_AZ):
                before, after = [], []
                for part in range(2):
                    tile, at = edge_at(r, part)
                    value = tiles[:, tile * LANES:tile * LANES + LANES]
                    after.append(pltpu.roll(value, LANES - at, 1) if at else value)
                    value = pltpu.roll(value, (LANES - 2 * REACH - at) % LANES, 1)
                    before.append(jnp.where(tile_row[:, 0:LANES] > 0, pltpu.roll(value, 1, 0), 0.0))
                recv[w, r] = jnp.concatenate(before, axis=1).astype(BF16)
                recv[w, SLOT * (steps + 2) + r] = jnp.concatenate(after, axis=1).astype(BF16)

    def band_split(dates, j):
        rows = []
        behind = SLOT * jnp.where(j == steps - 2, steps + 2, j + 2)
        for w in dates:
            here = recv[w, pl.ds(SLOT * (j + 1), ML_AZ)]
            before = recv[w, pl.ds(SLOT * j, ML_AZ)]
            after = recv[w, pl.ds(behind, ML_AZ)]
            edge = jnp.where(from_before, before, after)
            rows.append(jnp.concatenate([here, edge], axis=2).reshape(ML_AZ * SUB, 4 * LANES))
        made = jnp.dot(jnp.concatenate(rows, axis=0), mat[...], preferred_element_type=F32)
        return made.astype(BF16).astype(F32).reshape(len(dates), ML_AZ, SUB, 4 * LANES)

    def read(w, j, band, part):
        cols = slice((2 * band + part) * LANES, (2 * band + part + 1) * LANES)
        if w in OWN:
            return [bands_own[j, OWN.index(w), r, :, cols] for r in range(ML_AZ)]
        return [bands_far[FAR.index(w), r, :, cols] for r in range(ML_AZ)]

    def total(terms):
        terms = list(terms)
        while len(terms) > 1:
            terms = [a + b for a, b in zip(terms[::2], terms[1::2])]
        return terms[0]

    def keep_sum(j, at, value):
        high = value.astype(BF16)
        low = (value - high.astype(F32)).astype(BF16)
        both[j, at * SUB:at * SUB + SUB, 0:LANES] = high
        both[j, at * SUB:at * SUB + SUB, LANES:2 * LANES] = low

    def products(dates, pairs, j):
        for band in range(2):
            for w in dates:
                re, im = (read(w, j, band, part) for part in range(2))
                keep_sum(j, power_slot(band, w), total([a * a for a in re]) + total([a * a for a in im]))
            for w, k in pairs:
                a_re, a_im = (read(w, j, band, part) for part in range(2))
                b_re, b_im = (read(w + k, j, band, part) for part in range(2))
                re = total([a * b for a, b in zip(a_re, b_re)]) + total([a * b for a, b in zip(a_im, b_im)])
                im = total([a * b for a, b in zip(a_im, b_re)]) - total([a * b for a, b in zip(a_re, b_im)])
                keep_sum(j, pair_slot(0, band, w, k), re)
                keep_sum(j, pair_slot(1, band, w, k), im)

    def own_step(j):
        bands_own[j] = band_split(OWN, j)
        products(OWN, OWN_PAIRS, j)

    def far_step(j):
        bands_far[...] = band_split(FAR, j)
        products(FAR, FAR_PAIRS, j)
        red[j] = lax.dot_general(selector, both[j], contract, preferred_element_type=F32)

    def wave_signal():
        @pl.when(has_left)
        def _():
            pl.semaphore_signal(wave_sem.at[1], inc=1, device_id={"date": me - SPAN}, device_id_type=mesh_id)

        @pl.when(has_right)
        def _():
            pl.semaphore_signal(wave_sem.at[0], inc=1, device_id={"date": me + SPAN}, device_id_type=mesh_id)

    def wave(t, carry):
        @pl.when(has_left)
        def _():
            pl.semaphore_wait(wave_sem.at[0], 1)

        @pl.when(has_right)
        def _():
            pl.semaphore_wait(wave_sem.at[1], 1)

        @pl.when(t < slabs - 1)
        def _():
            wave_signal()

        return carry

    own_arrive(0, True)
    make_after(OWN)
    make_edges(OWN)

    wave_signal()

    def stream(t, carry):
        u = t - LAG

        @pl.when(t < steps)
        def _():
            own_arrive(t, False)

        @pl.when(t < slabs)
        def _():
            wave(t, 0)

        @pl.when(t <= steps)
        def _():
            own_step(t - 1)

        @pl.when(u == 0)
        def _():
            far_arrive(0, True)
            make_after(FAR)
            make_edges(FAR)

        @pl.when((u > 0) & (u < steps - 1))
        def _():
            far_arrive(u, False)

        @pl.when(u > 0)
        def _():
            far_step(u - 1)

        @pl.when(u == steps - 1)
        def _():
            far_arrive(u, False)

        return carry

    lax.fori_loop(1, steps + LAG + 1, stream, 0)
    lax.fori_loop(steps + LAG + 1, slabs, wave, 0)

    shape = (steps, CELLS, LANES)
    c_id = lax.broadcasted_iota(jnp.int32, shape, 1)
    l_id = lax.broadcasted_iota(jnp.int32, shape, 2)
    i_id = lax.rem(l_id, SUB)

    def box(value):
        prefix = value
        for hop in (1, 2, 4):
            prefix = prefix + jnp.where(c_id >= hop, pltpu.roll(prefix, hop, 1), 0.0)
        whole = jnp.sum(value, axis=1, keepdims=True)
        suffix = whole - prefix + value
        first = jnp.where(i_id[0:1] > 0, pltpu.roll(suffix[steps - 1:steps], 1, 2), 0.0)
        last = jnp.where(i_id[0:1] < SUB - 1, pltpu.roll(prefix[0:1], LANES - 1, 2), 0.0)
        before = jnp.concatenate([first, suffix[0:steps - 1]], axis=0)
        after = jnp.concatenate([prefix[1:steps], last], axis=0)
        return before + whole + after

    def register(at):
        return red[:, :, at * LANES:at * LANES + LANES]

    lane = lax.broadcasted_iota(jnp.int32, (CELLS, LANES), 1)
    span_lanes = SPAN * SUB

    def aligned(value, ks, partner):
        parts = []
        for at, k in enumerate(ks):
            w = first_date(k) + (k if partner else 0)
            move = (at * SPAN - w) * SUB % LANES
            parts.append(pltpu.roll(value, move, 2) if move else value)
        return jnp.where(l_id < span_lanes, parts[0], parts[1])

    for h in range(HALVES):
        ks = (HALVES * h + 1, HALVES * h + 2)
        cr0, ci0, cr1, ci1 = (register(m * HALVES + h) for m in range(4))
        ab0, ab1 = (
            aligned(power, ks, False) * aligned(power, ks, True) + eps_power
            for power in (register(4 * HALVES), register(4 * HALVES + 1))
        )
        flag = jnp.zeros((CELLS, LANES), F32)
        for at, k in enumerate(ks):
            for g in range(SPAN):
                one = recv[first_date(k) + g, SLOT + ML_AZ].astype(F32)[k - 1:k, 0:LANES]
                flag = jnp.where(lane >= (at * SPAN + g) * SUB, jnp.broadcast_to(one, flag.shape), flag)
        weight = flag[None] * 0.5 * ((cr0 * cr0 + ci0 * ci0) / ab0 + (cr1 * cr1 + ci1 * ci1) / ab1)
        phase = split_coef * (ci0 * cr1 - cr0 * ci1) / jnp.sqrt(ab0 * ab1)
        den = box(weight)
        num = box(weight * phase)
        quant[:, h] = den / (2 * RADIUS + 1)
        quant[:, HALVES + h] = num / (den + floor_weight)

    share = got.shape[1]
    workers = steps // share
    base = (slabs - workers) // 2
    is_worker = (z >= base) & (z < base + workers)

    def line_copy(u):
        return pltpu.make_async_remote_copy(
            src_ref=quant.at[pl.ds(u * share, share)], dst_ref=got.at[z],
            send_sem=send_sem.at[3], recv_sem=recv_sem.at[0, steps],
            device_id={"date": (base + u) * SPAN + q}, device_id_type=mesh_id,
        )

    for u in range(workers):
        @pl.when(z != base + u)
        def _():
            line_copy(u).start()

        @pl.when(z == base + u)
        def _():
            pltpu.make_async_copy(
                quant.at[pl.ds(u * share, share)], got.at[z], recv_sem.at[0, steps]
            ).start()

    def out_copy(target):
        return pltpu.make_async_remote_copy(
            src_ref=pack.at[target], dst_ref=back.at[(z - base) * SPAN + q],
            send_sem=send_sem.at[4], recv_sem=recv_sem.at[0, steps + 1],
            device_id={"date": target}, device_id_type=mesh_id,
        )

    def turned(rows):
        rows = list(rows)
        bit = 1
        while bit < len(rows):
            upper = lax.rem(lane // (SUB * bit), 2) == 1
            for a in range(len(rows)):
                if a & bit == 0:
                    low, high = rows[a], rows[a | bit]
                    rows[a] = jnp.where(upper, pltpu.roll(high, SUB * bit, 1), low)
                    rows[a | bit] = jnp.where(upper, high, pltpu.roll(low, LANES - SUB * bit, 1))
            bit *= 2
        return rows

    regs = n * SUB // LANES
    zero = jnp.zeros((CELLS, LANES), F32)
    per = LANES // span_lanes

    def gather(jj, kind, k):
        out = []
        at = (k - 1) % HALVES * span_lanes
        for v in range(regs):
            value = None
            for m in range(per):
                piece = got[v * per + m, jj, kind * HALVES + (k - 1) // HALVES]
                move = (m * span_lanes - at) % LANES
                piece = pltpu.roll(piece, move, 1) if move else piece
                value = piece if value is None else jnp.where(lane >= m * span_lanes, piece, value)
            out.append(value)
        return out

    def shift(x, dates):
        far, by = divmod(dates * SUB, LANES)
        out = []
        for v in range(regs):
            low = x[v + far] if 0 <= v + far < regs else zero
            if by == 0:
                out.append(low)
                continue
            high = x[v + far + 1] if 0 <= v + far + 1 < regs else zero
            out.append(pltpu.roll(jnp.where(lane >= by, low, high), LANES - by, 1))
        return out

    def add(x, y):
        return [a + b for a, b in zip(x, y)]

    def relax(jj):
        ahead, behind = [], []
        wsum = [zero] * regs
        rhs = [zero] * regs
        for k in range(1, SPAN + 1):
            skip = SIDE - first_date(k)
            w = gather(jj, 0, k)
            p = gather(jj, 1, k)
            wp = [a * b for a, b in zip(w, p)]
            ahead.append(shift(w, skip))
            behind.append(shift(w, skip - k))
            wsum = add(wsum, add(ahead[-1], behind[-1]))
            rhs = add(rhs, [b - a for a, b in zip(shift(wp, skip), shift(wp, skip - k))])
            if k == 1:
                chain = shift(p, skip)
        hop = 1
        while hop < n:
            chain = add(chain, shift(chain, -hop))
            hop *= 2
        chain = shift(chain, -1)
        rhs = [r + ridge_weight * c for r, c in zip(rhs, chain)]
        inv = [1.0 / (t + ridge_weight) for t in wsum]
        phi = chain
        for sweep in range(ITERS):
            acc = rhs
            for k in range(1, SPAN + 1):
                acc = add(acc, [a * b for a, b in zip(ahead[k - 1], shift(phi, k))])
                acc = add(acc, [a * b for a, b in zip(behind[k - 1], shift(phi, -k))])
            phi = [a * b for a, b in zip(acc, inv)]
        return phi, wsum

    half = LANES // 2
    ranks = LANES // SUB

    @pl.when(is_worker)
    def _():
        pltpu.make_async_copy(got, got, recv_sem.at[0, steps]).wait()
        made = [relax(jj) for jj in range(share)]
        for v in range(regs):
            rows = [zero] * ranks
            for jj in range(share):
                for kind in range(2):
                    rows[kind * ranks // 2 + jj] = made[jj][kind][v]
            for d, value in enumerate(turned(rows)):
                pack[v * ranks + d] = value

        def send_back(i, carry):
            out_copy(lax.rem(me + i, n)).start()
            return carry

        lax.fori_loop(1, n, send_back, 0)
        pltpu.make_async_copy(
            pack.at[me], back.at[(z - base) * SPAN + q], recv_sem.at[0, steps + 1]
        ).start()

    def drain(ref, sem):
        pltpu.make_async_copy(ref, ref, sem).wait()

    tiles = SLOT + ML_AZ * (steps - 1)
    drain(data.at[pl.ds(0, SPAN - 1), pl.ds(0, tiles)], send_sem.at[0])

    @pl.when(has_left)
    def _():
        drain(data.at[pl.ds(0, SIDE), pl.ds(0, tiles)], send_sem.at[1])

    @pl.when(has_right)
    def _():
        drain(data.at[pl.ds(0, SIDE), pl.ds(0, tiles)], send_sem.at[2])

    drain(quant.at[pl.ds(0, steps - share)], send_sem.at[3])

    @pl.when(jnp.logical_not(is_worker))
    def _():
        drain(quant.at[pl.ds(0, share)], send_sem.at[3])

    drain(back, recv_sem.at[0, steps + 1])

    @pl.when(is_worker)
    def _():
        drain(pack.at[pl.ds(0, n - 1)], send_sem.at[4])

    rows = []
    for kind in range(2):
        for s in range(SPAN):
            value = None
            for u in range(workers):
                move = (u * share * SUB - kind * half) % LANES
                piece = back[u * SPAN + s]
                piece = pltpu.roll(piece, move, 1) if move else piece
                value = piece if value is None else jnp.where(lane >= u * share * SUB, piece, value)
            rows.append(value)
    value = jnp.concatenate(rows, axis=0)
    high = value.astype(BF16)
    rest = value - high.astype(F32)
    middle = rest.astype(BF16)
    low = (rest - middle.astype(F32)).astype(BF16)
    spread = jnp.dot(
        jnp.concatenate([high, middle, low], axis=0), place[...],
        preferred_element_type=F32,
    )
    count = 2 * SPAN * CELLS
    spread = spread[0:count] + spread[count:2 * count] + spread[2 * count:3 * count]
    spread = spread.reshape(2 * SPAN, CELLS, width)
    s_row = lax.broadcasted_iota(jnp.int32, spread.shape, 1)
    s_col = lax.broadcasted_iota(jnp.int32, spread.shape, 2)
    result = jnp.sum(jnp.where(lax.rem(s_col, CELLS) == s_row, spread, 0.0), axis=1)
    out_ref[0] = result[0:SPAN]
    out_ref[1] = result[SPAN:2 * SPAN]


def local(slc_stack, band_taps, pair_flags):
    n = lax.axis_size("date")
    rows, span = slc_stack.shape[2:]
    steps = span // LANES // SUB
    slabs = n // SPAN
    assert rows == SUB and rows // ML_AZ == SPAN and span == LANES * LANES
    assert n % (LANES // SUB) == 0 and steps == LANES // SUB
    workers = 1
    while 2 * workers <= min(steps, slabs // 2):
        workers *= 2
    tiles = SLOT * (steps + 3)

    vmem = pl.BlockSpec(memory_space=pltpu.VMEM)
    small = lambda *lead: pltpu.VMEM((*lead, CELLS, LANES), F32)
    sem = lambda *lead: pltpu.SemaphoreType.DMA(lead)
    both = pl.pallas_call(
        functools.partial(kernel, n, steps),
        out_shape=jax.ShapeDtypeStruct((2, rows // ML_AZ, span // ML_RG), F32),
        in_specs=[pl.BlockSpec(memory_space=pl.ANY)] * 3,
        out_specs=vmem,
        scratch_shapes=[
            pltpu.VMEM((2, rows, span), BF16),
            pltpu.VMEM((1, SPAN), jnp.int32),
            pltpu.VMEM((2, 2, TAPS), BF16),
            pltpu.VMEM((8, LANES), F32),
            pltpu.VMEM((2 * SUB * SUB, LANES), F32),
            pltpu.VMEM((SPAN, tiles, SUB, 2 * LANES), BF16),
            pltpu.VMEM((WIN, tiles, SUB, 2 * LANES), BF16),
            pltpu.VMEM((4 * LANES, 4 * LANES), BF16),
            pltpu.VMEM((steps, SPAN, ML_AZ, SUB, 4 * LANES), F32),
            pltpu.VMEM((SPAN, ML_AZ, SUB, 4 * LANES), F32),
            pltpu.VMEM((steps, SLOTS * SUB, 2 * LANES), BF16),
            pltpu.VMEM((steps, CELLS, SLOTS * SUB), F32),
            small(steps, 2 * HALVES),
            small(slabs, steps // workers, 2 * HALVES),
            small(n),
            small(workers * SPAN),
            pltpu.VMEM((LANES, span // ML_RG), BF16),
            sem(3), sem(5), sem(3, steps + 2), pltpu.SemaphoreType.REGULAR((2,)),
        ],
        compiler_params=pltpu.CompilerParams(
            collective_id=0, has_side_effects=True, vmem_limit_bytes=60 * 1024 * 1024
        ),
    )(slc_stack, pair_flags, band_taps)
    return both[0:1], both[1:2]


def solution(mesh):
    in_specs = (P("date", None, "group", None), P(), P("date", None))
    out_specs = (P("date", "group", None), P("date", "group", None))
    return jax.shard_map(local, mesh=mesh, in_specs=in_specs, out_specs=out_specs, check_vma=False)
```

```python
import functools

import jax
import jax.numpy as jnp
from jax import lax
from jax.experimental import pallas as pl
from jax.experimental.pallas import tpu as pltpu
from jax.sharding import PartitionSpec as P

TAPS = 32
ML_AZ = 4
ML_RG = 16
SPAN = 4
RADIUS = 8
ITERS = 4

LANES = 128
CELLS = LANES // ML_RG
SUB = 16
SIDE = SPAN // 2
WIN = SPAN + 2 * SIDE
SLOT = ML_AZ + 2
REACH = TAPS // 2
LAG = 3

eps_power = 1e-06
floor_weight = 0.1
ridge_weight = 0.05
split_coef = 2.0

F32 = jnp.float32
BF16 = jnp.bfloat16

OWN = tuple(range(SIDE, SIDE + SPAN))
FAR = tuple(range(SIDE)) + tuple(range(SIDE + SPAN, WIN))


def first_date(k):
    return 0 if k == SPAN else 1


PAIRS = [(first_date(k) + g, k) for k in range(1, SPAN + 1) for g in range(SPAN)]
OWN_PAIRS = [(w, k) for w, k in PAIRS if w in OWN and w + k in OWN]
FAR_PAIRS = [p for p in PAIRS if p not in OWN_PAIRS]


HALVES = 2
GROUP = SPAN * SPAN // HALVES


def pair_slot(imag, band, w, k):
    return ((2 * band + imag) * HALVES + (k - 1) // HALVES) * GROUP + (k - 1) % HALVES * SPAN + w - first_date(k)


def power_slot(band, w):
    return 4 * HALVES * GROUP + band * WIN + w


SLOTS = power_slot(1, WIN - 1) + 1


def kernel(
    n, steps,
    slc_hbm, flags_hbm, taps_hbm, out_ref,
    slc, flags_in, taps_in, taps_ref, turn, data, recv, mat, bands_own, bands_far, both, red, quant,
    msg, got, pack, back, place,
    in_sem, send_sem, recv_sem, wave_sem,
):
    me = lax.axis_index("date")
    q = lax.rem(me, SPAN)
    z = me // SPAN
    slabs = n // SPAN
    has_left = z > 0
    has_right = z < slabs - 1
    mesh_id = pl.DeviceIdType.MESH

    slc_load = pltpu.make_async_copy(slc_hbm.at[0], slc, in_sem.at[0])
    slc_load.start()
    flags_load = pltpu.make_async_copy(flags_hbm, flags_in, in_sem.at[1])
    flags_load.start()
    taps_load = pltpu.make_async_copy(taps_hbm, taps_in, in_sem.at[2])
    taps_load.start()
    barrier = pltpu.get_barrier_semaphore()

    for hop in range(1, SPAN):
        pl.semaphore_signal(
            barrier, inc=1, device_id={"date": z * SPAN + lax.rem(q + hop, SPAN)}, device_id_type=mesh_id
        )

    @pl.when(has_left)
    def _():
        pl.semaphore_signal(barrier, inc=1, device_id={"date": me - SPAN}, device_id_type=mesh_id)

    @pl.when(has_right)
    def _():
        pl.semaphore_signal(barrier, inc=1, device_id={"date": me + SPAN}, device_id_type=mesh_id)

    flags_load.wait()
    tile_row = lax.broadcasted_iota(jnp.int32, (SUB, 2 * LANES), 0)
    own_flags = flags_in[...].astype(F32)
    flag_tile = jnp.zeros((SUB, 2 * LANES), F32)
    for k in range(SPAN):
        flag_tile = jnp.where(tile_row == k, jnp.broadcast_to(own_flags[0:1, k:k + 1], flag_tile.shape), flag_tile)
    flag_tile = flag_tile.astype(BF16)
    for s in range(SPAN):
        data[s, SLOT + ML_AZ] = flag_tile
    taps_load.wait()
    taps_ref[...] = jnp.zeros_like(taps_ref)
    for band in range(2):
        taps_ref[2 * band:2 * band + 2, 0:TAPS] = taps_in[band].astype(F32)

    k_id = lax.broadcasted_iota(jnp.int32, (LANES, LANES), 0)
    j_id = lax.broadcasted_iota(jnp.int32, (LANES, LANES), 1)
    reach = k_id - j_id + TAPS // 2
    circ = []
    for m in range(4):
        base = jnp.broadcast_to(taps_ref[m:m + 1, :], (LANES, LANES))
        circ.append(pltpu.roll(base, LANES - TAPS // 2, 1, stride=1, stride_axis=0).T)
    for edge in range(2):
        inside = (reach >= 0) & (reach < LANES)
        keep = inside if edge == 0 else jnp.logical_not(inside)
        row = edge * 2 * LANES
        for band in range(2):
            re_part = jnp.where(keep, circ[2 * band], 0.0).astype(BF16)
            im_value = jnp.where(keep, circ[2 * band + 1], 0.0)
            im_part = im_value.astype(BF16)
            im_minus = (-im_value).astype(BF16)
            col = band * 2 * LANES
            mat[row:row + 128, col:col + 128] = re_part
            mat[row:row + 128, col + 128:col + 256] = im_part
            mat[row + 128:row + 256, col:col + 128] = im_minus
            mat[row + 128:row + 256, col + 128:col + 256] = re_part

    slc_load.wait()

    def regroup(j, carry):
        for part in range(2):
            for i in range(SUB):
                at = pl.multiple_of((steps * i + j) * LANES, LANES)
                value = slc[part, :, pl.ds(at, LANES)].astype(F32)
                turn[(part * SUB + i) * SUB:(part * SUB + i + 1) * SUB, :] = value
        for part in range(2):
            for s in range(SPAN):
                for r in range(ML_AZ):
                    row = part * SUB * SUB + ML_AZ * s + r
                    value = turn[pl.ds(row, SUB, stride=SUB), :].astype(BF16)
                    data[s, SLOT * (j + 1) + r, :, part * LANES:part * LANES + LANES] = value
        return carry

    tap_lane = lax.broadcasted_iota(jnp.int32, (SUB, LANES), 1)


    def edge_at(r, part):
        return r // 2, (r % 2 * 2 + part) * 2 * REACH

    def send_edges():
        for s in range(SPAN):
            packed = [None, None]
            for r in range(ML_AZ):
                for part in range(2):
                    value = data[s, SLOT * steps + r, :, part * LANES:part * LANES + LANES].astype(F32)
                    tile, at = edge_at(r, part)
                    head = pltpu.roll(value, at, 1) if at else value
                    tail = pltpu.roll(value, (at + 2 * REACH) % LANES, 1)
                    both_ends = jnp.where(tap_lane < at + REACH, head, tail)
                    old = packed[tile]
                    packed[tile] = both_ends if old is None else jnp.where(tap_lane >= at, both_ends, old)
            data[s, SLOT + ML_AZ + 1] = jnp.concatenate(packed, axis=1).astype(BF16)

    regroup(steps - 1, 0)
    send_edges()
    regroup(0, 0)
    regroup(1, 0)

    def chunk(ref, j, first):
        return ref.at[pl.ds(SLOT * (j + 1), SLOT if first else ML_AZ)]

    def slab_copy(target, j, first):
        return pltpu.make_async_remote_copy(
            src_ref=chunk(data.at[target], j, first), dst_ref=chunk(recv.at[q + SIDE], j, first),
            send_sem=send_sem.at[0], recv_sem=recv_sem.at[1, j],
            device_id={"date": z * SPAN + target}, device_id_type=mesh_id,
        )

    def own_copy(j, first):
        return pltpu.make_async_copy(
            chunk(data.at[q], j, first), chunk(recv.at[q + SIDE], j, first), recv_sem.at[1, j]
        )

    def side_copy(w, j, first):
        go_left = w < SPAN
        to, device = (w + SPAN, me - SPAN) if go_left else (w - SPAN, me + SPAN)
        return pltpu.make_async_remote_copy(
            src_ref=chunk(recv.at[w], j, first), dst_ref=chunk(recv.at[to], j, first),
            send_sem=send_sem.at[1 if go_left else 2], recv_sem=recv_sem.at[2 if go_left else 0, j],
            device_id={"date": device}, device_id_type=mesh_id,
        )

    def arrived(dates, side, j, first):
        ref = recv.at[pl.ds(dates[0], len(dates)), pl.ds(SLOT * (j + 1), SLOT if first else ML_AZ)]
        pltpu.make_async_copy(ref, ref, recv_sem.at[side, j]).wait()

    near = SPAN - 1 + has_left.astype(jnp.int32) + has_right.astype(jnp.int32)
    pl.semaphore_wait(barrier, near)

    def send_chunk(j, first):
        own_copy(j, first).start()
        for hop in (2, 3, 1):
            slab_copy(lax.rem(q + hop, SPAN), j, first).start()

    send_chunk(0, True)

    def send_more(j, carry):
        regroup(j + 1, 0)
        send_chunk(j, False)
        return carry

    lax.fori_loop(1, steps - 2, send_more, 0)
    for j in range(steps - 2, steps):
        send_chunk(j, False)

    @pl.when(jnp.logical_not(has_left))
    def _():
        for w in range(SIDE):
            recv[w] = jnp.zeros(recv.shape[1:], BF16)

    @pl.when(jnp.logical_not(has_right))
    def _():
        for w in range(SIDE + SPAN, WIN):
            recv[w] = jnp.zeros(recv.shape[1:], BF16)

    width = out_ref.shape[2]
    place_row = lax.broadcasted_iota(jnp.int32, (LANES, width), 0)
    place_block = lax.broadcasted_iota(jnp.int32, (LANES, width), 1) // CELLS
    on_place = place_row == lax.rem(place_block, steps) * SUB + place_block // steps
    place[...] = jnp.where(on_place, 1.0, 0.0).astype(BF16)

    sel_row = lax.broadcasted_iota(jnp.int32, (CELLS, 2 * LANES), 0)
    sel_lane = lax.broadcasted_iota(jnp.int32, (CELLS, 2 * LANES), 1)
    selector = jnp.where(lax.rem(sel_lane, LANES) // ML_RG == sel_row, 1.0, 0.0).astype(BF16)
    contract = (((1,), (1,)), ((), ()))
    edge_lane = lax.rem(lax.broadcasted_iota(jnp.int32, (ML_AZ, SUB, 2 * LANES), 2), LANES)
    from_before = edge_lane >= LANES - TAPS // 2
    sub_row = lax.broadcasted_iota(jnp.int32, (ML_AZ, SUB, 2 * LANES), 1)

    def own_arrive(j, first):
        arrived(OWN, 1, j, first)

        @pl.when(has_left)
        def _():
            for w in OWN[:SIDE]:
                side_copy(w, j, first).start()

        @pl.when(has_right)
        def _():
            for w in OWN[SIDE:]:
                side_copy(w, j, first).start()

    def far_arrive(j, first):
        @pl.when(has_left)
        def _():
            arrived(FAR[:SIDE], 0, j, first)

        @pl.when(has_right)
        def _():
            arrived(FAR[SIDE:], 2, j, first)

    def make_after(dates):
        for w in dates:
            value = recv[w, SLOT:SLOT + ML_AZ].astype(F32)
            value = jnp.where(sub_row < SUB - 1, pltpu.roll(value, SUB - 1, 1), 0.0)
            recv[w, SLOT * (steps + 1):SLOT * (steps + 1) + ML_AZ] = value.astype(BF16)

    def make_edges(dates):
        for w in dates:
            tiles = recv[w, SLOT + ML_AZ + 1].astype(F32)
            for r in range(ML_AZ):
                before, after = [], []
                for part in range(2):
                    tile, at = edge_at(r, part)
                    value = tiles[:, tile * LANES:tile * LANES + LANES]
                    after.append(pltpu.roll(value, LANES - at, 1) if at else value)
                    value = pltpu.roll(value, (LANES - 2 * REACH - at) % LANES, 1)
                    before.append(jnp.where(tile_row[:, 0:LANES] > 0, pltpu.roll(value, 1, 0), 0.0))
                recv[w, r] = jnp.concatenate(before, axis=1).astype(BF16)
                recv[w, SLOT * (steps + 2) + r] = jnp.concatenate(after, axis=1).astype(BF16)

    def band_split(dates, j):
        rows = []
        behind = SLOT * jnp.where(j == steps - 2, steps + 2, j + 2)
        for w in dates:
            here = recv[w, pl.ds(SLOT * (j + 1), ML_AZ)]
            before = recv[w, pl.ds(SLOT * j, ML_AZ)]
            after = recv[w, pl.ds(behind, ML_AZ)]
            edge = jnp.where(from_before, before, after)
            rows.append(jnp.concatenate([here, edge], axis=2).reshape(ML_AZ * SUB, 4 * LANES))
        made = jnp.dot(jnp.concatenate(rows, axis=0), mat[...], preferred_element_type=F32)
        return made.astype(BF16).astype(F32).reshape(len(dates), ML_AZ, SUB, 4 * LANES)

    def read(w, j, band, part):
        cols = slice((2 * band + part) * LANES, (2 * band + part + 1) * LANES)
        if w in OWN:
            return [bands_own[j, OWN.index(w), r, :, cols] for r in range(ML_AZ)]
        return [bands_far[FAR.index(w), r, :, cols] for r in range(ML_AZ)]

    def total(terms):
        terms = list(terms)
        while len(terms) > 1:
            terms = [a + b for a, b in zip(terms[::2], terms[1::2])]
        return terms[0]

    def keep_sum(j, at, value):
        high = value.astype(BF16)
        low = (value - high.astype(F32)).astype(BF16)
        both[j, at * SUB:at * SUB + SUB, 0:LANES] = high
        both[j, at * SUB:at * SUB + SUB, LANES:2 * LANES] = low

    def products(dates, pairs, j):
        for band in range(2):
            for w in dates:
                re, im = (read(w, j, band, part) for part in range(2))
                keep_sum(j, power_slot(band, w), total([a * a for a in re]) + total([a * a for a in im]))
            for w, k in pairs:
                a_re, a_im = (read(w, j, band, part) for part in range(2))
                b_re, b_im = (read(w + k, j, band, part) for part in range(2))
                re = total([a * b for a, b in zip(a_re, b_re)]) + total([a * b for a, b in zip(a_im, b_im)])
                im = total([a * b for a, b in zip(a_im, b_re)]) - total([a * b for a, b in zip(a_re, b_im)])
                keep_sum(j, pair_slot(0, band, w, k), re)
                keep_sum(j, pair_slot(1, band, w, k), im)

    def own_step(j):
        bands_own[j] = band_split(OWN, j)
        products(OWN, OWN_PAIRS, j)

    def far_step(j):
        bands_far[...] = band_split(FAR, j)
        products(FAR, FAR_PAIRS, j)
        red[j] = lax.dot_general(selector, both[j], contract, preferred_element_type=F32)

    def wave_signal():
        @pl.when(has_left)
        def _():
            pl.semaphore_signal(wave_sem.at[1], inc=1, device_id={"date": me - SPAN}, device_id_type=mesh_id)

        @pl.when(has_right)
        def _():
            pl.semaphore_signal(wave_sem.at[0], inc=1, device_id={"date": me + SPAN}, device_id_type=mesh_id)

    def wave(t, carry):
        @pl.when(has_left)
        def _():
            pl.semaphore_wait(wave_sem.at[0], 1)

        @pl.when(has_right)
        def _():
            pl.semaphore_wait(wave_sem.at[1], 1)

        @pl.when(t < slabs - 1)
        def _():
            wave_signal()

        return carry

    own_arrive(0, True)
    make_after(OWN)
    make_edges(OWN)

    wave_signal()

    def stream(t, carry):
        u = t - LAG

        @pl.when(t < steps)
        def _():
            own_arrive(t, False)

        @pl.when(t < slabs)
        def _():
            wave(t, 0)

        @pl.when(t <= steps)
        def _():
            own_step(t - 1)

        @pl.when(u == 0)
        def _():
            far_arrive(0, True)
            make_after(FAR)
            make_edges(FAR)

        @pl.when((u > 0) & (u < steps - 1))
        def _():
            far_arrive(u, False)

        @pl.when(u > 0)
        def _():
            far_step(u - 1)

        @pl.when(u == steps - 1)
        def _():
            far_arrive(u, False)

        return carry

    lax.fori_loop(1, steps + LAG + 1, stream, 0)
    lax.fori_loop(steps + LAG + 1, slabs, wave, 0)

    shape = (steps, CELLS, LANES)
    c_id = lax.broadcasted_iota(jnp.int32, shape, 1)
    l_id = lax.broadcasted_iota(jnp.int32, shape, 2)
    i_id = lax.rem(l_id, SUB)

    def box(value):
        prefix = value
        for hop in (1, 2, 4):
            prefix = prefix + jnp.where(c_id >= hop, pltpu.roll(prefix, hop, 1), 0.0)
        whole = jnp.sum(value, axis=1, keepdims=True)
        suffix = whole - prefix + value
        first = jnp.where(i_id[0:1] > 0, pltpu.roll(suffix[steps - 1:steps], 1, 2), 0.0)
        last = jnp.where(i_id[0:1] < SUB - 1, pltpu.roll(prefix[0:1], LANES - 1, 2), 0.0)
        before = jnp.concatenate([first, suffix[0:steps - 1]], axis=0)
        after = jnp.concatenate([prefix[1:steps], last], axis=0)
        return before + whole + after

    def register(at):
        return red[:, :, at * LANES:at * LANES + LANES]

    lane = lax.broadcasted_iota(jnp.int32, (CELLS, LANES), 1)
    span_lanes = SPAN * SUB

    def aligned(value, ks, partner):
        parts = []
        for at, k in enumerate(ks):
            w = first_date(k) + (k if partner else 0)
            move = (at * SPAN - w) * SUB % LANES
            parts.append(pltpu.roll(value, move, 2) if move else value)
        return jnp.where(l_id < span_lanes, parts[0], parts[1])

    for h in range(HALVES):
        ks = (HALVES * h + 1, HALVES * h + 2)
        cr0, ci0, cr1, ci1 = (register(m * HALVES + h) for m in range(4))
        ab0, ab1 = (
            aligned(power, ks, False) * aligned(power, ks, True) + eps_power
            for power in (register(4 * HALVES), register(4 * HALVES + 1))
        )
        flag = jnp.zeros((CELLS, LANES), F32)
        for at, k in enumerate(ks):
            for g in range(SPAN):
                one = recv[first_date(k) + g, SLOT + ML_AZ].astype(F32)[k - 1:k, 0:LANES]
                flag = jnp.where(lane >= (at * SPAN + g) * SUB, jnp.broadcast_to(one, flag.shape), flag)
        weight = flag[None] * 0.5 * ((cr0 * cr0 + ci0 * ci0) / ab0 + (cr1 * cr1 + ci1 * ci1) / ab1)
        phase = split_coef * (ci0 * cr1 - cr0 * ci1) / jnp.sqrt(ab0 * ab1)
        den = box(weight)
        num = box(weight * phase)
        quant[:, h] = den / (2 * RADIUS + 1)
        quant[:, HALVES + h] = num / (den + floor_weight)

    workers = msg.shape[0]
    share = steps // workers
    base = (slabs - workers) // 2
    is_worker = (z >= base) & (z < base + workers)
    half = LANES // 2
    ranks = LANES // SUB
    zero = jnp.zeros((CELLS, LANES), F32)

    def turned(rows):
        rows = list(rows)
        bit = 1
        while bit < len(rows):
            upper = lax.rem(lane // (SUB * bit), 2) == 1
            for a in range(len(rows)):
                if a & bit == 0:
                    low, high = rows[a], rows[a | bit]
                    rows[a] = jnp.where(upper, pltpu.roll(high, SUB * bit, 1), low)
                    rows[a | bit] = jnp.where(upper, high, pltpu.roll(low, LANES - SUB * bit, 1))
            bit *= 2
        return rows

    def line_copy(u):
        return pltpu.make_async_remote_copy(
            src_ref=msg.at[u], dst_ref=got.at[z],
            send_sem=send_sem.at[3], recv_sem=recv_sem.at[0, steps],
            device_id={"date": (base + u) * SPAN + q}, device_id_type=mesh_id,
        )

    for u in range(workers):
        for kind in range(2):
            rows = [zero] * ranks
            for h in range(HALVES):
                for jj in range(share):
                    rows[h * ranks // 2 + jj] = quant[u * share + jj, kind * HALVES + h]
            for slot, value in enumerate(turned(rows)):
                msg[u, kind, slot] = value

        @pl.when(z != base + u)
        def _():
            line_copy(u).start()

        @pl.when(z == base + u)
        def _():
            pltpu.make_async_copy(msg.at[u], got.at[z], recv_sem.at[0, steps]).start()

    def out_copy(target):
        return pltpu.make_async_remote_copy(
            src_ref=pack.at[target], dst_ref=back.at[(z - base) * SPAN + q],
            send_sem=send_sem.at[4], recv_sem=recv_sem.at[0, steps + 1],
            device_id={"date": target}, device_id_type=mesh_id,
        )

    in_lower = lane < half

    def split(low, high):
        return jnp.where(in_lower, low, high)

    def fold(value):
        return value + pltpu.roll(value, half, 1)

    def at(values, d):
        return values[d] if 0 <= d < n else zero

    def held(kind, position, d):
        return got[d // SPAN, kind, position * SPAN + d % SPAN] if d < n else zero

    def relax():
        near, wide = [], []
        for kind in range(2):
            near.append([held(kind, 0, d + 1) for d in range(n)])
            wide.append([split(held(kind, 1, d + 1), held(kind, 1, d + 2)) for d in range(n)])
        near_back = [split(at(near[0], d - 1), at(near[0], d - 3)) for d in range(n)]
        wide_back = [split(at(wide[0], d - 2), at(wide[0], d - 4)) for d in range(n)]
        wsum = [fold((a + b) + (c + e)) for a, b, c, e in zip(near[0], wide[0], near_back, wide_back)]
        near_flow = [a * b for a, b in zip(*near)]
        wide_flow = [a * b for a, b in zip(*wide)]
        flow = [
            (split(at(near_flow, d - 1), at(near_flow, d - 3)) + split(at(wide_flow, d - 2), at(wide_flow, d - 4)))
            - (near_flow[d] + wide_flow[d]) for d in range(n)
        ]
        phi = [zero]
        for d in range(n - 1):
            first = near[1][d]
            phi.append(phi[-1] + split(first, pltpu.roll(first, half, 1)))
        pull = [ridge_weight * p for p in phi]
        inv = [1.0 / (t + ridge_weight) for t in wsum]
        for sweep in range(ITERS):
            up = [split(at(phi, d), at(phi, d + 2)) for d in range(n + 2)]
            down = [split(at(phi, d - 2), at(phi, d - 4)) for d in range(n + 2)]
            phi = [
                (
                    fold(
                        flow[d] + (near[0][d] * up[d + 1] + wide[0][d] * at(up[:n], d + 2))
                        + (near_back[d] * down[d + 1] + wide_back[d] * down[d])
                    ) + pull[d]
                ) * inv[d] for d in range(n)
            ]
        return phi, wsum

    @pl.when(is_worker)
    def _():
        pltpu.make_async_copy(got, got, recv_sem.at[0, steps]).wait()
        phi, wsum = relax()
        for d in range(n):
            pack[d] = split(phi[d], wsum[d])

        def send_back(i, carry):
            for g in range(SPAN):
                target = SPAN * jnp.where(z < slabs // 2, slabs - 1 - i, i) + g

                @pl.when(target != me)
                def _():
                    out_copy(target).start()
            return carry

        lax.fori_loop(0, slabs, send_back, 0)
        pltpu.make_async_copy(
            pack.at[me], back.at[(z - base) * SPAN + q], recv_sem.at[0, steps + 1]
        ).start()

    def drain(ref, sem):
        pltpu.make_async_copy(ref, ref, sem).wait()

    tiles = SLOT + ML_AZ * (steps - 1)
    drain(data.at[pl.ds(0, SPAN - 1), pl.ds(0, tiles)], send_sem.at[0])

    @pl.when(has_left)
    def _():
        drain(data.at[pl.ds(0, SIDE), pl.ds(0, tiles)], send_sem.at[1])

    @pl.when(has_right)
    def _():
        drain(data.at[pl.ds(0, SIDE), pl.ds(0, tiles)], send_sem.at[2])

    drain(msg.at[pl.ds(0, workers - 1)], send_sem.at[3])

    @pl.when(jnp.logical_not(is_worker))
    def _():
        drain(msg.at[0], send_sem.at[3])

    drain(back, recv_sem.at[0, steps + 1])

    @pl.when(is_worker)
    def _():
        drain(pack.at[pl.ds(0, n - 1)], send_sem.at[4])

    rows = []
    for kind in range(2):
        for s in range(SPAN):
            value = None
            for u in range(workers):
                move = (u * share * SUB - kind * half) % LANES
                piece = back[u * SPAN + s]
                piece = pltpu.roll(piece, move, 1) if move else piece
                value = piece if value is None else jnp.where(lane >= u * share * SUB, piece, value)
            rows.append(value)
    value = jnp.concatenate(rows, axis=0)
    high = value.astype(BF16)
    rest = value - high.astype(F32)
    middle = rest.astype(BF16)
    low = (rest - middle.astype(F32)).astype(BF16)
    spread = jnp.dot(
        jnp.concatenate([high, middle, low], axis=0), place[...],
        preferred_element_type=F32,
    )
    count = 2 * SPAN * CELLS
    spread = spread[0:count] + spread[count:2 * count] + spread[2 * count:3 * count]
    spread = spread.reshape(2 * SPAN, CELLS, width)
    s_row = lax.broadcasted_iota(jnp.int32, spread.shape, 1)
    s_col = lax.broadcasted_iota(jnp.int32, spread.shape, 2)
    result = jnp.sum(jnp.where(lax.rem(s_col, CELLS) == s_row, spread, 0.0), axis=1)
    out_ref[0] = result[0:SPAN]
    out_ref[1] = result[SPAN:2 * SPAN]


def local(slc_stack, band_taps, pair_flags):
    n = lax.axis_size("date")
    rows, span = slc_stack.shape[2:]
    steps = span // LANES // SUB
    slabs = n // SPAN
    assert rows == SUB and rows // ML_AZ == SPAN and span == LANES * LANES
    assert n % (LANES // SUB) == 0 and steps == LANES // SUB
    workers = 1
    while 2 * workers <= min(steps, slabs // 2):
        workers *= 2
    tiles = SLOT * (steps + 3)

    vmem = pl.BlockSpec(memory_space=pltpu.VMEM)
    small = lambda *lead: pltpu.VMEM((*lead, CELLS, LANES), F32)
    sem = lambda *lead: pltpu.SemaphoreType.DMA(lead)
    both = pl.pallas_call(
        functools.partial(kernel, n, steps),
        out_shape=jax.ShapeDtypeStruct((2, rows // ML_AZ, span // ML_RG), F32),
        in_specs=[pl.BlockSpec(memory_space=pl.ANY)] * 3,
        out_specs=vmem,
        scratch_shapes=[
            pltpu.VMEM((2, rows, span), BF16),
            pltpu.VMEM((1, SPAN), jnp.int32),
            pltpu.VMEM((2, 2, TAPS), BF16),
            pltpu.VMEM((8, LANES), F32),
            pltpu.VMEM((2 * SUB * SUB, LANES), F32),
            pltpu.VMEM((SPAN, tiles, SUB, 2 * LANES), BF16),
            pltpu.VMEM((WIN, tiles, SUB, 2 * LANES), BF16),
            pltpu.VMEM((4 * LANES, 4 * LANES), BF16),
            pltpu.VMEM((steps, SPAN, ML_AZ, SUB, 4 * LANES), F32),
            pltpu.VMEM((SPAN, ML_AZ, SUB, 4 * LANES), F32),
            pltpu.VMEM((steps, SLOTS * SUB, 2 * LANES), BF16),
            pltpu.VMEM((steps, CELLS, SLOTS * SUB), F32),
            small(steps, 2 * HALVES),
            small(workers, 2, GROUP),
            small(slabs, 2, GROUP),
            small(n),
            small(workers * SPAN),
            pltpu.VMEM((LANES, span // ML_RG), BF16),
            sem(3), sem(5), sem(3, steps + 2), pltpu.SemaphoreType.REGULAR((2,)),
        ],
        compiler_params=pltpu.CompilerParams(
            collective_id=0, has_side_effects=True, vmem_limit_bytes=60 * 1024 * 1024
        ),
    )(slc_stack, pair_flags, band_taps)
    return both[0:1], both[1:2]


def solution(mesh):
    in_specs = (P("date", None, "group", None), P(), P("date", None))
    out_specs = (P("date", "group", None), P("date", "group", None))
    return jax.shard_map(local, mesh=mesh, in_specs=in_specs, out_specs=out_specs, check_vma=False)
```

```python
import functools

import jax
import jax.numpy as jnp
from jax import lax
from jax.experimental import pallas as pl
from jax.experimental.pallas import tpu as pltpu
from jax.sharding import PartitionSpec as P

TAPS = 32
ML_AZ = 4
ML_RG = 16
SPAN = 4
RADIUS = 8
ITERS = 4

LANES = 128
CELLS = LANES // ML_RG
SUB = 16
SIDE = SPAN // 2
WIN = SPAN + 2 * SIDE
SLOT = ML_AZ + 1
REACH = TAPS // 2
LAG = 3

eps_power = 1e-06
floor_weight = 0.1
ridge_weight = 0.05
split_coef = 2.0

F32 = jnp.float32
BF16 = jnp.bfloat16

OWN = tuple(range(SIDE, SIDE + SPAN))
FAR = tuple(range(SIDE)) + tuple(range(SIDE + SPAN, WIN))


def first_date(k):
    return 0 if k == SPAN else 1


PAIRS = [(first_date(k) + g, k) for k in range(1, SPAN + 1) for g in range(SPAN)]
OWN_PAIRS = [(w, k) for w, k in PAIRS if w in OWN and w + k in OWN]
FAR_PAIRS = [p for p in PAIRS if p not in OWN_PAIRS]


HALVES = 2
GROUP = SPAN * SPAN // HALVES


def pair_slot(imag, band, w, k):
    return ((2 * band + imag) * HALVES + (k - 1) // HALVES) * GROUP + (k - 1) % HALVES * SPAN + w - first_date(k)


def power_slot(band, w):
    return 4 * HALVES * GROUP + band * WIN + w


SLOTS = power_slot(1, WIN - 1) + 1


def kernel(
    n, steps,
    slc_hbm, flags_hbm, taps_hbm, out_ref,
    slc, flags_in, taps_in, taps_ref, turn, data, recv, mat, bands_own, bands_far, both, red, quant,
    msg, got, pack, back, place, flag_of,
    in_sem, send_sem, recv_sem, wave_sem,
):
    me = lax.axis_index("date")
    q = lax.rem(me, SPAN)
    z = me // SPAN
    slabs = n // SPAN
    has_left = z > 0
    has_right = z < slabs - 1
    mesh_id = pl.DeviceIdType.MESH

    slc_load = pltpu.make_async_copy(slc_hbm.at[0], slc, in_sem.at[0])
    slc_load.start()
    flags_load = pltpu.make_async_copy(flags_hbm, flags_in, in_sem.at[1])
    flags_load.start()
    taps_load = pltpu.make_async_copy(taps_hbm, taps_in, in_sem.at[2])
    taps_load.start()
    barrier = pltpu.get_barrier_semaphore()

    for hop in range(1, SPAN):
        pl.semaphore_signal(
            barrier, inc=1, device_id={"date": z * SPAN + lax.rem(q + hop, SPAN)}, device_id_type=mesh_id
        )

    @pl.when(has_left)
    def _():
        pl.semaphore_signal(barrier, inc=1, device_id={"date": me - SPAN}, device_id_type=mesh_id)

    @pl.when(has_right)
    def _():
        pl.semaphore_signal(barrier, inc=1, device_id={"date": me + SPAN}, device_id_type=mesh_id)

    flags_load.wait()
    tile_row = lax.broadcasted_iota(jnp.int32, (SUB, 2 * LANES), 0)
    own_flags = flags_in[...].astype(F32)
    taps_load.wait()
    taps_ref[...] = jnp.zeros_like(taps_ref)
    for band in range(2):
        taps_ref[2 * band:2 * band + 2, 0:TAPS] = taps_in[band].astype(F32)

    k_id = lax.broadcasted_iota(jnp.int32, (LANES, LANES), 0)
    j_id = lax.broadcasted_iota(jnp.int32, (LANES, LANES), 1)
    reach = k_id - j_id + TAPS // 2
    circ = []
    for m in range(4):
        base = jnp.broadcast_to(taps_ref[m:m + 1, :], (LANES, LANES))
        circ.append(pltpu.roll(base, LANES - TAPS // 2, 1, stride=1, stride_axis=0).T)
    for edge in range(2):
        inside = (reach >= 0) & (reach < LANES)
        keep = inside if edge == 0 else jnp.logical_not(inside)
        row = edge * 2 * LANES
        for band in range(2):
            re_part = jnp.where(keep, circ[2 * band], 0.0).astype(BF16)
            im_value = jnp.where(keep, circ[2 * band + 1], 0.0)
            im_part = im_value.astype(BF16)
            im_minus = (-im_value).astype(BF16)
            col = band * 2 * LANES
            mat[row:row + 128, col:col + 128] = re_part
            mat[row:row + 128, col + 128:col + 256] = im_part
            mat[row + 128:row + 256, col:col + 128] = im_minus
            mat[row + 128:row + 256, col + 128:col + 256] = re_part

    slc_load.wait()

    def regroup(j, carry):
        for part in range(2):
            for i in range(SUB):
                at = pl.multiple_of((steps * i + j) * LANES, LANES)
                value = slc[part, :, pl.ds(at, LANES)].astype(F32)
                turn[(part * SUB + i) * SUB:(part * SUB + i + 1) * SUB, :] = value
        for part in range(2):
            for s in range(SPAN):
                for r in range(ML_AZ):
                    row = part * SUB * SUB + ML_AZ * s + r
                    value = turn[pl.ds(row, SUB, stride=SUB), :].astype(BF16)
                    data[s, SLOT * (j + 1) + r, :, part * LANES:part * LANES + LANES] = value
        return carry

    tap_lane = lax.broadcasted_iota(jnp.int32, (SUB, LANES), 1)


    def edge_at(r, part):
        return r // 2, (r % 2 * 2 + part) * 2 * REACH

    def send_edges():
        for s in range(SPAN):
            packed = [None, None]
            for r in range(ML_AZ):
                for part in range(2):
                    value = data[s, SLOT * steps + r, :, part * LANES:part * LANES + LANES].astype(F32)
                    tile, at = edge_at(r, part)
                    head = pltpu.roll(value, at, 1) if at else value
                    tail = pltpu.roll(value, (at + 2 * REACH) % LANES, 1)
                    both_ends = jnp.where(tap_lane < at + REACH, head, tail)
                    if part == 0:
                        flag = jnp.broadcast_to(own_flags[0:1, r:r + 1], both_ends.shape)
                        both_ends = jnp.where(tap_lane == at + REACH - 1, flag, both_ends)
                    old = packed[tile]
                    packed[tile] = both_ends if old is None else jnp.where(tap_lane >= at, both_ends, old)
            data[s, SLOT + ML_AZ] = jnp.concatenate(packed, axis=1).astype(BF16)

    regroup(steps - 1, 0)
    send_edges()
    regroup(0, 0)
    regroup(1, 0)

    def chunk(ref, j, first):
        return ref.at[pl.ds(SLOT * (j + 1), SLOT if first else ML_AZ)]

    def slab_copy(target, j, first):
        return pltpu.make_async_remote_copy(
            src_ref=chunk(data.at[target], j, first), dst_ref=chunk(recv.at[q + SIDE], j, first),
            send_sem=send_sem.at[0], recv_sem=recv_sem.at[1, j],
            device_id={"date": z * SPAN + target}, device_id_type=mesh_id,
        )

    def own_copy(j, first):
        return pltpu.make_async_copy(
            chunk(data.at[q], j, first), chunk(recv.at[q + SIDE], j, first), recv_sem.at[1, j]
        )

    def side_copy(w, j, first):
        go_left = w < SPAN
        to, device = (w + SPAN, me - SPAN) if go_left else (w - SPAN, me + SPAN)
        return pltpu.make_async_remote_copy(
            src_ref=chunk(recv.at[w], j, first), dst_ref=chunk(recv.at[to], j, first),
            send_sem=send_sem.at[1 if go_left else 2], recv_sem=recv_sem.at[2 if go_left else 0, j],
            device_id={"date": device}, device_id_type=mesh_id,
        )

    def arrived(dates, side, j, first):
        ref = recv.at[pl.ds(dates[0], len(dates)), pl.ds(SLOT * (j + 1), SLOT if first else ML_AZ)]
        pltpu.make_async_copy(ref, ref, recv_sem.at[side, j]).wait()

    near = SPAN - 1 + has_left.astype(jnp.int32) + has_right.astype(jnp.int32)
    pl.semaphore_wait(barrier, near)

    def send_chunk(j, first):
        own_copy(j, first).start()
        for hop in (2, 3, 1):
            slab_copy(lax.rem(q + hop, SPAN), j, first).start()

    send_chunk(0, True)

    def send_more(j, carry):
        regroup(j + 1, 0)
        send_chunk(j, False)
        return carry

    lax.fori_loop(1, steps - 2, send_more, 0)
    for j in range(steps - 2, steps):
        send_chunk(j, False)

    @pl.when(jnp.logical_not(has_left))
    def _():
        for w in range(SIDE):
            recv[w] = jnp.zeros(recv.shape[1:], BF16)

    @pl.when(jnp.logical_not(has_right))
    def _():
        for w in range(SIDE + SPAN, WIN):
            recv[w] = jnp.zeros(recv.shape[1:], BF16)

    width = out_ref.shape[2]
    place_row = lax.broadcasted_iota(jnp.int32, (LANES, width), 0)
    place_block = lax.broadcasted_iota(jnp.int32, (LANES, width), 1) // CELLS
    on_place = place_row == lax.rem(place_block, steps) * SUB + place_block // steps
    place[...] = jnp.where(on_place, 1.0, 0.0).astype(BF16)

    sel_row = lax.broadcasted_iota(jnp.int32, (CELLS, 2 * LANES), 0)
    sel_lane = lax.broadcasted_iota(jnp.int32, (CELLS, 2 * LANES), 1)
    selector = jnp.where(lax.rem(sel_lane, LANES) // ML_RG == sel_row, 1.0, 0.0).astype(BF16)
    contract = (((1,), (1,)), ((), ()))
    edge_lane = lax.rem(lax.broadcasted_iota(jnp.int32, (ML_AZ, SUB, 2 * LANES), 2), LANES)
    from_before = edge_lane >= LANES - TAPS // 2
    sub_row = lax.broadcasted_iota(jnp.int32, (ML_AZ, SUB, 2 * LANES), 1)

    def own_arrive(j, first):
        arrived(OWN, 1, j, first)

        @pl.when(has_left)
        def _():
            for w in OWN[:SIDE]:
                side_copy(w, j, first).start()

        @pl.when(has_right)
        def _():
            for w in OWN[SIDE:]:
                side_copy(w, j, first).start()

    def far_arrive(j, first):
        @pl.when(has_left)
        def _():
            arrived(FAR[:SIDE], 0, j, first)

        @pl.when(has_right)
        def _():
            arrived(FAR[SIDE:], 2, j, first)

    def make_after(dates):
        for w in dates:
            value = recv[w, SLOT:SLOT + ML_AZ].astype(F32)
            value = jnp.where(sub_row < SUB - 1, pltpu.roll(value, SUB - 1, 1), 0.0)
            recv[w, SLOT * (steps + 1):SLOT * (steps + 1) + ML_AZ] = value.astype(BF16)

    def make_edges(dates):
        for w in dates:
            tiles = recv[w, SLOT + ML_AZ].astype(F32)
            for r in range(ML_AZ):
                before, after = [], []
                for part in range(2):
                    tile, at = edge_at(r, part)
                    value = tiles[:, tile * LANES:tile * LANES + LANES]
                    after.append(pltpu.roll(value, LANES - at, 1) if at else value)
                    value = pltpu.roll(value, (LANES - 2 * REACH - at) % LANES, 1)
                    before.append(jnp.where(tile_row[:, 0:LANES] > 0, pltpu.roll(value, 1, 0), 0.0))
                recv[w, r] = jnp.concatenate(before, axis=1).astype(BF16)
                recv[w, SLOT * (steps + 2) + r] = jnp.concatenate(after, axis=1).astype(BF16)

    def make_flags():
        flag_lane = lax.broadcasted_iota(jnp.int32, (CELLS, LANES), 1)
        for h in range(HALVES):
            flags = None
            for slot in range(GROUP):
                k, g = HALVES * h + slot // SPAN + 1, slot % SPAN
                tile, at = edge_at(k - 1, 0)
                at += tile * LANES + REACH - 1
                tiles = recv[first_date(k) + g, SLOT + ML_AZ].astype(F32)
                one = jnp.broadcast_to(tiles[0:CELLS, at:at + 1], (CELLS, LANES))
                flags = one if flags is None else jnp.where(flag_lane >= slot * SUB, one, flags)
            flag_of[h] = flags

    def band_split(dates, j):
        rows = []
        behind = SLOT * jnp.where(j == steps - 2, steps + 2, j + 2)
        for w in dates:
            here = recv[w, pl.ds(SLOT * (j + 1), ML_AZ)]
            before = recv[w, pl.ds(SLOT * j, ML_AZ)]
            after = recv[w, pl.ds(behind, ML_AZ)]
            edge = jnp.where(from_before, before, after)
            rows.append(jnp.concatenate([here, edge], axis=2).reshape(ML_AZ * SUB, 4 * LANES))
        made = jnp.dot(jnp.concatenate(rows, axis=0), mat[...], preferred_element_type=F32)
        return made.astype(BF16).astype(F32).reshape(len(dates), ML_AZ, SUB, 4 * LANES)

    def read(w, j, band, part):
        cols = slice((2 * band + part) * LANES, (2 * band + part + 1) * LANES)
        if w in OWN:
            return [bands_own[j, OWN.index(w), r, :, cols] for r in range(ML_AZ)]
        return [bands_far[FAR.index(w), r, :, cols] for r in range(ML_AZ)]

    def total(terms):
        terms = list(terms)
        while len(terms) > 1:
            terms = [a + b for a, b in zip(terms[::2], terms[1::2])]
        return terms[0]

    def keep_sum(j, at, value):
        high = value.astype(BF16)
        low = (value - high.astype(F32)).astype(BF16)
        both[j, at * SUB:at * SUB + SUB, 0:LANES] = high
        both[j, at * SUB:at * SUB + SUB, LANES:2 * LANES] = low

    def products(dates, pairs, j):
        for band in range(2):
            for w in dates:
                re, im = (read(w, j, band, part) for part in range(2))
                keep_sum(j, power_slot(band, w), total([a * a for a in re]) + total([a * a for a in im]))
            for w, k in pairs:
                a_re, a_im = (read(w, j, band, part) for part in range(2))
                b_re, b_im = (read(w + k, j, band, part) for part in range(2))
                re = total([a * b for a, b in zip(a_re, b_re)]) + total([a * b for a, b in zip(a_im, b_im)])
                im = total([a * b for a, b in zip(a_im, b_re)]) - total([a * b for a, b in zip(a_re, b_im)])
                keep_sum(j, pair_slot(0, band, w, k), re)
                keep_sum(j, pair_slot(1, band, w, k), im)

    def own_step(j):
        bands_own[j] = band_split(OWN, j)
        products(OWN, OWN_PAIRS, j)

    def far_step(j):
        bands_far[...] = band_split(FAR, j)
        products(FAR, FAR_PAIRS, j)
        red[j] = lax.dot_general(selector, both[j], contract, preferred_element_type=F32)

    def wave_signal():
        @pl.when(has_left)
        def _():
            pl.semaphore_signal(wave_sem.at[1], inc=1, device_id={"date": me - SPAN}, device_id_type=mesh_id)

        @pl.when(has_right)
        def _():
            pl.semaphore_signal(wave_sem.at[0], inc=1, device_id={"date": me + SPAN}, device_id_type=mesh_id)

    def wave(t, carry):
        @pl.when(has_left)
        def _():
            pl.semaphore_wait(wave_sem.at[0], 1)

        @pl.when(has_right)
        def _():
            pl.semaphore_wait(wave_sem.at[1], 1)

        @pl.when(t < slabs - 1)
        def _():
            wave_signal()

        return carry

    own_arrive(0, True)
    make_after(OWN)
    make_edges(OWN)

    wave_signal()

    def stream(t, carry):
        u = t - LAG

        @pl.when(t < steps)
        def _():
            own_arrive(t, False)

        @pl.when(t < slabs)
        def _():
            wave(t, 0)

        @pl.when(t <= steps)
        def _():
            own_step(t - 1)

        @pl.when(u == 0)
        def _():
            far_arrive(0, True)
            make_after(FAR)
            make_edges(FAR)
            make_flags()

        @pl.when((u > 0) & (u < steps - 1))
        def _():
            far_arrive(u, False)

        @pl.when(u > 0)
        def _():
            far_step(u - 1)

        @pl.when(u == steps - 1)
        def _():
            far_arrive(u, False)

        return carry

    lax.fori_loop(1, steps + LAG + 1, stream, 0)
    lax.fori_loop(steps + LAG + 1, slabs, wave, 0)

    shape = (steps, CELLS, LANES)
    c_id = lax.broadcasted_iota(jnp.int32, shape, 1)
    l_id = lax.broadcasted_iota(jnp.int32, shape, 2)
    i_id = lax.rem(l_id, SUB)

    def box(value):
        prefix = value
        for hop in (1, 2, 4):
            prefix = prefix + jnp.where(c_id >= hop, pltpu.roll(prefix, hop, 1), 0.0)
        whole = jnp.sum(value, axis=1, keepdims=True)
        suffix = whole - prefix + value
        first = jnp.where(i_id[0:1] > 0, pltpu.roll(suffix[steps - 1:steps], 1, 2), 0.0)
        last = jnp.where(i_id[0:1] < SUB - 1, pltpu.roll(prefix[0:1], LANES - 1, 2), 0.0)
        before = jnp.concatenate([first, suffix[0:steps - 1]], axis=0)
        after = jnp.concatenate([prefix[1:steps], last], axis=0)
        return before + whole + after

    def register(at):
        return red[:, :, at * LANES:at * LANES + LANES]

    lane = lax.broadcasted_iota(jnp.int32, (CELLS, LANES), 1)
    span_lanes = SPAN * SUB

    def aligned(value, ks, partner):
        parts = []
        for at, k in enumerate(ks):
            w = first_date(k) + (k if partner else 0)
            move = (at * SPAN - w) * SUB % LANES
            parts.append(pltpu.roll(value, move, 2) if move else value)
        return jnp.where(l_id < span_lanes, parts[0], parts[1])

    for h in range(HALVES):
        ks = (HALVES * h + 1, HALVES * h + 2)
        cr0, ci0, cr1, ci1 = (register(m * HALVES + h) for m in range(4))
        ab0, ab1 = (
            aligned(power, ks, False) * aligned(power, ks, True) + eps_power
            for power in (register(4 * HALVES), register(4 * HALVES + 1))
        )
        weight = flag_of[h][None] * 0.5 * ((cr0 * cr0 + ci0 * ci0) / ab0 + (cr1 * cr1 + ci1 * ci1) / ab1)
        phase = split_coef * (ci0 * cr1 - cr0 * ci1) / jnp.sqrt(ab0 * ab1)
        den = box(weight)
        num = box(weight * phase)
        quant[:, h] = den / (2 * RADIUS + 1)
        quant[:, HALVES + h] = num / (den + floor_weight)

    workers = msg.shape[0]
    share = steps // workers
    base = (slabs - workers) // 2
    is_worker = (z >= base) & (z < base + workers)
    half = LANES // 2
    ranks = LANES // SUB
    zero = jnp.zeros((CELLS, LANES), F32)

    def turned(rows):
        rows = list(rows)
        bit = 1
        while bit < len(rows):
            upper = lax.rem(lane // (SUB * bit), 2) == 1
            for a in range(len(rows)):
                if a & bit == 0:
                    low, high = rows[a], rows[a | bit]
                    rows[a] = jnp.where(upper, pltpu.roll(high, SUB * bit, 1), low)
                    rows[a | bit] = jnp.where(upper, high, pltpu.roll(low, LANES - SUB * bit, 1))
            bit *= 2
        return rows

    def line_copy(u):
        return pltpu.make_async_remote_copy(
            src_ref=msg.at[u], dst_ref=got.at[z],
            send_sem=send_sem.at[3], recv_sem=recv_sem.at[0, steps],
            device_id={"date": (base + u) * SPAN + q}, device_id_type=mesh_id,
        )

    for u in range(workers):
        for kind in range(2):
            rows = [zero] * ranks
            for h in range(HALVES):
                for jj in range(share):
                    rows[h * ranks // 2 + jj] = quant[u * share + jj, kind * HALVES + h]
            for slot, value in enumerate(turned(rows)):
                msg[u, kind, slot] = value

        @pl.when(z != base + u)
        def _():
            line_copy(u).start()

        @pl.when(z == base + u)
        def _():
            pltpu.make_async_copy(msg.at[u], got.at[z], recv_sem.at[0, steps]).start()

    def out_copy(target):
        return pltpu.make_async_remote_copy(
            src_ref=pack.at[target], dst_ref=back.at[(z - base) * SPAN + q],
            send_sem=send_sem.at[4], recv_sem=recv_sem.at[0, steps + 1],
            device_id={"date": target}, device_id_type=mesh_id,
        )

    in_lower = lane < half

    def split(low, high):
        return jnp.where(in_lower, low, high)

    def fold(value):
        return value + pltpu.roll(value, half, 1)

    def at(values, d):
        return values[d] if 0 <= d < n else zero

    def held(kind, position, d):
        return got[d // SPAN, kind, position * SPAN + d % SPAN] if d < n else zero

    def relax():
        near, wide = [], []
        for kind in range(2):
            near.append([held(kind, 0, d + 1) for d in range(n)])
            wide.append([split(held(kind, 1, d + 1), held(kind, 1, d + 2)) for d in range(n)])
        near_back = [split(at(near[0], d - 1), at(near[0], d - 3)) for d in range(n)]
        wide_back = [split(at(wide[0], d - 2), at(wide[0], d - 4)) for d in range(n)]
        wsum = [fold((a + b) + (c + e)) for a, b, c, e in zip(near[0], wide[0], near_back, wide_back)]
        near_flow = [a * b for a, b in zip(*near)]
        wide_flow = [a * b for a, b in zip(*wide)]
        flow = [
            (split(at(near_flow, d - 1), at(near_flow, d - 3)) + split(at(wide_flow, d - 2), at(wide_flow, d - 4)))
            - (near_flow[d] + wide_flow[d]) for d in range(n)
        ]
        phi = [zero]
        for d in range(n - 1):
            first = near[1][d]
            phi.append(phi[-1] + split(first, pltpu.roll(first, half, 1)))
        pull = [ridge_weight * p for p in phi]
        inv = [1.0 / (t + ridge_weight) for t in wsum]
        for sweep in range(ITERS):
            up = [split(at(phi, d), at(phi, d + 2)) for d in range(n + 2)]
            down = [split(at(phi, d - 2), at(phi, d - 4)) for d in range(n + 2)]
            phi = [
                (
                    fold(
                        flow[d] + (near[0][d] * up[d + 1] + wide[0][d] * at(up[:n], d + 2))
                        + (near_back[d] * down[d + 1] + wide_back[d] * down[d])
                    ) + pull[d]
                ) * inv[d] for d in range(n)
            ]
        return phi, wsum

    @pl.when(is_worker)
    def _():
        pltpu.make_async_copy(got, got, recv_sem.at[0, steps]).wait()
        phi, wsum = relax()
        for d in range(n):
            pack[d] = split(phi[d], wsum[d])

        def send_back(i, carry):
            for g in range(SPAN):
                target = SPAN * jnp.where(z < slabs // 2, slabs - 1 - i, i) + g

                @pl.when(target != me)
                def _():
                    out_copy(target).start()
            return carry

        lax.fori_loop(0, slabs, send_back, 0)
        pltpu.make_async_copy(
            pack.at[me], back.at[(z - base) * SPAN + q], recv_sem.at[0, steps + 1]
        ).start()

    def drain(ref, sem):
        pltpu.make_async_copy(ref, ref, sem).wait()

    tiles = SLOT + ML_AZ * (steps - 1)
    drain(data.at[pl.ds(0, SPAN - 1), pl.ds(0, tiles)], send_sem.at[0])

    @pl.when(has_left)
    def _():
        drain(data.at[pl.ds(0, SIDE), pl.ds(0, tiles)], send_sem.at[1])

    @pl.when(has_right)
    def _():
        drain(data.at[pl.ds(0, SIDE), pl.ds(0, tiles)], send_sem.at[2])

    drain(msg.at[pl.ds(0, workers - 1)], send_sem.at[3])

    @pl.when(jnp.logical_not(is_worker))
    def _():
        drain(msg.at[0], send_sem.at[3])

    drain(back, recv_sem.at[0, steps + 1])

    @pl.when(is_worker)
    def _():
        drain(pack.at[pl.ds(0, n - 1)], send_sem.at[4])

    rows = []
    for kind in range(2):
        for s in range(SPAN):
            value = None
            for u in range(workers):
                move = (u * share * SUB - kind * half) % LANES
                piece = back[u * SPAN + s]
                piece = pltpu.roll(piece, move, 1) if move else piece
                value = piece if value is None else jnp.where(lane >= u * share * SUB, piece, value)
            rows.append(value)
    value = jnp.concatenate(rows, axis=0)
    high = value.astype(BF16)
    low = (value - high.astype(F32)).astype(BF16)
    spread = jnp.dot(
        jnp.concatenate([high, low], axis=0), place[...],
        preferred_element_type=F32,
    )
    count = 2 * SPAN * CELLS
    spread = spread[0:count] + spread[count:2 * count]
    spread = spread.reshape(2 * SPAN, CELLS, width)
    s_row = lax.broadcasted_iota(jnp.int32, spread.shape, 1)
    s_col = lax.broadcasted_iota(jnp.int32, spread.shape, 2)
    result = jnp.sum(jnp.where(lax.rem(s_col, CELLS) == s_row, spread, 0.0), axis=1)
    out_ref[0] = result[0:SPAN]
    out_ref[1] = result[SPAN:2 * SPAN]


def local(slc_stack, band_taps, pair_flags):
    n = lax.axis_size("date")
    rows, span = slc_stack.shape[2:]
    steps = span // LANES // SUB
    slabs = n // SPAN
    assert rows == SUB and rows // ML_AZ == SPAN and span == LANES * LANES
    assert n % (LANES // SUB) == 0 and steps == LANES // SUB
    workers = 1
    while 2 * workers <= min(steps, slabs // 2):
        workers *= 2
    tiles = SLOT * (steps + 3)

    vmem = pl.BlockSpec(memory_space=pltpu.VMEM)
    small = lambda *lead: pltpu.VMEM((*lead, CELLS, LANES), F32)
    sem = lambda *lead: pltpu.SemaphoreType.DMA(lead)
    both = pl.pallas_call(
        functools.partial(kernel, n, steps),
        out_shape=jax.ShapeDtypeStruct((2, rows // ML_AZ, span // ML_RG), F32),
        in_specs=[pl.BlockSpec(memory_space=pl.ANY)] * 3,
        out_specs=vmem,
        scratch_shapes=[
            pltpu.VMEM((2, rows, span), BF16),
            pltpu.VMEM((1, SPAN), jnp.int32),
            pltpu.VMEM((2, 2, TAPS), BF16),
            pltpu.VMEM((8, LANES), F32),
            pltpu.VMEM((2 * SUB * SUB, LANES), F32),
            pltpu.VMEM((SPAN, tiles, SUB, 2 * LANES), BF16),
            pltpu.VMEM((WIN, tiles, SUB, 2 * LANES), BF16),
            pltpu.VMEM((4 * LANES, 4 * LANES), BF16),
            pltpu.VMEM((steps, SPAN, ML_AZ, SUB, 4 * LANES), F32),
            pltpu.VMEM((SPAN, ML_AZ, SUB, 4 * LANES), F32),
            pltpu.VMEM((steps, SLOTS * SUB, 2 * LANES), BF16),
            pltpu.VMEM((steps, CELLS, SLOTS * SUB), F32),
            small(steps, 2 * HALVES),
            small(workers, 2, GROUP),
            small(slabs, 2, GROUP),
            small(n),
            small(workers * SPAN),
            pltpu.VMEM((LANES, span // ML_RG), BF16),
            small(HALVES),
            sem(3), sem(5), sem(3, steps + 2), pltpu.SemaphoreType.REGULAR((2,)),
        ],
        compiler_params=pltpu.CompilerParams(
            collective_id=0, has_side_effects=True, vmem_limit_bytes=60 * 1024 * 1024
        ),
    )(slc_stack, pair_flags, band_taps)
    return both[0:1], both[1:2]


def solution(mesh):
    in_specs = (P("date", None, "group", None), P(), P("date", None))
    out_specs = (P("date", "group", None), P("date", "group", None))
    return jax.shard_map(local, mesh=mesh, in_specs=in_specs, out_specs=out_specs, check_vma=False)
```

```python
import functools

import jax
import jax.numpy as jnp
from jax import lax
from jax.experimental import pallas as pl
from jax.experimental.pallas import tpu as pltpu
from jax.sharding import PartitionSpec as P

TAPS = 32
ML_AZ = 4
ML_RG = 16
SPAN = 4
RADIUS = 8
ITERS = 4

LANES = 128
CELLS = LANES // ML_RG
SUB = 16
SIDE = SPAN // 2
WIN = SPAN + 2 * SIDE
SLOT = ML_AZ + 1
REACH = TAPS // 2
LAG = 3

eps_power = 1e-06
floor_weight = 0.1
ridge_weight = 0.05
split_coef = 2.0

F32 = jnp.float32
BF16 = jnp.bfloat16

OWN = tuple(range(SIDE, SIDE + SPAN))
FAR = tuple(range(SIDE)) + tuple(range(SIDE + SPAN, WIN))


def first_date(k):
    return 0 if k == SPAN else 1


PAIRS = [(first_date(k) + g, k) for k in range(1, SPAN + 1) for g in range(SPAN)]
OWN_PAIRS = [(w, k) for w, k in PAIRS if w in OWN and w + k in OWN]
FAR_PAIRS = [p for p in PAIRS if p not in OWN_PAIRS]


HALVES = 2
GROUP = SPAN * SPAN // HALVES


def pair_slot(imag, band, w, k):
    return ((2 * band + imag) * HALVES + (k - 1) // HALVES) * GROUP + (k - 1) % HALVES * SPAN + w - first_date(k)


def power_slot(band, w):
    return 4 * HALVES * GROUP + band * WIN + w


SLOTS = power_slot(1, WIN - 1) + 1


def kernel(
    n, steps,
    slc_hbm, flags_hbm, taps_hbm, out_ref,
    slc, flags_in, taps_in, taps_ref, turn, data, recv, mat, bands_own, bands_far, both, red, quant,
    msg, got, pack, back, place, flag_of,
    in_sem, send_sem, recv_sem, wave_sem,
):
    me = lax.axis_index("date")
    q = lax.rem(me, SPAN)
    z = me // SPAN
    slabs = n // SPAN
    has_left = z > 0
    has_right = z < slabs - 1
    mesh_id = pl.DeviceIdType.MESH

    slc_load = pltpu.make_async_copy(slc_hbm.at[0], slc, in_sem.at[0])
    slc_load.start()
    flags_load = pltpu.make_async_copy(flags_hbm, flags_in, in_sem.at[1])
    flags_load.start()
    taps_load = pltpu.make_async_copy(taps_hbm, taps_in, in_sem.at[2])
    taps_load.start()
    barrier = pltpu.get_barrier_semaphore()

    for hop in range(1, SPAN):
        pl.semaphore_signal(
            barrier, inc=1, device_id={"date": z * SPAN + lax.rem(q + hop, SPAN)}, device_id_type=mesh_id
        )

    @pl.when(has_left)
    def _():
        pl.semaphore_signal(barrier, inc=1, device_id={"date": me - SPAN}, device_id_type=mesh_id)

    @pl.when(has_right)
    def _():
        pl.semaphore_signal(barrier, inc=1, device_id={"date": me + SPAN}, device_id_type=mesh_id)

    flags_load.wait()
    tile_row = lax.broadcasted_iota(jnp.int32, (SUB, 2 * LANES), 0)
    own_flags = flags_in[...].astype(F32)
    taps_load.wait()
    taps_ref[...] = jnp.zeros_like(taps_ref)
    for band in range(2):
        taps_ref[2 * band:2 * band + 2, 0:TAPS] = taps_in[band].astype(F32)

    k_id = lax.broadcasted_iota(jnp.int32, (LANES, LANES), 0)
    j_id = lax.broadcasted_iota(jnp.int32, (LANES, LANES), 1)
    reach = k_id - j_id + TAPS // 2
    circ = []
    for m in range(4):
        base = jnp.broadcast_to(taps_ref[m:m + 1, :], (LANES, LANES))
        circ.append(pltpu.roll(base, LANES - TAPS // 2, 1, stride=1, stride_axis=0).T)
    for edge in range(2):
        inside = (reach >= 0) & (reach < LANES)
        keep = inside if edge == 0 else jnp.logical_not(inside)
        row = edge * 2 * LANES
        for band in range(2):
            re_part = jnp.where(keep, circ[2 * band], 0.0).astype(BF16)
            im_value = jnp.where(keep, circ[2 * band + 1], 0.0)
            im_part = im_value.astype(BF16)
            im_minus = (-im_value).astype(BF16)
            col = band * 2 * LANES
            mat[row:row + 128, col:col + 128] = re_part
            mat[row:row + 128, col + 128:col + 256] = im_part
            mat[row + 128:row + 256, col:col + 128] = im_minus
            mat[row + 128:row + 256, col + 128:col + 256] = re_part

    slc_load.wait()

    def regroup(j, carry):
        for part in range(2):
            for i in range(SUB):
                at = pl.multiple_of((steps * i + j) * LANES, LANES)
                value = slc[part, :, pl.ds(at, LANES)].astype(F32)
                turn[(part * SUB + i) * SUB:(part * SUB + i + 1) * SUB, :] = value
        for part in range(2):
            for s in range(SPAN):
                for r in range(ML_AZ):
                    row = part * SUB * SUB + ML_AZ * s + r
                    value = turn[pl.ds(row, SUB, stride=SUB), :].astype(BF16)
                    data[s, SLOT * (j + 1) + r, :, part * LANES:part * LANES + LANES] = value
        return carry

    tap_lane = lax.broadcasted_iota(jnp.int32, (SUB, LANES), 1)


    def edge_at(r, part):
        return r // 2, (r % 2 * 2 + part) * 2 * REACH

    def send_edges():
        for s in range(SPAN):
            packed = [None, None]
            for r in range(ML_AZ):
                for part in range(2):
                    value = data[s, SLOT * steps + r, :, part * LANES:part * LANES + LANES].astype(F32)
                    tile, at = edge_at(r, part)
                    head = pltpu.roll(value, at, 1) if at else value
                    tail = pltpu.roll(value, (at + 2 * REACH) % LANES, 1)
                    both_ends = jnp.where(tap_lane < at + REACH, head, tail)
                    if part == 0:
                        flag = jnp.broadcast_to(own_flags[0:1, r:r + 1], both_ends.shape)
                        both_ends = jnp.where(tap_lane == at + REACH - 1, flag, both_ends)
                    old = packed[tile]
                    packed[tile] = both_ends if old is None else jnp.where(tap_lane >= at, both_ends, old)
            data[s, SLOT + ML_AZ] = jnp.concatenate(packed, axis=1).astype(BF16)

    regroup(steps - 1, 0)
    send_edges()
    regroup(0, 0)
    regroup(1, 0)

    def chunk(ref, j, first):
        return ref.at[pl.ds(SLOT * (j + 1), SLOT if first else ML_AZ)]

    def slab_copy(target, j, first):
        return pltpu.make_async_remote_copy(
            src_ref=chunk(data.at[target], j, first), dst_ref=chunk(recv.at[q + SIDE], j, first),
            send_sem=send_sem.at[0], recv_sem=recv_sem.at[1, j],
            device_id={"date": z * SPAN + target}, device_id_type=mesh_id,
        )

    def own_copy(j, first):
        return pltpu.make_async_copy(
            chunk(data.at[q], j, first), chunk(recv.at[q + SIDE], j, first), recv_sem.at[1, j]
        )

    def side_copy(w, j, first):
        go_left = w < SPAN
        to, device = (w + SPAN, me - SPAN) if go_left else (w - SPAN, me + SPAN)
        return pltpu.make_async_remote_copy(
            src_ref=chunk(recv.at[w], j, first), dst_ref=chunk(recv.at[to], j, first),
            send_sem=send_sem.at[1 if go_left else 2], recv_sem=recv_sem.at[2 if go_left else 0, j],
            device_id={"date": device}, device_id_type=mesh_id,
        )

    def arrived(dates, side, j, first):
        ref = recv.at[pl.ds(dates[0], len(dates)), pl.ds(SLOT * (j + 1), SLOT if first else ML_AZ)]
        pltpu.make_async_copy(ref, ref, recv_sem.at[side, j]).wait()

    near = SPAN - 1 + has_left.astype(jnp.int32) + has_right.astype(jnp.int32)
    pl.semaphore_wait(barrier, near)

    def send_chunk(j, first):
        own_copy(j, first).start()
        for hop in (2, 3, 1):
            slab_copy(lax.rem(q + hop, SPAN), j, first).start()

    send_chunk(0, True)

    def send_more(j, carry):
        regroup(j + 1, 0)
        send_chunk(j, False)
        return carry

    lax.fori_loop(1, steps - 2, send_more, 0)
    for j in range(steps - 2, steps):
        send_chunk(j, False)

    @pl.when(jnp.logical_not(has_left))
    def _():
        for w in range(SIDE):
            recv[w] = jnp.zeros(recv.shape[1:], BF16)

    @pl.when(jnp.logical_not(has_right))
    def _():
        for w in range(SIDE + SPAN, WIN):
            recv[w] = jnp.zeros(recv.shape[1:], BF16)

    width = out_ref.shape[2]
    place_row = lax.broadcasted_iota(jnp.int32, (LANES, width), 0)
    place_block = lax.broadcasted_iota(jnp.int32, (LANES, width), 1) // CELLS
    on_place = place_row == lax.rem(place_block, steps) * SUB + place_block // steps
    place[...] = jnp.where(on_place, 1.0, 0.0).astype(BF16)

    sel_row = lax.broadcasted_iota(jnp.int32, (CELLS, 2 * LANES), 0)
    sel_lane = lax.broadcasted_iota(jnp.int32, (CELLS, 2 * LANES), 1)
    selector = jnp.where(lax.rem(sel_lane, LANES) // ML_RG == sel_row, 1.0, 0.0).astype(BF16)
    contract = (((1,), (1,)), ((), ()))
    edge_lane = lax.rem(lax.broadcasted_iota(jnp.int32, (ML_AZ, SUB, 2 * LANES), 2), LANES)
    from_before = edge_lane >= LANES - TAPS // 2
    sub_row = lax.broadcasted_iota(jnp.int32, (ML_AZ, SUB, 2 * LANES), 1)

    def own_arrive(j, first):
        arrived(OWN, 1, j, first)

        @pl.when(has_left)
        def _():
            for w in OWN[:SIDE]:
                side_copy(w, j, first).start()

        @pl.when(has_right)
        def _():
            for w in OWN[SIDE:]:
                side_copy(w, j, first).start()

    def far_arrive(j, first):
        @pl.when(has_left)
        def _():
            arrived(FAR[:SIDE], 0, j, first)

        @pl.when(has_right)
        def _():
            arrived(FAR[SIDE:], 2, j, first)

    def make_after(dates):
        for w in dates:
            value = recv[w, SLOT:SLOT + ML_AZ].astype(F32)
            value = jnp.where(sub_row < SUB - 1, pltpu.roll(value, SUB - 1, 1), 0.0)
            recv[w, SLOT * (steps + 1):SLOT * (steps + 1) + ML_AZ] = value.astype(BF16)

    def make_edges(dates):
        for w in dates:
            tiles = recv[w, SLOT + ML_AZ].astype(F32)
            for r in range(ML_AZ):
                before, after = [], []
                for part in range(2):
                    tile, at = edge_at(r, part)
                    value = tiles[:, tile * LANES:tile * LANES + LANES]
                    after.append(pltpu.roll(value, LANES - at, 1) if at else value)
                    value = pltpu.roll(value, (LANES - 2 * REACH - at) % LANES, 1)
                    before.append(jnp.where(tile_row[:, 0:LANES] > 0, pltpu.roll(value, 1, 0), 0.0))
                recv[w, r] = jnp.concatenate(before, axis=1).astype(BF16)
                recv[w, SLOT * (steps + 2) + r] = jnp.concatenate(after, axis=1).astype(BF16)

    def make_flags():
        flag_lane = lax.broadcasted_iota(jnp.int32, (CELLS, LANES), 1)
        for h in range(HALVES):
            flags = None
            for slot in range(GROUP):
                k, g = HALVES * h + slot // SPAN + 1, slot % SPAN
                tile, at = edge_at(k - 1, 0)
                at += tile * LANES + REACH - 1
                tiles = recv[first_date(k) + g, SLOT + ML_AZ].astype(F32)
                one = jnp.broadcast_to(tiles[0:CELLS, at:at + 1], (CELLS, LANES))
                flags = one if flags is None else jnp.where(flag_lane >= slot * SUB, one, flags)
            flag_of[h] = flags

    def band_split(dates, j):
        rows = []
        behind = SLOT * jnp.where(j == steps - 2, steps + 2, j + 2)
        for w in dates:
            here = recv[w, pl.ds(SLOT * (j + 1), ML_AZ)]
            before = recv[w, pl.ds(SLOT * j, ML_AZ)]
            after = recv[w, pl.ds(behind, ML_AZ)]
            edge = jnp.where(from_before, before, after)
            rows.append(jnp.concatenate([here, edge], axis=2).reshape(ML_AZ * SUB, 4 * LANES))
        made = jnp.dot(jnp.concatenate(rows, axis=0), mat[...], preferred_element_type=F32)
        return made.astype(BF16).astype(F32).reshape(len(dates), ML_AZ, SUB, 4 * LANES)

    def read(w, j, band, part):
        cols = slice((2 * band + part) * LANES, (2 * band + part + 1) * LANES)
        if w in OWN:
            return [bands_own[j, OWN.index(w), r, :, cols] for r in range(ML_AZ)]
        return [bands_far[FAR.index(w), r, :, cols] for r in range(ML_AZ)]

    def total(terms):
        terms = list(terms)
        while len(terms) > 1:
            terms = [a + b for a, b in zip(terms[::2], terms[1::2])]
        return terms[0]

    def keep_sum(j, at, value):
        high = value.astype(BF16)
        low = (value - high.astype(F32)).astype(BF16)
        both[j, at * SUB:at * SUB + SUB, 0:LANES] = high
        both[j, at * SUB:at * SUB + SUB, LANES:2 * LANES] = low

    def products(dates, pairs, j):
        for band in range(2):
            for w in dates:
                re, im = (read(w, j, band, part) for part in range(2))
                keep_sum(j, power_slot(band, w), total([a * a for a in re]) + total([a * a for a in im]))
            for w, k in pairs:
                a_re, a_im = (read(w, j, band, part) for part in range(2))
                b_re, b_im = (read(w + k, j, band, part) for part in range(2))
                re = total([a * b for a, b in zip(a_re, b_re)]) + total([a * b for a, b in zip(a_im, b_im)])
                im = total([a * b for a, b in zip(a_im, b_re)]) - total([a * b for a, b in zip(a_re, b_im)])
                keep_sum(j, pair_slot(0, band, w, k), re)
                keep_sum(j, pair_slot(1, band, w, k), im)

    def own_step(j):
        bands_own[j] = band_split(OWN, j)
        products(OWN, OWN_PAIRS, j)

    def far_step(j):
        bands_far[...] = band_split(FAR, j)
        products(FAR, FAR_PAIRS, j)
        red[j] = lax.dot_general(selector, both[j], contract, preferred_element_type=F32)

    def wave_signal():
        @pl.when(has_left)
        def _():
            pl.semaphore_signal(wave_sem.at[1], inc=1, device_id={"date": me - SPAN}, device_id_type=mesh_id)

        @pl.when(has_right)
        def _():
            pl.semaphore_signal(wave_sem.at[0], inc=1, device_id={"date": me + SPAN}, device_id_type=mesh_id)

    def wave(t, carry):
        @pl.when(has_left)
        def _():
            pl.semaphore_wait(wave_sem.at[0], 1)

        @pl.when(has_right)
        def _():
            pl.semaphore_wait(wave_sem.at[1], 1)

        @pl.when(t < slabs - 1)
        def _():
            wave_signal()

        return carry

    own_arrive(0, True)
    make_after(OWN)
    make_edges(OWN)

    wave_signal()

    def stream(t, carry):
        u = t - LAG

        @pl.when(t < steps)
        def _():
            own_arrive(t, False)

        @pl.when(t < slabs)
        def _():
            wave(t, 0)

        @pl.when(t <= steps)
        def _():
            own_step(t - 1)

        @pl.when(u == 0)
        def _():
            far_arrive(0, True)
            make_after(FAR)
            make_edges(FAR)
            make_flags()

        @pl.when((u > 0) & (u < steps - 1))
        def _():
            far_arrive(u, False)

        @pl.when(u > 0)
        def _():
            far_step(u - 1)

        @pl.when(u == steps - 1)
        def _():
            far_arrive(u, False)

        return carry

    lax.fori_loop(1, steps + LAG + 1, stream, 0)
    lax.fori_loop(steps + LAG + 1, slabs, wave, 0)

    shape = (steps, CELLS, LANES)
    c_id = lax.broadcasted_iota(jnp.int32, shape, 1)
    l_id = lax.broadcasted_iota(jnp.int32, shape, 2)
    i_id = lax.rem(l_id, SUB)

    def box(value):
        prefix = value
        for hop in (1, 2, 4):
            prefix = prefix + jnp.where(c_id >= hop, pltpu.roll(prefix, hop, 1), 0.0)
        whole = jnp.sum(value, axis=1, keepdims=True)
        suffix = whole - prefix + value
        first = jnp.where(i_id[0:1] > 0, pltpu.roll(suffix[steps - 1:steps], 1, 2), 0.0)
        last = jnp.where(i_id[0:1] < SUB - 1, pltpu.roll(prefix[0:1], LANES - 1, 2), 0.0)
        before = jnp.concatenate([first, suffix[0:steps - 1]], axis=0)
        after = jnp.concatenate([prefix[1:steps], last], axis=0)
        return before + whole + after

    def register(at):
        return red[:, :, at * LANES:at * LANES + LANES]

    lane = lax.broadcasted_iota(jnp.int32, (CELLS, LANES), 1)
    span_lanes = SPAN * SUB

    def aligned(value, ks, partner):
        parts = []
        for at, k in enumerate(ks):
            w = first_date(k) + (k if partner else 0)
            move = (at * SPAN - w) * SUB % LANES
            parts.append(pltpu.roll(value, move, 2) if move else value)
        return jnp.where(l_id < span_lanes, parts[0], parts[1])

    for h in range(HALVES):
        ks = (HALVES * h + 1, HALVES * h + 2)
        cr0, ci0, cr1, ci1 = (register(m * HALVES + h) for m in range(4))
        ab0, ab1 = (
            aligned(power, ks, False) * aligned(power, ks, True) + eps_power
            for power in (register(4 * HALVES), register(4 * HALVES + 1))
        )
        abab = ab0 * ab1
        shared = (cr0 * cr0 + ci0 * ci0) * ab1 + (cr1 * cr1 + ci1 * ci1) * ab0
        weight = flag_of[h][None] * 0.5 * (shared / abab)
        phase = split_coef * (ci0 * cr1 - cr0 * ci1) / jnp.sqrt(abab)
        den = box(weight)
        num = box(weight * phase)
        quant[:, h] = den * (1.0 / (2 * RADIUS + 1))
        quant[:, HALVES + h] = num / (den + floor_weight)

    workers = msg.shape[0]
    share = steps // workers
    base = (slabs - workers) // 2
    is_worker = (z >= base) & (z < base + workers)
    half = LANES // 2
    ranks = LANES // SUB
    zero = jnp.zeros((CELLS, LANES), F32)

    def turned(rows):
        rows = list(rows)
        bit = 1
        while bit < len(rows):
            upper = lax.rem(lane // (SUB * bit), 2) == 1
            for a in range(len(rows)):
                if a & bit == 0:
                    low, high = rows[a], rows[a | bit]
                    rows[a] = jnp.where(upper, pltpu.roll(high, SUB * bit, 1), low)
                    rows[a | bit] = jnp.where(upper, high, pltpu.roll(low, LANES - SUB * bit, 1))
            bit *= 2
        return rows

    def line_copy(u):
        return pltpu.make_async_remote_copy(
            src_ref=msg.at[u], dst_ref=got.at[z],
            send_sem=send_sem.at[3], recv_sem=recv_sem.at[0, steps],
            device_id={"date": (base + u) * SPAN + q}, device_id_type=mesh_id,
        )

    for u in range(workers):
        for kind in range(2):
            rows = [zero] * ranks
            for h in range(HALVES):
                for jj in range(share):
                    rows[h * ranks // 2 + jj] = quant[u * share + jj, kind * HALVES + h]
            for slot, value in enumerate(turned(rows)):
                msg[u, kind, slot] = value

        @pl.when(z != base + u)
        def _():
            line_copy(u).start()

        @pl.when(z == base + u)
        def _():
            pltpu.make_async_copy(msg.at[u], got.at[z], recv_sem.at[0, steps]).start()

    def out_copy(target):
        return pltpu.make_async_remote_copy(
            src_ref=pack.at[target], dst_ref=back.at[(z - base) * SPAN + q],
            send_sem=send_sem.at[4], recv_sem=recv_sem.at[0, steps + 1],
            device_id={"date": target}, device_id_type=mesh_id,
        )

    in_lower = lane < half

    def split(low, high):
        return jnp.where(in_lower, low, high)

    def fold(value):
        return value + pltpu.roll(value, half, 1)

    def at(values, d):
        return values[d] if 0 <= d < n else zero

    def held(kind, position, d):
        return got[d // SPAN, kind, position * SPAN + d % SPAN] if d < n else zero

    def relax():
        near, wide = [], []
        for kind in range(2):
            near.append([held(kind, 0, d + 1) for d in range(n)])
            wide.append([split(held(kind, 1, d + 1), held(kind, 1, d + 2)) for d in range(n)])
        near_back = [split(at(near[0], d - 1), at(near[0], d - 3)) for d in range(n)]
        wide_back = [split(at(wide[0], d - 2), at(wide[0], d - 4)) for d in range(n)]
        wsum = [fold((a + b) + (c + e)) for a, b, c, e in zip(near[0], wide[0], near_back, wide_back)]
        near_flow = [a * b for a, b in zip(*near)]
        wide_flow = [a * b for a, b in zip(*wide)]
        flow = [
            (split(at(near_flow, d - 1), at(near_flow, d - 3)) + split(at(wide_flow, d - 2), at(wide_flow, d - 4)))
            - (near_flow[d] + wide_flow[d]) for d in range(n)
        ]
        phi = [zero]
        for d in range(n - 1):
            first = near[1][d]
            phi.append(phi[-1] + split(first, pltpu.roll(first, half, 1)))
        pull = [ridge_weight * p for p in phi]
        inv = [1.0 / (t + ridge_weight) for t in wsum]
        for sweep in range(ITERS):
            up = [split(at(phi, d), at(phi, d + 2)) for d in range(n + 2)]
            down = [split(at(phi, d - 2), at(phi, d - 4)) for d in range(n + 2)]
            phi = [
                (
                    fold(
                        flow[d] + (near[0][d] * up[d + 1] + wide[0][d] * at(up[:n], d + 2))
                        + (near_back[d] * down[d + 1] + wide_back[d] * down[d])
                    ) + pull[d]
                ) * inv[d] for d in range(n)
            ]
        return phi, wsum

    @pl.when(is_worker)
    def _():
        pltpu.make_async_copy(got, got, recv_sem.at[0, steps]).wait()
        phi, wsum = relax()
        for d in range(n):
            pack[d] = split(phi[d], wsum[d])

        def send_back(i, carry):
            for g in range(SPAN):
                target = SPAN * jnp.where(z < slabs // 2, slabs - 1 - i, i) + g

                @pl.when(target != me)
                def _():
                    out_copy(target).start()
            return carry

        lax.fori_loop(0, slabs, send_back, 0)
        pltpu.make_async_copy(
            pack.at[me], back.at[(z - base) * SPAN + q], recv_sem.at[0, steps + 1]
        ).start()

    def drain(ref, sem):
        pltpu.make_async_copy(ref, ref, sem).wait()

    tiles = SLOT + ML_AZ * (steps - 1)
    drain(data.at[pl.ds(0, SPAN - 1), pl.ds(0, tiles)], send_sem.at[0])

    @pl.when(has_left)
    def _():
        drain(data.at[pl.ds(0, SIDE), pl.ds(0, tiles)], send_sem.at[1])

    @pl.when(has_right)
    def _():
        drain(data.at[pl.ds(0, SIDE), pl.ds(0, tiles)], send_sem.at[2])

    drain(msg.at[pl.ds(0, workers - 1)], send_sem.at[3])

    @pl.when(jnp.logical_not(is_worker))
    def _():
        drain(msg.at[0], send_sem.at[3])

    drain(back, recv_sem.at[0, steps + 1])

    @pl.when(is_worker)
    def _():
        drain(pack.at[pl.ds(0, n - 1)], send_sem.at[4])

    rows = []
    for kind in range(2):
        for s in range(SPAN):
            value = None
            for u in range(workers):
                move = (u * share * SUB - kind * half) % LANES
                piece = back[u * SPAN + s]
                piece = pltpu.roll(piece, move, 1) if move else piece
                value = piece if value is None else jnp.where(lane >= u * share * SUB, piece, value)
            rows.append(value)
    value = jnp.concatenate(rows, axis=0)
    high = value.astype(BF16)
    low = (value - high.astype(F32)).astype(BF16)
    spread = jnp.dot(
        jnp.concatenate([high, low], axis=0), place[...],
        preferred_element_type=F32,
    )
    count = 2 * SPAN * CELLS
    spread = spread[0:count] + spread[count:2 * count]
    spread = spread.reshape(2 * SPAN, CELLS, width)
    s_row = lax.broadcasted_iota(jnp.int32, spread.shape, 1)
    s_col = lax.broadcasted_iota(jnp.int32, spread.shape, 2)
    result = jnp.sum(jnp.where(lax.rem(s_col, CELLS) == s_row, spread, 0.0), axis=1)
    out_ref[0] = result[0:SPAN]
    out_ref[1] = result[SPAN:2 * SPAN]


def local(slc_stack, band_taps, pair_flags):
    n = lax.axis_size("date")
    rows, span = slc_stack.shape[2:]
    steps = span // LANES // SUB
    slabs = n // SPAN
    assert rows == SUB and rows // ML_AZ == SPAN and span == LANES * LANES
    assert n % (LANES // SUB) == 0 and steps == LANES // SUB
    workers = 1
    while 2 * workers <= min(steps, slabs // 2):
        workers *= 2
    tiles = SLOT * (steps + 3)

    vmem = pl.BlockSpec(memory_space=pltpu.VMEM)
    small = lambda *lead: pltpu.VMEM((*lead, CELLS, LANES), F32)
    sem = lambda *lead: pltpu.SemaphoreType.DMA(lead)
    both = pl.pallas_call(
        functools.partial(kernel, n, steps),
        out_shape=jax.ShapeDtypeStruct((2, rows // ML_AZ, span // ML_RG), F32),
        in_specs=[pl.BlockSpec(memory_space=pl.ANY)] * 3,
        out_specs=vmem,
        scratch_shapes=[
            pltpu.VMEM((2, rows, span), BF16),
            pltpu.VMEM((1, SPAN), jnp.int32),
            pltpu.VMEM((2, 2, TAPS), BF16),
            pltpu.VMEM((8, LANES), F32),
            pltpu.VMEM((2 * SUB * SUB, LANES), F32),
            pltpu.VMEM((SPAN, tiles, SUB, 2 * LANES), BF16),
            pltpu.VMEM((WIN, tiles, SUB, 2 * LANES), BF16),
            pltpu.VMEM((4 * LANES, 4 * LANES), BF16),
            pltpu.VMEM((steps, SPAN, ML_AZ, SUB, 4 * LANES), F32),
            pltpu.VMEM((SPAN, ML_AZ, SUB, 4 * LANES), F32),
            pltpu.VMEM((steps, SLOTS * SUB, 2 * LANES), BF16),
            pltpu.VMEM((steps, CELLS, SLOTS * SUB), F32),
            small(steps, 2 * HALVES),
            small(workers, 2, GROUP),
            small(slabs, 2, GROUP),
            small(n),
            small(workers * SPAN),
            pltpu.VMEM((LANES, span // ML_RG), BF16),
            small(HALVES),
            sem(3), sem(5), sem(3, steps + 2), pltpu.SemaphoreType.REGULAR((2,)),
        ],
        compiler_params=pltpu.CompilerParams(
            collective_id=0, has_side_effects=True, vmem_limit_bytes=60 * 1024 * 1024
        ),
    )(slc_stack, pair_flags, band_taps)
    return both[0:1], both[1:2]


def solution(mesh):
    in_specs = (P("date", None, "group", None), P(), P("date", None))
    out_specs = (P("date", "group", None), P("date", "group", None))
    return jax.shard_map(local, mesh=mesh, in_specs=in_specs, out_specs=out_specs, check_vma=False)
```

```python
import functools

import jax
import jax.numpy as jnp
from jax import lax
from jax.experimental import pallas as pl
from jax.experimental.pallas import tpu as pltpu
from jax.sharding import PartitionSpec as P

TAPS = 32
ML_AZ = 4
ML_RG = 16
SPAN = 4
RADIUS = 8
ITERS = 4

LANES = 128
CELLS = LANES // ML_RG
SUB = 16
SIDE = SPAN // 2
WIN = SPAN + 2 * SIDE
SLOT = ML_AZ + 1
REACH = TAPS // 2
LAG = 3

eps_power = 1e-06
floor_weight = 0.1
ridge_weight = 0.05
split_coef = 2.0

F32 = jnp.float32
BF16 = jnp.bfloat16

OWN = tuple(range(SIDE, SIDE + SPAN))
FAR = tuple(range(SIDE)) + tuple(range(SIDE + SPAN, WIN))


def first_date(k):
    return 0 if k == SPAN else 1


PAIRS = [(first_date(k) + g, k) for k in range(1, SPAN + 1) for g in range(SPAN)]
OWN_PAIRS = [(w, k) for w, k in PAIRS if w in OWN and w + k in OWN]
FAR_PAIRS = [p for p in PAIRS if p not in OWN_PAIRS]


HALVES = 2
GROUP = SPAN * SPAN // HALVES


def pair_slot(imag, band, w, k):
    return ((2 * band + imag) * HALVES + (k - 1) // HALVES) * GROUP + (k - 1) % HALVES * SPAN + w - first_date(k)


def power_slot(band, w):
    return 4 * HALVES * GROUP + band * WIN + w


SLOTS = power_slot(1, WIN - 1) + 1


def kernel(
    n, steps,
    slc_hbm, flags_hbm, taps_hbm, out_ref,
    slc, flags_in, taps_in, taps_ref, turn, data, recv, mat, bands_own, bands_far, both, red, quant,
    msg, got, pack, back, place, flag_of,
    in_sem, send_sem, recv_sem, wave_sem,
):
    me = lax.axis_index("date")
    q = lax.rem(me, SPAN)
    z = me // SPAN
    slabs = n // SPAN
    has_left = z > 0
    has_right = z < slabs - 1
    mesh_id = pl.DeviceIdType.MESH

    slc_load = pltpu.make_async_copy(slc_hbm.at[0], slc, in_sem.at[0])
    slc_load.start()
    flags_load = pltpu.make_async_copy(flags_hbm, flags_in, in_sem.at[1])
    flags_load.start()
    taps_load = pltpu.make_async_copy(taps_hbm, taps_in, in_sem.at[2])
    taps_load.start()
    barrier = pltpu.get_barrier_semaphore()

    for hop in range(1, SPAN):
        pl.semaphore_signal(
            barrier, inc=1, device_id={"date": z * SPAN + lax.rem(q + hop, SPAN)}, device_id_type=mesh_id
        )

    @pl.when(has_left)
    def _():
        pl.semaphore_signal(barrier, inc=1, device_id={"date": me - SPAN}, device_id_type=mesh_id)

    @pl.when(has_right)
    def _():
        pl.semaphore_signal(barrier, inc=1, device_id={"date": me + SPAN}, device_id_type=mesh_id)

    flags_load.wait()
    tile_row = lax.broadcasted_iota(jnp.int32, (SUB, 2 * LANES), 0)
    own_flags = flags_in[...].astype(F32)
    taps_load.wait()
    taps_ref[...] = jnp.zeros_like(taps_ref)
    for band in range(2):
        taps_ref[2 * band:2 * band + 2, 0:TAPS] = taps_in[band].astype(F32)

    k_id = lax.broadcasted_iota(jnp.int32, (LANES, LANES), 0)
    j_id = lax.broadcasted_iota(jnp.int32, (LANES, LANES), 1)
    reach = k_id - j_id + TAPS // 2
    circ = []
    for m in range(4):
        base = jnp.broadcast_to(taps_ref[m:m + 1, :], (LANES, LANES))
        circ.append(pltpu.roll(base, LANES - TAPS // 2, 1, stride=1, stride_axis=0).T)
    for edge in range(2):
        inside = (reach >= 0) & (reach < LANES)
        keep = inside if edge == 0 else jnp.logical_not(inside)
        row = edge * 2 * LANES
        for band in range(2):
            re_part = jnp.where(keep, circ[2 * band], 0.0).astype(BF16)
            im_value = jnp.where(keep, circ[2 * band + 1], 0.0)
            im_part = im_value.astype(BF16)
            im_minus = (-im_value).astype(BF16)
            col = band * 2 * LANES
            mat[row:row + 128, col:col + 128] = re_part
            mat[row:row + 128, col + 128:col + 256] = im_part
            mat[row + 128:row + 256, col:col + 128] = im_minus
            mat[row + 128:row + 256, col + 128:col + 256] = re_part

    slc_load.wait()

    def regroup(j, carry):
        for part in range(2):
            for i in range(SUB):
                at = pl.multiple_of((steps * i + j) * LANES, LANES)
                value = slc[part, :, pl.ds(at, LANES)].astype(F32)
                turn[(part * SUB + i) * SUB:(part * SUB + i + 1) * SUB, :] = value
        for part in range(2):
            for s in range(SPAN):
                for r in range(ML_AZ):
                    row = part * SUB * SUB + ML_AZ * s + r
                    value = turn[pl.ds(row, SUB, stride=SUB), :].astype(BF16)
                    data[s, SLOT * (j + 1) + r, :, part * LANES:part * LANES + LANES] = value
        return carry

    tap_lane = lax.broadcasted_iota(jnp.int32, (SUB, LANES), 1)


    def edge_at(r, part):
        return r // 2, (r % 2 * 2 + part) * 2 * REACH

    def send_edges():
        for s in range(SPAN):
            packed = [None, None]
            for r in range(ML_AZ):
                for part in range(2):
                    value = data[s, SLOT * steps + r, :, part * LANES:part * LANES + LANES].astype(F32)
                    tile, at = edge_at(r, part)
                    head = pltpu.roll(value, at, 1) if at else value
                    tail = pltpu.roll(value, (at + 2 * REACH) % LANES, 1)
                    both_ends = jnp.where(tap_lane < at + REACH, head, tail)
                    if part == 0:
                        flag = jnp.broadcast_to(own_flags[0:1, r:r + 1], both_ends.shape)
                        both_ends = jnp.where(tap_lane == at + REACH - 1, flag, both_ends)
                    old = packed[tile]
                    packed[tile] = both_ends if old is None else jnp.where(tap_lane >= at, both_ends, old)
            data[s, SLOT + ML_AZ] = jnp.concatenate(packed, axis=1).astype(BF16)

    regroup(steps - 1, 0)
    send_edges()
    regroup(0, 0)
    regroup(1, 0)

    def chunk(ref, j, first):
        return ref.at[pl.ds(SLOT * (j + 1), SLOT if first else ML_AZ)]

    def slab_copy(target, j, first):
        return pltpu.make_async_remote_copy(
            src_ref=chunk(data.at[target], j, first), dst_ref=chunk(recv.at[q + SIDE], j, first),
            send_sem=send_sem.at[0], recv_sem=recv_sem.at[1, j],
            device_id={"date": z * SPAN + target}, device_id_type=mesh_id,
        )

    def own_copy(j, first):
        return pltpu.make_async_copy(
            chunk(data.at[q], j, first), chunk(recv.at[q + SIDE], j, first), recv_sem.at[1, j]
        )

    def side_copy(w, j, first):
        go_left = w < SPAN
        to, device = (w + SPAN, me - SPAN) if go_left else (w - SPAN, me + SPAN)
        return pltpu.make_async_remote_copy(
            src_ref=chunk(recv.at[w], j, first), dst_ref=chunk(recv.at[to], j, first),
            send_sem=send_sem.at[1 if go_left else 2], recv_sem=recv_sem.at[2 if go_left else 0, j],
            device_id={"date": device}, device_id_type=mesh_id,
        )

    def arrived(dates, side, j, first):
        ref = recv.at[pl.ds(dates[0], len(dates)), pl.ds(SLOT * (j + 1), SLOT if first else ML_AZ)]
        pltpu.make_async_copy(ref, ref, recv_sem.at[side, j]).wait()

    near = SPAN - 1 + has_left.astype(jnp.int32) + has_right.astype(jnp.int32)
    pl.semaphore_wait(barrier, near)

    def send_chunk(j, first):
        own_copy(j, first).start()
        for hop in (2, 3, 1):
            slab_copy(lax.rem(q + hop, SPAN), j, first).start()

    send_chunk(0, True)

    def send_more(j, carry):
        regroup(j + 1, 0)
        send_chunk(j, False)
        return carry

    lax.fori_loop(1, steps - 2, send_more, 0)
    for j in range(steps - 2, steps):
        send_chunk(j, False)

    @pl.when(jnp.logical_not(has_left))
    def _():
        for w in range(SIDE):
            recv[w] = jnp.zeros(recv.shape[1:], BF16)

    @pl.when(jnp.logical_not(has_right))
    def _():
        for w in range(SIDE + SPAN, WIN):
            recv[w] = jnp.zeros(recv.shape[1:], BF16)

    width = out_ref.shape[2]
    place_row = lax.broadcasted_iota(jnp.int32, (LANES, width), 0)
    place_block = lax.broadcasted_iota(jnp.int32, (LANES, width), 1) // CELLS
    on_place = place_row == lax.rem(place_block, steps) * SUB + place_block // steps
    place[...] = jnp.where(on_place, 1.0, 0.0).astype(BF16)

    sel_row = lax.broadcasted_iota(jnp.int32, (CELLS, 2 * LANES), 0)
    sel_lane = lax.broadcasted_iota(jnp.int32, (CELLS, 2 * LANES), 1)
    selector = jnp.where(lax.rem(sel_lane, LANES) // ML_RG == sel_row, 1.0, 0.0).astype(BF16)
    contract = (((1,), (1,)), ((), ()))
    edge_lane = lax.rem(lax.broadcasted_iota(jnp.int32, (ML_AZ, SUB, 2 * LANES), 2), LANES)
    from_before = edge_lane >= LANES - TAPS // 2
    sub_row = lax.broadcasted_iota(jnp.int32, (ML_AZ, SUB, 2 * LANES), 1)

    def own_arrive(j, first):
        arrived(OWN, 1, j, first)

        @pl.when(has_left)
        def _():
            for w in OWN[:SIDE]:
                side_copy(w, j, first).start()

        @pl.when(has_right)
        def _():
            for w in OWN[SIDE:]:
                side_copy(w, j, first).start()

    def far_arrive(j, first):
        @pl.when(has_left)
        def _():
            arrived(FAR[:SIDE], 0, j, first)

        @pl.when(has_right)
        def _():
            arrived(FAR[SIDE:], 2, j, first)

    def make_after(dates):
        for w in dates:
            value = recv[w, SLOT:SLOT + ML_AZ].astype(F32)
            value = jnp.where(sub_row < SUB - 1, pltpu.roll(value, SUB - 1, 1), 0.0)
            recv[w, SLOT * (steps + 1):SLOT * (steps + 1) + ML_AZ] = value.astype(BF16)

    def make_edges(dates):
        for w in dates:
            tiles = recv[w, SLOT + ML_AZ].astype(F32)
            for r in range(ML_AZ):
                before, after = [], []
                for part in range(2):
                    tile, at = edge_at(r, part)
                    value = tiles[:, tile * LANES:tile * LANES + LANES]
                    after.append(pltpu.roll(value, LANES - at, 1) if at else value)
                    value = pltpu.roll(value, (LANES - 2 * REACH - at) % LANES, 1)
                    before.append(jnp.where(tile_row[:, 0:LANES] > 0, pltpu.roll(value, 1, 0), 0.0))
                recv[w, r] = jnp.concatenate(before, axis=1).astype(BF16)
                recv[w, SLOT * (steps + 2) + r] = jnp.concatenate(after, axis=1).astype(BF16)

    def make_flags():
        flag_lane = lax.broadcasted_iota(jnp.int32, (CELLS, LANES), 1)
        for h in range(HALVES):
            flags = None
            for slot in range(GROUP):
                k, g = HALVES * h + slot // SPAN + 1, slot % SPAN
                tile, at = edge_at(k - 1, 0)
                at += tile * LANES + REACH - 1
                tiles = recv[first_date(k) + g, SLOT + ML_AZ].astype(F32)
                one = jnp.broadcast_to(tiles[0:CELLS, at:at + 1], (CELLS, LANES))
                flags = one if flags is None else jnp.where(flag_lane >= slot * SUB, one, flags)
            flag_of[h] = flags

    def band_split(dates, j):
        rows = []
        behind = SLOT * jnp.where(j == steps - 2, steps + 2, j + 2)
        for w in dates:
            here = recv[w, pl.ds(SLOT * (j + 1), ML_AZ)]
            before = recv[w, pl.ds(SLOT * j, ML_AZ)]
            after = recv[w, pl.ds(behind, ML_AZ)]
            edge = jnp.where(from_before, before, after)
            rows.append(jnp.concatenate([here, edge], axis=2).reshape(ML_AZ * SUB, 4 * LANES))
        made = jnp.dot(jnp.concatenate(rows, axis=0), mat[...], preferred_element_type=F32)
        return made.astype(BF16).astype(F32).reshape(len(dates), ML_AZ, SUB, 4 * LANES)

    def read(w, j, band, part):
        cols = slice((2 * band + part) * LANES, (2 * band + part + 1) * LANES)
        if w in OWN:
            return [bands_own[j, OWN.index(w), r, :, cols] for r in range(ML_AZ)]
        return [bands_far[FAR.index(w), r, :, cols] for r in range(ML_AZ)]

    def total(terms):
        terms = list(terms)
        while len(terms) > 1:
            terms = [a + b for a, b in zip(terms[::2], terms[1::2])]
        return terms[0]

    def keep_sum(j, at, value):
        high = value.astype(BF16)
        low = (value - high.astype(F32)).astype(BF16)
        both[j, at * SUB:at * SUB + SUB, 0:LANES] = high
        both[j, at * SUB:at * SUB + SUB, LANES:2 * LANES] = low

    def products(dates, pairs, j):
        for band in range(2):
            for w in dates:
                re, im = (read(w, j, band, part) for part in range(2))
                keep_sum(j, power_slot(band, w), total([a * a for a in re]) + total([a * a for a in im]))
            for w, k in pairs:
                a_re, a_im = (read(w, j, band, part) for part in range(2))
                b_re, b_im = (read(w + k, j, band, part) for part in range(2))
                re = total([a * b for a, b in zip(a_re, b_re)]) + total([a * b for a, b in zip(a_im, b_im)])
                im = total([a * b for a, b in zip(a_im, b_re)]) - total([a * b for a, b in zip(a_re, b_im)])
                keep_sum(j, pair_slot(0, band, w, k), re)
                keep_sum(j, pair_slot(1, band, w, k), im)

    def own_step(j):
        bands_own[j] = band_split(OWN, j)
        products(OWN, OWN_PAIRS, j)

    def far_step(j):
        bands_far[...] = band_split(FAR, j)
        products(FAR, FAR_PAIRS, j)
        red[j] = lax.dot_general(selector, both[j], contract, preferred_element_type=F32)

    def wave_signal():
        @pl.when(has_left)
        def _():
            pl.semaphore_signal(wave_sem.at[1], inc=1, device_id={"date": me - SPAN}, device_id_type=mesh_id)

        @pl.when(has_right)
        def _():
            pl.semaphore_signal(wave_sem.at[0], inc=1, device_id={"date": me + SPAN}, device_id_type=mesh_id)

    def wave(t, carry):
        @pl.when(has_left)
        def _():
            pl.semaphore_wait(wave_sem.at[0], 1)

        @pl.when(has_right)
        def _():
            pl.semaphore_wait(wave_sem.at[1], 1)

        @pl.when(t < slabs - 1)
        def _():
            wave_signal()

        return carry

    own_arrive(0, True)
    make_after(OWN)
    make_edges(OWN)

    wave_signal()

    def stream(t, carry):
        u = t - LAG

        @pl.when(t < steps)
        def _():
            own_arrive(t, False)

        @pl.when(t < slabs)
        def _():
            wave(t, 0)

        @pl.when(t <= steps)
        def _():
            own_step(t - 1)

        @pl.when(u == 0)
        def _():
            far_arrive(0, True)
            make_after(FAR)
            make_edges(FAR)
            make_flags()

        @pl.when((u > 0) & (u < steps - 1))
        def _():
            far_arrive(u, False)

        @pl.when(u > 0)
        def _():
            far_step(u - 1)

        @pl.when(u == steps - 1)
        def _():
            far_arrive(u, False)

        return carry

    lax.fori_loop(1, steps + LAG, stream, 0)
    lax.fori_loop(steps + LAG, slabs, wave, 0)
    far_step(steps - 1)

    shape = (steps, CELLS, LANES)
    c_id = lax.broadcasted_iota(jnp.int32, shape, 1)
    l_id = lax.broadcasted_iota(jnp.int32, shape, 2)
    i_id = lax.rem(l_id, SUB)

    def box(value):
        prefix = value
        for hop in (1, 2, 4):
            prefix = prefix + jnp.where(c_id >= hop, pltpu.roll(prefix, hop, 1), 0.0)
        whole = jnp.sum(value, axis=1, keepdims=True)
        suffix = whole - prefix + value
        first = jnp.where(i_id[0:1] > 0, pltpu.roll(suffix[steps - 1:steps], 1, 2), 0.0)
        last = jnp.where(i_id[0:1] < SUB - 1, pltpu.roll(prefix[0:1], LANES - 1, 2), 0.0)
        before = jnp.concatenate([first, suffix[0:steps - 1]], axis=0)
        after = jnp.concatenate([prefix[1:steps], last], axis=0)
        return before + whole + after

    def register(at):
        return red[:, :, at * LANES:at * LANES + LANES]

    lane = lax.broadcasted_iota(jnp.int32, (CELLS, LANES), 1)
    span_lanes = SPAN * SUB

    def aligned(value, ks, partner):
        parts = []
        for at, k in enumerate(ks):
            w = first_date(k) + (k if partner else 0)
            move = (at * SPAN - w) * SUB % LANES
            parts.append(pltpu.roll(value, move, 2) if move else value)
        return jnp.where(l_id < span_lanes, parts[0], parts[1])

    for h in range(HALVES):
        ks = (HALVES * h + 1, HALVES * h + 2)
        cr0, ci0, cr1, ci1 = (register(m * HALVES + h) for m in range(4))
        ab0, ab1 = (
            aligned(power, ks, False) * aligned(power, ks, True) + eps_power
            for power in (register(4 * HALVES), register(4 * HALVES + 1))
        )
        weight = flag_of[h][None] * 0.5 * ((cr0 * cr0 + ci0 * ci0) / ab0 + (cr1 * cr1 + ci1 * ci1) / ab1)
        phase = split_coef * (ci0 * cr1 - cr0 * ci1) / jnp.sqrt(ab0 * ab1)
        den = box(weight)
        num = box(weight * phase)
        quant[:, h] = den / (2 * RADIUS + 1)
        quant[:, HALVES + h] = num / (den + floor_weight)

    workers = msg.shape[0]
    share = steps // workers
    base = (slabs - workers) // 2
    is_worker = (z >= base) & (z < base + workers)
    half = LANES // 2
    ranks = LANES // SUB
    zero = jnp.zeros((CELLS, LANES), F32)

    def turned(rows):
        rows = list(rows)
        bit = 1
        while bit < len(rows):
            upper = lax.rem(lane // (SUB * bit), 2) == 1
            for a in range(len(rows)):
                if a & bit == 0:
                    low, high = rows[a], rows[a | bit]
                    rows[a] = jnp.where(upper, pltpu.roll(high, SUB * bit, 1), low)
                    rows[a | bit] = jnp.where(upper, high, pltpu.roll(low, LANES - SUB * bit, 1))
            bit *= 2
        return rows

    def line_copy(u):
        return pltpu.make_async_remote_copy(
            src_ref=msg.at[u], dst_ref=got.at[z],
            send_sem=send_sem.at[3], recv_sem=recv_sem.at[0, steps],
            device_id={"date": (base + u) * SPAN + q}, device_id_type=mesh_id,
        )

    for u in range(workers):
        for kind in range(2):
            rows = [zero] * ranks
            for h in range(HALVES):
                for jj in range(share):
                    rows[h * ranks // 2 + jj] = quant[u * share + jj, kind * HALVES + h]
            for slot, value in enumerate(turned(rows)):
                msg[u, kind, slot] = value

        @pl.when(z != base + u)
        def _():
            line_copy(u).start()

        @pl.when(z == base + u)
        def _():
            pltpu.make_async_copy(msg.at[u], got.at[z], recv_sem.at[0, steps]).start()

    def out_copy(target):
        return pltpu.make_async_remote_copy(
            src_ref=pack.at[target], dst_ref=back.at[(z - base) * SPAN + q],
            send_sem=send_sem.at[4], recv_sem=recv_sem.at[0, steps + 1],
            device_id={"date": target}, device_id_type=mesh_id,
        )

    in_lower = lane < half

    def split(low, high):
        return jnp.where(in_lower, low, high)

    def fold(value):
        return value + pltpu.roll(value, half, 1)

    def at(values, d):
        return values[d] if 0 <= d < n else zero

    def held(kind, position, d):
        return got[d // SPAN, kind, position * SPAN + d % SPAN] if d < n else zero

    def relax():
        near, wide = [], []
        for kind in range(2):
            near.append([held(kind, 0, d + 1) for d in range(n)])
            wide.append([split(held(kind, 1, d + 1), held(kind, 1, d + 2)) for d in range(n)])
        near_back = [split(at(near[0], d - 1), at(near[0], d - 3)) for d in range(n)]
        wide_back = [split(at(wide[0], d - 2), at(wide[0], d - 4)) for d in range(n)]
        wsum = [fold((a + b) + (c + e)) for a, b, c, e in zip(near[0], wide[0], near_back, wide_back)]
        near_flow = [a * b for a, b in zip(*near)]
        wide_flow = [a * b for a, b in zip(*wide)]
        flow = [
            (split(at(near_flow, d - 1), at(near_flow, d - 3)) + split(at(wide_flow, d - 2), at(wide_flow, d - 4)))
            - (near_flow[d] + wide_flow[d]) for d in range(n)
        ]
        phi = [zero]
        for d in range(n - 1):
            first = near[1][d]
            phi.append(phi[-1] + split(first, pltpu.roll(first, half, 1)))
        pull = [ridge_weight * p for p in phi]
        inv = [1.0 / (t + ridge_weight) for t in wsum]
        for sweep in range(ITERS):
            up = [split(at(phi, d), at(phi, d + 2)) for d in range(n + 2)]
            down = [split(at(phi, d - 2), at(phi, d - 4)) for d in range(n + 2)]
            phi = [
                (
                    fold(
                        flow[d] + (near[0][d] * up[d + 1] + wide[0][d] * at(up[:n], d + 2))
                        + (near_back[d] * down[d + 1] + wide_back[d] * down[d])
                    ) + pull[d]
                ) * inv[d] for d in range(n)
            ]
        return phi, wsum

    @pl.when(is_worker)
    def _():
        pltpu.make_async_copy(got, got, recv_sem.at[0, steps]).wait()
        phi, wsum = relax()
        for d in range(n):
            pack[d] = split(phi[d], wsum[d])

        def send_back(i, carry):
            for g in range(SPAN):
                target = SPAN * jnp.where(z < slabs // 2, slabs - 1 - i, i) + g

                @pl.when(target != me)
                def _():
                    out_copy(target).start()
            return carry

        lax.fori_loop(0, slabs, send_back, 0)
        pltpu.make_async_copy(
            pack.at[me], back.at[(z - base) * SPAN + q], recv_sem.at[0, steps + 1]
        ).start()

    def drain(ref, sem):
        pltpu.make_async_copy(ref, ref, sem).wait()

    tiles = SLOT + ML_AZ * (steps - 1)
    drain(data.at[pl.ds(0, SPAN - 1), pl.ds(0, tiles)], send_sem.at[0])

    @pl.when(has_left)
    def _():
        drain(data.at[pl.ds(0, SIDE), pl.ds(0, tiles)], send_sem.at[1])

    @pl.when(has_right)
    def _():
        drain(data.at[pl.ds(0, SIDE), pl.ds(0, tiles)], send_sem.at[2])

    drain(msg.at[pl.ds(0, workers - 1)], send_sem.at[3])

    @pl.when(jnp.logical_not(is_worker))
    def _():
        drain(msg.at[0], send_sem.at[3])

    drain(back, recv_sem.at[0, steps + 1])

    @pl.when(is_worker)
    def _():
        drain(pack.at[pl.ds(0, n - 1)], send_sem.at[4])

    rows = []
    for kind in range(2):
        for s in range(SPAN):
            value = None
            for u in range(workers):
                move = (u * share * SUB - kind * half) % LANES
                piece = back[u * SPAN + s]
                piece = pltpu.roll(piece, move, 1) if move else piece
                value = piece if value is None else jnp.where(lane >= u * share * SUB, piece, value)
            rows.append(value)
    value = jnp.concatenate(rows, axis=0)
    high = value.astype(BF16)
    low = (value - high.astype(F32)).astype(BF16)
    spread = jnp.dot(
        jnp.concatenate([high, low], axis=0), place[...],
        preferred_element_type=F32,
    )
    count = 2 * SPAN * CELLS
    spread = spread[0:count] + spread[count:2 * count]
    spread = spread.reshape(2 * SPAN, CELLS, width)
    s_row = lax.broadcasted_iota(jnp.int32, spread.shape, 1)
    s_col = lax.broadcasted_iota(jnp.int32, spread.shape, 2)
    result = jnp.sum(jnp.where(lax.rem(s_col, CELLS) == s_row, spread, 0.0), axis=1)
    out_ref[0] = result[0:SPAN]
    out_ref[1] = result[SPAN:2 * SPAN]


def local(slc_stack, band_taps, pair_flags):
    n = lax.axis_size("date")
    rows, span = slc_stack.shape[2:]
    steps = span // LANES // SUB
    slabs = n // SPAN
    assert rows == SUB and rows // ML_AZ == SPAN and span == LANES * LANES
    assert n % (LANES // SUB) == 0 and steps == LANES // SUB
    workers = 1
    while 2 * workers <= min(steps, slabs // 2):
        workers *= 2
    tiles = SLOT * (steps + 3)

    vmem = pl.BlockSpec(memory_space=pltpu.VMEM)
    small = lambda *lead: pltpu.VMEM((*lead, CELLS, LANES), F32)
    sem = lambda *lead: pltpu.SemaphoreType.DMA(lead)
    both = pl.pallas_call(
        functools.partial(kernel, n, steps),
        out_shape=jax.ShapeDtypeStruct((2, rows // ML_AZ, span // ML_RG), F32),
        in_specs=[pl.BlockSpec(memory_space=pl.ANY)] * 3,
        out_specs=vmem,
        scratch_shapes=[
            pltpu.VMEM((2, rows, span), BF16),
            pltpu.VMEM((1, SPAN), jnp.int32),
            pltpu.VMEM((2, 2, TAPS), BF16),
            pltpu.VMEM((8, LANES), F32),
            pltpu.VMEM((2 * SUB * SUB, LANES), F32),
            pltpu.VMEM((SPAN, tiles, SUB, 2 * LANES), BF16),
            pltpu.VMEM((WIN, tiles, SUB, 2 * LANES), BF16),
            pltpu.VMEM((4 * LANES, 4 * LANES), BF16),
            pltpu.VMEM((steps, SPAN, ML_AZ, SUB, 4 * LANES), F32),
            pltpu.VMEM((SPAN, ML_AZ, SUB, 4 * LANES), F32),
            pltpu.VMEM((steps, SLOTS * SUB, 2 * LANES), BF16),
            pltpu.VMEM((steps, CELLS, SLOTS * SUB), F32),
            small(steps, 2 * HALVES),
            small(workers, 2, GROUP),
            small(slabs, 2, GROUP),
            small(n),
            small(workers * SPAN),
            pltpu.VMEM((LANES, span // ML_RG), BF16),
            small(HALVES),
            sem(3), sem(5), sem(3, steps + 2), pltpu.SemaphoreType.REGULAR((2,)),
        ],
        compiler_params=pltpu.CompilerParams(
            collective_id=0, has_side_effects=True, vmem_limit_bytes=60 * 1024 * 1024
        ),
    )(slc_stack, pair_flags, band_taps)
    return both[0:1], both[1:2]


def solution(mesh):
    in_specs = (P("date", None, "group", None), P(), P("date", None))
    out_specs = (P("date", "group", None), P("date", "group", None))
    return jax.shard_map(local, mesh=mesh, in_specs=in_specs, out_specs=out_specs, check_vma=False)
```
